512 devices in a mesh: dp: 16 (over x, z_hi), pack: 32 (over z_lo, y, core).
Axes of the slice: x: 4, y: 8, z: 8 (z_hi: 4, z_lo: 2; z = z_hi * 2 + z_lo), core: 2. Of those that a mesh axis runs over, the one named last changes fastest.
Arguments:
- hidden_in: bfloat16 [1024, 4096], P('dp', 'pack'), may hold values from -6 to 6
- attn_gain: float32 [4096], P('pack'), may hold values from 0.25 to 1.75
- w_query: bfloat16 [4096, 4096], P(None, 'pack'), may hold values from -0.09375 to 0.09375
- query_gain: float32 [128], replicated, may hold values from 0.25 to 1.75
- cached_keys: bfloat16 [163840, 1024], P(('dp', 'pack')), may hold values from -200 to 200
- cached_values: bfloat16 [163840, 1024], P(('dp', 'pack')), may hold values from -9 to 9
- w_out: bfloat16 [4096, 4096], P('pack'), may hold values from -0.09375 to 0.09375
- final_gain: float32 [4096], P('pack'), may hold values from 0.25 to 1.75
- lengths: int32 [16, 64], P('dp'), may hold values from 16 to 304, as said below
- pack_order: int32 [16, 64], P('dp'), may hold values from 0 to 63, each once within a row
- partner: int32 [1024], replicated, may hold values from 0 to 1023, as said below
Outputs:
- pooled: bfloat16 [1024, 4096], P('dp', 'pack')
- loss_rows: float32 [1024], P(('dp', 'pack'))
- grad_hidden: bfloat16 [1024, 4096], P('dp', 'pack')
The draws below stay inside these ranges and needn't reach their ends.
Inputs may be any that keep to these rules, and one draw needn't show every extreme that they name: Statements 2k and 2k+1 of a group have lengths that sum to 320, so a group's lengths sum to 320 * 32. `pack_order`: each row is a permutation of the group's statement indices. `partner`: no statement is its own positive.
All inputs are finite; a program needn't handle non-finite values.
Results may differ from the reference program's by a relative error of at most 0.019.
Values may be sent and summed in bfloat16 or wider, within the bound.
A program may use at most 128 MiB of HBM per device.

```python
import math
import jax
import jax.numpy as jnp
from jax import lax

D = 4096
HEADS = 32
KV_HEADS = 8
HEAD_DIM = 128
MEANLEN = 160
TOK_DEV = 320
STMTS = 64
GROUPS = 16
ALL_STMTS = 1024
N_DP = 16
N_PACK = 32


def draw_lengths(key, part):
    pair_sum = 2 * MEANLEN
    shorter = jax.random.randint(key, (GROUPS, STMTS // 2), 16, pair_sum - 15, dtype=jnp.int32)
    first_col = jnp.arange(STMTS // 2, dtype=jnp.int32)[None, :] == 0
    shorter = jnp.where(first_col, 16, shorter).astype(jnp.int32)
    return jnp.stack([shorter, pair_sum - shorter], axis=2).reshape(GROUPS, STMTS).astype(jnp.int32)


def draw_partner(key, part):
    offset = jax.random.randint(key, (ALL_STMTS,), 1, ALL_STMTS, dtype=jnp.int32)
    return ((jnp.arange(ALL_STMTS, dtype=jnp.int32) + offset) % ALL_STMTS).astype(jnp.int32)


def draw_cached_keys(key, part):
    row_count = TOK_DEV * N_PACK * N_DP
    base_key = jax.random.fold_in(key, 11)
    entries = jax.random.truncated_normal(base_key, -6.0, 6.0, (row_count, KV_HEADS, HEAD_DIM), jnp.float32)
    drawn = entries * 2.5
    return drawn.reshape(row_count, KV_HEADS * HEAD_DIM).astype(jnp.bfloat16)


def block_scale(rng, dims, shards, low, high):
    level = 1.0
    for dim, blocks in shards:
        draws = jax.random.uniform(jax.random.fold_in(jax.random.fold_in(rng, 6), dim), (blocks,), jnp.float32, low / len(shards), high / len(shards))
        level = level * jnp.repeat(jnp.exp(draws), dims[dim] // blocks).reshape((-1,) + (1,) * (len(dims) - 1 - dim))
    return level


def normal_values(key, extent, width, most, shards=(), kind=jnp.bfloat16):
    values = width * jax.random.normal(key, extent, jnp.float32)
    if shards:
        values = values * block_scale(key, extent, shards, -0.22, 0.18)
    return jnp.clip(values, -most, most).astype(kind)


def setup_inputs(seed: int = 0) -> dict:
    splits = jax.random.split(jax.random.key(seed), 12)
    return {
        "hidden_in": normal_values(splits[0], (ALL_STMTS, D), 1.0, 6.0, ((0, 16), (1, 32))),
        "attn_gain": jnp.clip(1.0 + 0.15 * jax.random.normal(splits[1], (D,), jnp.float32), 0.25, 1.75),
        "w_query": normal_values(splits[2], (D, HEADS * HEAD_DIM), D ** -0.5, 0.09375, ((1, 32),)),
        "query_gain": jnp.clip(1.0 + 0.15 * jax.random.normal(splits[3], (HEAD_DIM,), jnp.float32), 0.25, 1.75),
        "cached_keys": draw_cached_keys(jax.random.fold_in(splits[11], 71), 0),
        "cached_values": normal_values(splits[5], (TOK_DEV * N_PACK * N_DP, KV_HEADS * HEAD_DIM), 1.5, 9.0, ((0, 512),)),
        "w_out": normal_values(splits[6], (HEADS * HEAD_DIM, D), (HEADS * HEAD_DIM) ** -0.5, 0.09375, ((0, 32),)),
        "final_gain": jnp.clip(1.0 + 0.15 * jax.random.normal(splits[7], (D,), jnp.float32), 0.25, 1.75),
        "lengths": draw_lengths(jax.random.fold_in(splits[11], 71), 0),
        "pack_order": jax.vmap(lambda own: jax.random.permutation(own, STMTS))(jax.random.split(splits[9], GROUPS)).reshape((GROUPS, STMTS)).astype(jnp.int32),
        "partner": draw_partner(jax.random.fold_in(splits[11], 71), 0),
    }


EPSILON = 1e-06
SOFTMAX_WARMTH = 0.05
ROPE_BASE = 1000000.0
MASKED_LOGIT = -1e+30

def rotate_heads(queries, position):
    head_dim = queries.shape[-1]
    half_dim = head_dim // 2
    frequency = jnp.power(jnp.float32(ROPE_BASE), -jnp.arange(half_dim).astype(jnp.float32) * 2.0 / head_dim)
    angles = position[:, None] * frequency[None, :]
    cosine = jnp.concatenate([jnp.cos(angles), jnp.cos(angles)], axis=1)[:, None, :]
    sine_part = jnp.concatenate([jnp.sin(angles), jnp.sin(angles)], axis=1)[:, None, :]
    turned = jnp.concatenate([-queries[..., half_dim:], queries[..., :half_dim]], axis=-1)
    return queries * cosine + turned * sine_part

def token_owner(lengths_row, order_row, first_token, token_count):
    stmt_count = order_row.shape[0]
    picked = order_row[:, None] == jnp.arange(stmt_count, dtype=jnp.int32)[None, :]
    packed_len = lax.optimization_barrier(jnp.sum(jnp.where(picked, lengths_row[None, :], 0), axis=1)).astype(jnp.int32)
    range_end = jnp.cumsum(packed_len).astype(jnp.int32)
    token_index = first_token + jnp.arange(token_count, dtype=jnp.int32)
    slot_index = lax.optimization_barrier(jnp.sum((token_index[:, None] >= range_end[None, :]).astype(jnp.int32), axis=1)).astype(jnp.int32)
    return jnp.take(order_row, slot_index)

def shard_attention(group_queries, shard_keys, shard_values, token_owners):
    stmt_count = group_queries.shape[0]
    grouped = group_queries.astype(jnp.float32).reshape(stmt_count, KV_HEADS, HEADS // KV_HEADS, HEAD_DIM)
    key_heads = shard_keys.astype(jnp.float32).reshape(-1, KV_HEADS, HEAD_DIM)
    value_heads = shard_values.astype(jnp.float32).reshape(-1, KV_HEADS, HEAD_DIM)
    scores = jnp.einsum('skgd,tkd->skgt', grouped, key_heads) * HEAD_DIM ** (-0.5)
    token_mask = (token_owners[None, :] == jnp.arange(stmt_count, dtype=jnp.int32)[:, None])[:, None, None, :]
    block_max = lax.optimization_barrier(jnp.max(jnp.where(token_mask, scores, MASKED_LOGIT), axis=3))
    softmax_weights = jnp.where(token_mask, jnp.exp(scores - block_max[..., None]), 0.0)
    block_sum = lax.optimization_barrier(jnp.sum(softmax_weights, axis=3))
    rounded = lax.optimization_barrier(softmax_weights.astype(jnp.bfloat16)).astype(jnp.float32)
    numerators = jnp.einsum('skgt,tkd->skgd', rounded, value_heads)
    return (block_max.reshape(stmt_count, HEADS), block_sum.reshape(stmt_count, HEADS), numerators.reshape(stmt_count, HEADS, HEAD_DIM))

def reference(hidden_in, attn_gain, w_query, query_gain, cached_keys, cached_values, w_out, final_gain, lengths, pack_order, partner):
    group_tokens = TOK_DEV * N_PACK
    inputs32 = hidden_in.astype(jnp.float32)
    input_rms = lax.rsqrt(lax.optimization_barrier(jnp.sum(inputs32 * inputs32, axis=1, keepdims=True)) / D + EPSILON)
    normed = (inputs32 * input_rms * attn_gain[None, :]).astype(jnp.bfloat16)
    projected = jnp.dot(normed, w_query, preferred_element_type=jnp.float32).reshape(ALL_STMTS, HEADS, HEAD_DIM)
    queries = projected * lax.rsqrt(lax.optimization_barrier(jnp.mean(projected * projected, axis=2, keepdims=True)) + EPSILON) * query_gain
    position = (lengths.reshape(ALL_STMTS) - 1).astype(jnp.float32)
    queries = rotate_heads(queries, position).astype(jnp.bfloat16)

    def one_group(packed):
        group_queries, group_keys, group_values, lengths_row, order_row = packed
        owners = token_owner(lengths_row, order_row, 0, group_tokens).reshape(N_PACK, TOK_DEV)

        def one_shard(shard_data):
            return shard_attention(group_queries, shard_data[0], shard_data[1], shard_data[2])
        block_max, block_sum, numerators = lax.map(one_shard, (group_keys.reshape(N_PACK, TOK_DEV, -1), group_values.reshape(N_PACK, TOK_DEV, -1), owners))
        highest = lax.optimization_barrier(jnp.max(block_max, axis=0))
        factor = jnp.exp(block_max - highest[None])
        denominator = lax.optimization_barrier(jnp.sum(block_sum * factor, axis=0))
        summed = lax.optimization_barrier(jnp.sum(numerators * factor[..., None], axis=0))
        return (summed / denominator[..., None]).astype(jnp.bfloat16)
    attended = lax.map(one_group, (queries.reshape(N_DP, STMTS, HEADS, HEAD_DIM), cached_keys.reshape(N_DP, group_tokens, -1), cached_values.reshape(N_DP, group_tokens, -1), lengths, pack_order))
    attended = attended.reshape(ALL_STMTS, HEADS * HEAD_DIM)
    hidden = inputs32 + jnp.dot(attended, w_out, preferred_element_type=jnp.float32)
    hidden_rms = jnp.sqrt(lax.optimization_barrier(jnp.sum(hidden * hidden, axis=1, keepdims=True)) / D + EPSILON)
    pooled = (hidden / hidden_rms * final_gain[None, :]).astype(jnp.bfloat16)
    pooled32 = pooled.astype(jnp.float32)
    pooled_norm = jnp.sqrt(lax.optimization_barrier(jnp.sum(pooled32 * pooled32, axis=1, keepdims=True)))
    premise_vectors = (pooled32 / pooled_norm).astype(jnp.bfloat16)
    unscaled_logits = jnp.dot(premise_vectors, premise_vectors.T, preferred_element_type=jnp.float32)
    identity_matrix = jnp.arange(ALL_STMTS, dtype=jnp.int32)
    similarity_logits = jnp.where(identity_matrix[None, :] == identity_matrix[:, None], MASKED_LOGIT, unscaled_logits / SOFTMAX_WARMTH)
    highest = lax.optimization_barrier(jnp.max(similarity_logits, axis=1))
    row_lse = highest + jnp.log(lax.optimization_barrier(jnp.sum(jnp.exp(similarity_logits - highest[:, None]), axis=1)))
    is_partner = identity_matrix[None, :] == partner[:, None]
    target = lax.optimization_barrier(jnp.sum(jnp.where(is_partner, similarity_logits, 0.0), axis=1))
    loss_rows = row_lse - target
    pair_weight = jnp.exp(similarity_logits - row_lse[:, None]) + jnp.exp(similarity_logits - row_lse[None, :]) - is_partner.astype(jnp.float32) - is_partner.T.astype(jnp.float32)
    softmax_weights = pair_weight.astype(jnp.bfloat16)
    embedding_gradient = jnp.dot(softmax_weights, premise_vectors, preferred_element_type=jnp.float32) / SOFTMAX_WARMTH
    embed32 = premise_vectors.astype(jnp.float32)
    inner_sum = lax.optimization_barrier(jnp.sum(embed32 * embedding_gradient, axis=1, keepdims=True))
    grad_pooled = (embedding_gradient - embed32 * inner_sum) / pooled_norm
    grad_hidden = (math.sqrt(D) * final_gain[None, :] * grad_pooled / hidden_rms).astype(jnp.bfloat16)
    return (pooled, loss_rows, grad_hidden)
```

```python
import math

import jax
import jax.numpy as jnp
from jax import lax
from jax.experimental import pallas as pl
from jax.experimental.pallas import tpu as pltpu
from jax.sharding import PartitionSpec as P

EPSILON = 1e-06
WARMTH = 0.05
ROPE_BASE = 1000000.0
MASKED = -1e30
F32 = jnp.float32
BF16 = jnp.bfloat16
I32 = jnp.int32

SLOTS = 24
STAT = SLOTS - 1
PACK = 32
CHIPS = 16
DP = 16
MESH = pl.DeviceIdType.MESH


def far_first(k, half):
    return half + (1 - 2 * lax.rem(k, 2)) * lax.div(k + 1, 2)


def dot_t(a, b):
    return lax.dot_general(a, b, (((1,), (1,)), ((), ())), preferred_element_type=F32)


def dot(a, b):
    return jnp.dot(a, b, preferred_element_type=F32)


def iota(shape, dim):
    return lax.broadcasted_iota(I32, shape, dim)


def kernel(
    hid_ref, again_ref, wq_hbm, qgain_ref, k_hbm, v_hbm, wo_hbm, fgain_ref, len_ref, ord_ref, part_ref,
    pooled_ref, loss_ref, grad_ref,
    x_ref, wq, kk, vv, wo, msg, ints, selbig, sel, bias, cosr, sinr,
    sq, qb, ob_out, ob, att, po_out, po_in, pb, st_own, st_in, ds_own, ds_in,
    pls, lb, lb_in, ub, ls_own, ls_in, uf,
    load_sem, x_send, x_recv, f_send, f_recv, ss, rs,
):
    g = lax.axis_index("dp")
    p = lax.axis_index("pack")
    z, y, c = lax.div(p, 16), lax.div(lax.rem(p, 16), 2), lax.rem(p, 2)
    sib = p + 1 - 2 * c
    chip = z * 8 + y
    n_stmt = hid_ref.shape[0]

    def pack_peer(i):
        k, r = lax.div(i, 4), lax.rem(i, 4)
        py = lax.rem(y + far_first(k, 4), 8)
        pz = lax.rem(z + 1 - lax.div(r, 2), 2)
        pc = lax.rem(c + 1 - lax.rem(r, 2), 2)
        return pz * 16 + py * 2 + pc

    def chip_peer(i):
        k = lax.div(i, 2)
        py = lax.rem(y + far_first(k, 4), 8)
        pz = lax.rem(z + 1 - lax.rem(i, 2), 2)
        return pz * 8 + py

    gx, gz = lax.div(g, 4), lax.rem(g, 4)

    def dp_peer(i):
        a, b = lax.div(i, 4), lax.rem(i, 4)
        return lax.rem(gx + far_first(a, 2), 4) * 4 + lax.rem(gz + far_first(b, 2), 4)

    def remote(src, dst, send, recv, dg, dp_):
        return pltpu.make_async_remote_copy(
            src_ref=src, dst_ref=dst, send_sem=send, recv_sem=recv,
            device_id=(dg, dp_), device_id_type=MESH,
        )

    loads = [
        pltpu.make_async_copy(wq_hbm.at[:, 0], wq.at[0], load_sem.at[0]),
        pltpu.make_async_copy(wq_hbm.at[:, 1], wq.at[1], load_sem.at[1]),
        pltpu.make_async_copy(k_hbm, kk, load_sem.at[2]),
        pltpu.make_async_copy(v_hbm, vv, load_sem.at[3]),
        pltpu.make_async_copy(wo_hbm, wo.at[c], load_sem.at[4]),
    ]
    barrier = pltpu.get_barrier_semaphore()

    def greet_pack(i, carry):
        pl.semaphore_signal(barrier, inc=1, device_id=(g, pack_peer(i)), device_id_type=MESH)
        return carry

    def greet_dp(i, carry):
        pl.semaphore_signal(barrier, inc=1, device_id=(dp_peer(i), p), device_id_type=MESH)
        return carry

    lax.fori_loop(0, DP - 1, greet_dp, 0)
    lax.fori_loop(0, PACK - 1, greet_pack, 0)
    for load in loads:
        load.start()

    lane = iota((n_stmt, 128), 1)
    sub = iota((n_stmt, 128), 0)
    same = lane == sub
    lane1 = iota((1, 128), 1)

    def to_row(col):
        return jnp.sum(jnp.where(same, col, 0.0), axis=0, keepdims=True)

    def to_col(row):
        return jnp.sum(jnp.where(same, row, 0.0), axis=1, keepdims=True)

    h32 = hid_ref[...].astype(F32)
    msg[0:n_stmt, :] = (h32 * again_ref[...]).astype(BF16)
    sq_row = to_row(jnp.sum(h32 * h32, axis=1, keepdims=True))
    sq_hi = sq_row.astype(BF16).astype(F32)
    row16 = iota((16, 128), 0)
    msg[n_stmt:, :] = jnp.where(
        row16 == 0, sq_hi, jnp.where(row16 == 1, sq_row - sq_hi, 0.0)
    ).astype(BF16)

    row8 = iota((8, 128), 0)
    ints[...] = jnp.where(row8 == 1, -1.0, 0.0)
    ints[0:1, 0:n_stmt] = len_ref[...].astype(F32)
    ints[1:2, 0:n_stmt] = ord_ref[...].astype(F32)
    len_row = ints[0:1, :]
    ord_row = ints[1:2, :]
    len_col = to_col(len_row)
    lane_f = lane.astype(F32)
    sub_f = sub.astype(F32)
    at = sub_f == ord_row
    plen_row = jnp.sum(jnp.where(at, len_col, 0.0), axis=0, keepdims=True)
    plen_col = to_col(plen_row)
    end_row = jnp.sum(jnp.where(sub <= lane, plen_col, 0.0), axis=0, keepdims=True)
    start_row = end_row - plen_row
    place_col = jnp.sum(jnp.where(at, lane_f, 0.0), axis=1, keepdims=True)
    place_row = jnp.where(lane1 < n_stmt, to_row(place_col), -1000.0)
    start_col = jnp.sum(jnp.where(at, start_row, 0.0), axis=1, keepdims=True)
    end_col = jnp.sum(jnp.where(at, end_row, 0.0), axis=1, keepdims=True)
    tokens = float(k_hbm.shape[0])
    end_real = jnp.where(lane1 < n_stmt, end_row, 1e9)

    def before(tok):
        return jnp.sum(jnp.where(end_real <= tok, 1.0, 0.0), axis=1, keepdims=True)

    b3 = iota((PACK, SLOTS, 128), 0).reshape(PACK * SLOTS, 128).astype(F32)
    j3 = iota((PACK, SLOTS, 128), 1).reshape(PACK * SLOTS, 128).astype(F32)
    first_big = before(b3 * tokens)
    selbig[...] = jnp.where(place_row == first_big + j3, 1.0, 0.0).astype(BF16)

    block_a = jnp.floor((start_col + 0.5) * (1.0 / tokens))
    block_b = jnp.floor((end_col - 0.5) * (1.0 / tokens))
    slot_a = place_col - before(block_a * tokens)
    slot_b = place_col - before(block_b * tokens)
    wide = iota((n_stmt, PACK * SLOTS), 1).astype(F32)
    for i, (blk, slot) in enumerate(
        ((block_a, slot_a), (block_b, slot_b), (block_a, float(STAT)), (block_b, float(STAT)))
    ):
        sel[i * n_stmt:(i + 1) * n_stmt, :] = jnp.where(
            wide == blk * SLOTS + slot, 1.0, 0.0
        ).astype(BF16)

    pf = p.astype(F32)
    slot_id = before(jnp.zeros((SLOTS, 128), F32) + pf * tokens) + iota((SLOTS, 1), 0).astype(F32)
    lane24 = iota((SLOTS, 128), 1).astype(F32)
    st = jnp.sum(jnp.where(lane24 == slot_id, start_row, 0.0), axis=1, keepdims=True)
    en = jnp.sum(jnp.where(lane24 == slot_id, end_row, 0.0), axis=1, keepdims=True)
    tok = iota((SLOTS, k_hbm.shape[0]), 1).astype(F32) + pf * tokens
    own_bias = jnp.where((tok >= st) & (tok < en), 0.0, MASKED)
    for i in range(4):
        bias[i * SLOTS:(i + 1) * SLOTS, :] = own_bias

    freq = jnp.exp(
        jnp.where(lane1 < 64, lane1, lane1 - 64).astype(F32) * (-2.0 / 128.0 * math.log(ROPE_BASE))
    )
    angle = (len_col - 1.0) * freq
    cosr[...] = jnp.cos(angle)
    sinr[...] = jnp.where(lane < 64, -1.0, 1.0) * jnp.sin(angle)

    pl.semaphore_wait(barrier, PACK - 1 + DP - 1)

    def x_cols(ch):
        return pl.ds(pl.multiple_of(ch * 128, 128), 128)

    def x_start(i, carry):
        to = chip_peer(i)
        remote(msg, x_ref.at[c, :, x_cols(chip)], x_send, x_recv.at[14 - i], g, to * 2 + c).start()
        return carry

    lax.fori_loop(0, CHIPS - 1, x_start, 0)
    remote(msg, x_ref.at[c, :, x_cols(chip)], f_send, f_recv, g, sib).start()
    x_ref[c, :, x_cols(chip)] = msg[...]

    def source_chip(i):
        k = lax.div(i, 2)
        py = lax.rem(y + 8 - far_first(k, 4), 8)
        pz = lax.rem(z + 1 - lax.rem(i, 2), 2)
        return pz * 8 + py

    def x_forward(n, carry):
        src = source_chip(14 - n)
        view = x_ref.at[c, :, x_cols(src)]
        remote(view, view, x_send, x_recv.at[n], g, p).wait_recv()
        remote(view, view, f_send, f_recv, g, sib).start()
        return carry

    lax.fori_loop(0, CHIPS - 1, x_forward, 0)
    w_copy = remote(wo_hbm, wo.at[c], ss.at[0], rs.at[0], g, sib)
    loads[0].wait()
    loads[1].wait()
    q_own = dot(x_ref[c, 0:n_stmt, :], wq[c].reshape(CHIPS * 128, 128))
    f_all = x_ref.at[1 - c]
    remote(f_all, f_all, f_send, f_recv, g, sib).wait_recv()
    q_raw = q_own + dot(x_ref[1 - c, 0:n_stmt, :], wq[1 - c].reshape(CHIPS * 128, 128))
    sq_sum = jnp.zeros((16, 128), F32)
    for i in range(2):
        for j in range(CHIPS):
            sq_sum = sq_sum + x_ref[i, n_stmt:, j * 128:(j + 1) * 128].astype(F32)
    total = to_col(sq_sum[0:1, :] + sq_sum[1:2, :])
    mean_sq = jnp.sum(q_raw * q_raw, axis=1, keepdims=True) * (1.0 / 128.0)
    inv = lax.rsqrt(mean_sq + EPSILON * (total * (1.0 / (PACK * 128)) + EPSILON))
    q = q_raw * inv * qgain_ref[...]
    q = (q * cosr[...] + pltpu.roll(q, 64, 1) * sinr[...]).astype(BF16)
    q128 = jnp.concatenate([q, jnp.zeros((128 - n_stmt, 128), BF16)], axis=0)
    sq[...] = dot(selbig[...], q128).astype(BF16).reshape(PACK, SLOTS, 128)

    def q_start(i, carry):
        to = pack_peer(i)
        remote(sq.at[to], qb.at[p], ss.at[1], rs.at[1], g, to).start()
        return carry

    lax.fori_loop(0, PACK - 1, q_start, 0)
    qb[p] = sq[p]
    w_copy.start()
    loads[2].wait()
    loads[3].wait()
    q31 = qb.at[0:PACK - 1]
    remote(q31, q31, ss.at[1], rs.at[1], g, sib).wait_recv()

    scale = 128 ** -0.5
    jr = iota((SLOTS, 128), 0)
    jl = iota((SLOTS, 128), 1)
    for n in range(8):
        dj = (2, 1, 3, 0)[n // 2]
        kz = lax.rem(z + 1 - n % 2, 2)
        kh = kz * 4 + lax.rem(lax.div(y, 2) + dj, 4)
        cols = pl.ds(pl.multiple_of(kh * 128, 128), 128)
        qs = qb[pl.ds(kh * 4, 4)].reshape(4 * SLOTS, 128)
        s = dot_t(qs, kk[:, cols]) * scale + bias[...]
        m = jnp.max(s, axis=1, keepdims=True)
        w = jnp.exp(s - m)
        l = jnp.sum(w, axis=1, keepdims=True)
        o = dot(w.astype(BF16), vv[:, cols]) / l
        lse = m + jnp.log(l)
        hi = lse.astype(BF16).astype(F32)
        mid = (lse - hi).astype(BF16).astype(F32)
        lo = lse - hi - mid
        for r in range(4):
            part = slice(r * SLOTS, (r + 1) * SLOTS)
            stat = jnp.where(
                jl == jr, hi[part], jnp.where(
                    jl == jr + 32, mid[part], jnp.where(jl == jr + 64, lo[part], 0.0)
                )
            )
            stat = jnp.sum(stat, axis=0, keepdims=True)
            ob_out[kh * 4 + r] = jnp.where(jr == STAT, stat, o[part]).astype(BF16)
        if n < 7:
            for r in range(4):
                to = kh * 4 + r
                remote(ob_out.at[to], ob.at[p], ss.at[2], rs.at[2], g, to).start()
        else:
            for r in range(1, 4):
                to = kh * 4 + lax.rem(lax.rem(p, 4) + r, 4)
                remote(ob_out.at[to], ob.at[p], ss.at[2], rs.at[2], g, to).start()
    ob[p] = ob_out[p]
    o31 = ob.at[0:PACK - 1]
    remote(o31, o31, ss.at[2], rs.at[2], g, sib).wait_recv()

    got = dot(sel[...], ob[...].reshape(PACK * SLOTS, 128))

    def stat_of(rows, slot):
        hit = (lane_f == slot) | (lane_f == slot + 32.0) | (lane_f == slot + 64.0)
        return jnp.sum(jnp.where(hit, rows, 0.0), axis=1, keepdims=True)

    lse_a = stat_of(got[2 * n_stmt:3 * n_stmt], slot_a)
    lse_b = stat_of(got[3 * n_stmt:], slot_b)
    top = jnp.maximum(lse_a, lse_b)
    w_a = jnp.exp(lse_a - top)
    w_b = jnp.where(block_a == block_b, 0.0, jnp.exp(lse_b - top))
    own_att = ((w_a * got[0:n_stmt] + w_b * got[n_stmt:2 * n_stmt]) / (w_a + w_b)).astype(BF16)
    att[c] = own_att
    remote(att.at[c], att.at[c], ss.at[3], rs.at[3], g, sib).start()
    loads[4].wait()
    w_copy.wait_recv()
    remote(att.at[c], att.at[1 - c], ss.at[3], rs.at[3], g, sib).wait_recv()
    heads = jnp.concatenate([att[0], att[1]], axis=1)
    for i in range(CHIPS):
        to = chip_peer(i)
        cols = pl.ds(pl.multiple_of((to * 2 + c) * 128, 128), 128)
        w2 = jnp.concatenate([wo[0, :, cols], wo[1, :, cols]], axis=0)
        part = dot(heads, w2)
        if i < CHIPS - 1:
            po_out[i] = part.astype(BF16)
            remote(po_out.at[i], po_in.at[i], ss.at[4], rs.at[4], g, to * 2 + c).start()
        else:
            own_part = part
    remote(po_out, po_in, ss.at[4], rs.at[4], g, sib).wait_recv()
    hid = hid_ref[...].astype(F32) + own_part
    for i in range(CHIPS - 1):
        hid = hid + po_in[i].astype(F32)

    fgain = fgain_ref[...]
    feat = (hid * fgain).astype(BF16)
    pb[g] = feat
    f32feat = feat.astype(F32)

    def p_start(i, carry):
        remote(pb.at[g], pb.at[g], ss.at[5], rs.at[5], dp_peer(i), p).start()
        return carry

    lax.fori_loop(0, DP - 1, p_start, 0)
    s1 = jnp.sum(hid * hid, axis=1, keepdims=True)
    s2 = jnp.sum(f32feat * f32feat, axis=1, keepdims=True)
    st_row = jnp.sum(
        jnp.where(same, s1, 0.0) + jnp.where(lane == sub + 64, s2, 0.0), axis=0, keepdims=True
    )
    st_own[...] = st_row
    st_in[p] = st_row

    def s_start(i, carry):
        remote(st_own, st_in.at[p], ss.at[6], rs.at[6], g, pack_peer(i)).start()
        return carry

    lax.fori_loop(0, PACK - 1, s_start, 0)
    s31 = st_in.at[0:PACK - 1]
    remote(s31, s31, ss.at[6], rs.at[6], g, sib).wait_recv()
    st_row = jnp.sum(st_in[...], axis=0)
    odd = lax.rem(g, 2)
    half_row = lax.div(g, 2)
    in_half = lax.div(lane1, 64) == odd

    def own_half(row):
        return jnp.where(in_half, jnp.where(odd == 1, row, pltpu.roll(row, 64, 1)), 0.0)

    ds_own[...] = own_half(st_row)
    ds_in[odd, half_row] = ds_own[...]

    def d_start(i, carry):
        remote(ds_own, ds_in.at[odd, half_row], ss.at[7], rs.at[7], dp_peer(i), p).start()
        return carry

    lax.fori_loop(0, DP - 1, d_start, 0)
    s1_all = to_col(jnp.where(lane1 < 64, st_row, 0.0))
    s2_all = to_col(jnp.where(lane1 < 64, pltpu.roll(st_row, 64, 1), 0.0))
    inv_norm = lax.rsqrt(s2_all)
    rms = jnp.sqrt(s1_all * (1.0 / (PACK * 128)) + EPSILON)
    pooled_ref[...] = (hid / rms * fgain).astype(BF16)
    p15 = pb.at[0:DP - 1]
    remote(p15, p15, ss.at[5], rs.at[5], g, sib).wait_recv()

    for j in range(8):
        cols = pb[2 * j:2 * j + 2].reshape(128, 128)
        pls[pl.ds(j, n_stmt, stride=8), :] = dot_t(feat, cols)
    lb[...] = pls[...].astype(BF16).reshape(PACK, 16, 128)

    def l_start(i, carry):
        to = pack_peer(i)
        remote(lb.at[to], lb_in.at[p], ss.at[8], rs.at[8], g, to).start()
        return carry

    lax.fori_loop(0, PACK - 1, l_start, 0)
    lb_in[p] = lb[p]
    dall = st_in.at[0:DP - 1]
    remote(dall, dall, ss.at[7], rs.at[7], g, sib).wait_recv()
    inv_all = lax.rsqrt((ds_in[0] + ds_in[1]).reshape(8, 128))
    l31 = lb_in.at[0:PACK - 1]
    remote(l31, l31, ss.at[8], rs.at[8], g, sib).wait_recv()
    acc = jnp.zeros((16, 128), F32)
    for i in range(PACK):
        acc = acc + lb_in[i].astype(F32)
    col_id = iota((8, 128), 0) * 128 + iota((8, 128), 1)
    partner = part_ref[...]

    def whole(x):
        return jnp.sum(jnp.sum(x, axis=1, keepdims=True), axis=0, keepdims=True)

    losses = []
    exps = []
    for i in range(2):
        row_id = g * n_stmt + p * 2 + i
        diag = col_id == row_id
        own_inv = whole(jnp.where(diag, inv_all, 0.0))
        logit = acc[8 * i:8 * i + 8] * inv_all * (own_inv * (1.0 / WARMTH))
        e = jnp.where(diag, 0.0, jnp.exp(logit))
        own_partner = whole(jnp.where(diag, partner.astype(F32), 0.0))
        target = whole(jnp.where(col_id.astype(F32) == own_partner, logit, 0.0))
        losses.append(jnp.log(whole(e)) - target)
        exps.append(e)
    lane2 = iota((1, 2), 1)
    loss_ref[...] = jnp.where(lane2 == 0, losses[0], losses[1])
    ub[p] = jnp.concatenate(exps, axis=0).astype(BF16)

    def u_start(i, carry):
        remote(ub.at[p], ub.at[p], ss.at[9], rs.at[9], g, pack_peer(i)).start()
        return carry

    lax.fori_loop(0, PACK - 1, u_start, 0)
    u31 = ub.at[0:PACK - 1]
    remote(u31, u31, ss.at[9], rs.at[9], g, sib).wait_recv()
    uf[...] = ub[...].reshape(PACK * 16, 128).astype(F32)
    mats = [uf[pl.ds(j, n_stmt, stride=8), :] for j in range(8)]
    row_sum = mats[0]
    for j in range(1, 8):
        row_sum = row_sum + mats[j]
    inv_sum = 1.0 / jnp.sum(row_sum, axis=1, keepdims=True)
    inv_row = jnp.sum(jnp.where(lane == sub + 64, inv_sum, 0.0), axis=0, keepdims=True)
    ls_own[...] = own_half(inv_row)
    ls_in[odd, half_row] = ls_own[...]

    def e_start(i, carry):
        remote(ls_own, ls_in.at[odd, half_row], ss.at[10], rs.at[10], dp_peer(i), p).start()
        return carry

    lax.fori_loop(0, DP - 1, e_start, 0)
    row_f = (g * n_stmt + iota((n_stmt, 1), 0)).astype(F32)
    part_f = partner.astype(F32)
    own_part_col = jnp.zeros((n_stmt, 1), F32)
    for j in range(8):
        own_part_col = own_part_col + jnp.sum(
            jnp.where((lane + 128 * j).astype(F32) == row_f, part_f[j:j + 1, :], 0.0), axis=1, keepdims=True
        )
    pairs = []
    logs = []
    for j in range(8):
        cid = (lane + 128 * j).astype(F32)
        pairs.append(
            jnp.where(cid == own_part_col, 1.0, 0.0) + jnp.where(part_f[j:j + 1, :] == row_f, 1.0, 0.0)
        )
        logs.append(jnp.log(jnp.maximum(mats[j], 1e-30)))
    remote(dall, dall, ss.at[10], rs.at[10], g, sib).wait_recv()
    sums_all = (ls_in[0] + ls_in[1]).reshape(8, 128)
    grad = jnp.zeros((n_stmt, 128), F32)
    inner_acc = jnp.zeros((n_stmt, 128), F32)
    for j in range(8):
        wj = mats[j] * (inv_sum + sums_all[j:j + 1, :]) - pairs[j]
        inner_acc = inner_acc + wj * logs[j]
        grad = grad + dot(
            (wj * inv_all[j:j + 1, :]).astype(BF16), pb[2 * j:2 * j + 2].reshape(128, 128)
        )
    inner = jnp.sum(inner_acc, axis=1, keepdims=True)
    out = grad * (1.0 / WARMTH) - f32feat * (inv_norm * inner)
    grad_ref[...] = (out * fgain * (inv_norm * float(PACK * 128) ** 0.5)).astype(BF16)

    x15 = x_ref.at[0, :, 0:(CHIPS - 1) * 128]
    remote(x15, x15, x_send, f_recv, g, sib).wait_send()
    remote(f_all, f_all, f_send, f_recv, g, sib).wait_send()
    w_copy.wait_send()
    for i, view in ((1, q31), (2, o31), (3, att.at[0]), (4, po_out), (5, p15), (6, s31), (7, dall), (8, l31), (9, u31), (10, dall)):
        remote(view, view, ss.at[i], rs.at[i], g, sib).wait_send()


def local(
    hidden_in, attn_gain, w_query, query_gain, cached_keys, cached_values, w_out, final_gain,
    lengths, pack_order, partner,
):
    n = hidden_in.shape[0]
    toks, kvw = cached_keys.shape
    width = w_query.shape[0]
    vmem = pl.BlockSpec(memory_space=pltpu.VMEM)
    hbm = pl.BlockSpec(memory_space=pl.ANY)
    V = pltpu.VMEM
    dma = pltpu.SemaphoreType.DMA
    pooled, loss, grad = pl.pallas_call(
        kernel,
        out_shape=(
            jax.ShapeDtypeStruct((n, 128), BF16),
            jax.ShapeDtypeStruct((1, 2), F32),
            jax.ShapeDtypeStruct((n, 128), BF16),
        ),
        in_specs=[vmem, vmem, hbm, vmem, hbm, hbm, hbm, vmem, vmem, vmem, vmem],
        out_specs=(vmem, vmem, vmem),
        scratch_shapes=[
            V((2, n + 16, CHIPS * 128), BF16),
            V((2, CHIPS, 128, 128), BF16),
            V((toks, kvw), BF16),
            V((toks, kvw), BF16),
            V((2, 128, width), BF16),
            V((n + 16, 128), BF16),
            V((8, 128), F32),
            V((PACK * SLOTS, 128), BF16),
            V((4 * n, PACK * SLOTS), BF16),
            V((4 * SLOTS, toks), F32),
            V((n, 128), F32),
            V((n, 128), F32),
            V((PACK, SLOTS, 128), BF16),
            V((PACK, SLOTS, 128), BF16),
            V((PACK, SLOTS, 128), BF16),
            V((PACK, SLOTS, 128), BF16),
            V((2, n, 128), BF16),
            V((CHIPS - 1, n, 128), BF16),
            V((CHIPS - 1, n, 128), BF16),
            V((DP, n, 128), BF16),
            V((1, 128), F32),
            V((PACK, 1, 128), F32),
            V((1, 128), F32),
            V((2, 8, 1, 128), F32),
            V((n * 8, 128), F32),
            V((PACK, 16, 128), BF16),
            V((PACK, 16, 128), BF16),
            V((PACK, 16, 128), BF16),
            V((1, 128), F32),
            V((2, 8, 1, 128), F32),
            V((n * 8, 128), F32),
            dma((5,)),
            dma(()),
            dma((CHIPS - 1,)),
            dma(()),
            dma(()),
            dma((11,)),
            dma((11,)),
        ],
        compiler_params=pltpu.CompilerParams(
            collective_id=0, has_side_effects=True, vmem_limit_bytes=48 * 1024 * 1024
        ),
    )(
        hidden_in,
        attn_gain.reshape(1, 128),
        w_query.reshape(CHIPS, 2, 128, 128),
        query_gain.reshape(1, 128),
        cached_keys,
        cached_values,
        w_out,
        final_gain.reshape(1, 128),
        lengths,
        pack_order,
        partner.reshape(8, 128),
    )
    return pooled, loss.reshape(2), grad


def solution(mesh):
    in_specs = (
        P("dp", "pack"),
        P("pack"),
        P(None, "pack"),
        P(),
        P(("dp", "pack"), None),
        P(("dp", "pack"), None),
        P("pack", None),
        P("pack"),
        P("dp", None),
        P("dp", None),
        P(),
    )
    out_specs = (P("dp", "pack"), P(("dp", "pack")), P("dp", "pack"))
    return jax.shard_map(local, mesh=mesh, in_specs=in_specs, out_specs=out_specs, check_vma=False)
```

```python
import math

import jax
import jax.numpy as jnp
from jax import lax
from jax.experimental import pallas as pl
from jax.experimental.pallas import tpu as pltpu
from jax.sharding import PartitionSpec as P

EPSILON = 1e-06
WARMTH = 0.05
ROPE_BASE = 1000000.0
MASKED = -1e30
F32 = jnp.float32
BF16 = jnp.bfloat16
I32 = jnp.int32

SLOTS = 24
STAT = SLOTS - 1
PACK = 32
CHIPS = 16
DP = 16
MESH = pl.DeviceIdType.MESH


def far_first(k, half):
    return half + (1 - 2 * (k % 2)) * ((k + 1) // 2)


def each(n, step):
    for i in range(n):
        step(i)


def dot_t(a, b):
    return lax.dot_general(a, b, (((1,), (1,)), ((), ())), preferred_element_type=F32)


def dot(a, b):
    return jnp.dot(a, b, preferred_element_type=F32)


def iota(shape, dim):
    return lax.broadcasted_iota(I32, shape, dim)


def kernel(
    hid_ref, again_ref, wq_hbm, qgain_ref, k_hbm, v_hbm, wo_hbm, fgain_ref, len_ref, ord_ref, part_ref,
    pooled_ref, loss_ref, grad_ref,
    x_ref, qx, wq, kk, vv, wo, msg, ints, selbig, sel, bias, cosr, sinr,
    sq, qb, ob_out, ob, att, po_out, po_in, pb, st_own, st_in, ds_own, ds_in,
    pls, lb, lb_in, ub, ls_own, ls_in, uf,
    load_sem, ss, rs, x_recv,
):
    g = lax.axis_index("dp")
    p = lax.axis_index("pack")
    z, y, c = lax.div(p, 16), lax.div(lax.rem(p, 16), 2), lax.rem(p, 2)
    sib = p + 1 - 2 * c
    chip = z * 8 + y
    n_stmt = hid_ref.shape[0]

    def pack_peer(i):
        k, r = i // 4, i % 4
        py = lax.rem(y + far_first(k, 4), 8)
        pz = (z, 1 - z)[1 - r // 2]
        pc = (c, 1 - c)[1 - r % 2]
        return pz * 16 + py * 2 + pc

    def chip_peer(i):
        py = lax.rem(y + far_first(i // 2, 4), 8)
        pz = (z, 1 - z)[1 - i % 2]
        return pz * 8 + py

    gx, gz = lax.div(g, 4), lax.rem(g, 4)

    def dp_peer(i):
        a, b = i // 4, i % 4
        return lax.rem(gx + far_first(a, 2), 4) * 4 + lax.rem(gz + far_first(b, 2), 4)

    def remote(src, dst, send, recv, dg, dp_):
        return pltpu.make_async_remote_copy(
            src_ref=src, dst_ref=dst, send_sem=send, recv_sem=recv,
            device_id=(dg, dp_), device_id_type=MESH,
        )

    pending = []
    loads = [
        pltpu.make_async_copy(wq_hbm.at[:, c], wq.at[c], load_sem.at[0]),
        pltpu.make_async_copy(k_hbm, kk, load_sem.at[1]),
        pltpu.make_async_copy(v_hbm, vv, load_sem.at[2]),
        pltpu.make_async_copy(wo_hbm, wo.at[c], load_sem.at[3]),
    ]
    barrier = pltpu.get_barrier_semaphore()

    def greet_pack(i):
        pl.semaphore_signal(barrier, inc=1, device_id=(g, pack_peer(i)), device_id_type=MESH)

    def greet_dp(i):
        pl.semaphore_signal(barrier, inc=1, device_id=(dp_peer(i), p), device_id_type=MESH)

    each(DP - 1, greet_dp)
    each(PACK - 1, greet_pack)
    for load in loads:
        load.start()

    lane = iota((n_stmt, 128), 1)
    sub = iota((n_stmt, 128), 0)
    same = lane == sub
    lane1 = iota((1, 128), 1)

    def to_row(col):
        return jnp.sum(jnp.where(same, col, 0.0), axis=0, keepdims=True)

    def to_col(row):
        return jnp.sum(jnp.where(same, row, 0.0), axis=1, keepdims=True)

    row8 = iota((8, 128), 0)
    h32 = hid_ref[...].astype(F32)
    msg[0:n_stmt, :] = (h32 * again_ref[...]).astype(BF16)
    sq_row = to_row(jnp.sum(h32 * h32, axis=1, keepdims=True))
    sq_hi = sq_row.astype(BF16).astype(F32)
    msg[n_stmt:, :] = jnp.where(
        row8 == 0, sq_hi, jnp.where(row8 == 1, sq_row - sq_hi, 0.0)
    ).astype(BF16)

    pl.semaphore_wait(barrier, PACK - 1 + DP - 1)

    wq_copy = remote(wq_hbm.at[:, 1 - c], wq.at[c], ss.at[11], rs.at[11], g, sib)

    def x_start(i):
        remote(msg, x_ref.at[i], ss.at[0], x_recv.at[i // 4], g, chip_peer(i) * 2 + c).start()

    def source_chip(i):
        py = lax.rem(y + 8 - far_first(i // 2, 4), 8)
        pz = (z, 1 - z)[1 - i % 2]
        return pz * 8 + py

    each(CHIPS - 1, x_start)
    wq_copy.start()
    x_ref[CHIPS - 1] = msg[...]

    ints[...] = jnp.where(row8 == 1, -1.0, 0.0)
    ints[0:1, 0:n_stmt] = len_ref[...].astype(F32)
    ints[1:2, 0:n_stmt] = ord_ref[...].astype(F32)
    len_row = ints[0:1, :]
    ord_row = ints[1:2, :]
    len_col = to_col(len_row)
    lane_f = lane.astype(F32)
    sub_f = sub.astype(F32)
    at = sub_f == ord_row
    plen_row = jnp.sum(jnp.where(at, len_col, 0.0), axis=0, keepdims=True)
    plen_col = to_col(plen_row)
    end_row = jnp.sum(jnp.where(sub <= lane, plen_col, 0.0), axis=0, keepdims=True)
    start_row = end_row - plen_row
    place_col = jnp.sum(jnp.where(at, lane_f, 0.0), axis=1, keepdims=True)
    place_row = jnp.where(lane1 < n_stmt, to_row(place_col), -1000.0)
    start_col = jnp.sum(jnp.where(at, start_row, 0.0), axis=1, keepdims=True)
    end_col = jnp.sum(jnp.where(at, end_row, 0.0), axis=1, keepdims=True)
    tokens = float(k_hbm.shape[0])
    end_real = jnp.where(lane1 < n_stmt, end_row, 1e9)

    def before(tok):
        return jnp.sum(jnp.where(end_real <= tok, 1.0, 0.0), axis=1, keepdims=True)

    b3 = iota((PACK, SLOTS, 128), 0).reshape(PACK * SLOTS, 128).astype(F32)
    j3 = iota((PACK, SLOTS, 128), 1).reshape(PACK * SLOTS, 128).astype(F32)
    first_big = before(b3 * tokens)
    selbig[...] = jnp.where(place_row == first_big + j3, 1.0, 0.0).astype(BF16)

    block_a = jnp.floor((start_col + 0.5) * (1.0 / tokens))
    block_b = jnp.floor((end_col - 0.5) * (1.0 / tokens))
    slot_a = place_col - before(block_a * tokens)
    slot_b = place_col - before(block_b * tokens)
    wide = iota((n_stmt, PACK * SLOTS), 1).astype(F32)
    for i, (blk, slot) in enumerate(
        ((block_a, slot_a), (block_b, slot_b), (block_a, float(STAT)), (block_b, float(STAT)))
    ):
        sel[i * n_stmt:(i + 1) * n_stmt, :] = jnp.where(
            wide == blk * SLOTS + slot, 1.0, 0.0
        ).astype(BF16)

    pf = p.astype(F32)
    slot_id = before(jnp.zeros((SLOTS, 128), F32) + pf * tokens) + iota((SLOTS, 1), 0).astype(F32)
    lane24 = iota((SLOTS, 128), 1).astype(F32)
    st = jnp.sum(jnp.where(lane24 == slot_id, start_row, 0.0), axis=1, keepdims=True)
    en = jnp.sum(jnp.where(lane24 == slot_id, end_row, 0.0), axis=1, keepdims=True)
    tok = iota((SLOTS, k_hbm.shape[0]), 1).astype(F32) + pf * tokens
    own_bias = jnp.where((tok >= st) & (tok < en), 0.0, MASKED)
    for i in range(4):
        bias[i * SLOTS:(i + 1) * SLOTS, :] = own_bias

    freq = jnp.exp(
        jnp.where(lane1 < 64, lane1, lane1 - 64).astype(F32) * (-2.0 / 128.0 * math.log(ROPE_BASE))
    )
    angle = (len_col - 1.0) * freq
    cosr[...] = jnp.cos(angle)
    sinr[...] = jnp.where(lane < 64, -1.0, 1.0) * jnp.sin(angle)

    w_copy = remote(wo_hbm, wo.at[c], ss.at[13], rs.at[13], g, sib)
    loads[0].wait()
    x15 = x_ref.at[0:CHIPS - 1]
    wq_copy.wait_recv()
    pending.append(remote(x15, x15, ss.at[0], rs.at[0], g, sib).wait_send)
    pending.append(wq_copy.wait_send)
    parts = [jnp.zeros((n_stmt, 128), F32), jnp.zeros((n_stmt, 128), F32)]
    sq_sum = jnp.zeros((8, 128), F32)
    for k in (3, 2, 1, 0):
        group = x_ref.at[4 * k:min(4 * k + 4, CHIPS - 1)]
        remote(group, group, ss.at[0], x_recv.at[k], g, sib).wait_recv()
        slots = list(range(4 * k, 4 * k + 4))
        blocks = jnp.concatenate([x_ref[i, 0:n_stmt, :] for i in slots], axis=1)
        for i in slots:
            sq_sum = sq_sum + x_ref[i, n_stmt:, :].astype(F32)
        for h in range(2):
            head = (1 - c, c)[h]
            weights = jnp.concatenate([wq[head, source_chip(i)] for i in slots], axis=0)
            parts[h] = parts[h] + dot(blocks, weights)
            if k == 0 and h == 0:
                qx[0, 0:n_stmt, :] = parts[0]
                qx[0, n_stmt:, :] = sq_sum
                q_copy = remote(qx.at[0], qx.at[1], ss.at[12], rs.at[12], g, sib)
                q_copy.start()
                pending.append(q_copy.wait_send)
    q_copy.wait_recv()
    q_raw = parts[1] + qx[1, 0:n_stmt, :]
    sq_sum = sq_sum + qx[1, n_stmt:, :]
    total = to_col(sq_sum[0:1, :] + sq_sum[1:2, :])
    mean_sq = jnp.sum(q_raw * q_raw, axis=1, keepdims=True) * (1.0 / 128.0)
    inv = lax.rsqrt(mean_sq + EPSILON * (total * (1.0 / (PACK * 128)) + EPSILON))
    q = q_raw * inv * qgain_ref[...]
    q = (q * cosr[...] + pltpu.roll(q, 64, 1) * sinr[...]).astype(BF16)
    q128 = jnp.concatenate([q, jnp.zeros((128 - n_stmt, 128), BF16)], axis=0)
    sq[...] = dot(selbig[...], q128).astype(BF16).reshape(PACK, SLOTS, 128)

    def q_start(i):
        to = pack_peer(i)
        remote(sq.at[to], qb.at[p], ss.at[1], rs.at[1], g, to).start()

    each(PACK - 1, q_start)
    qb[p] = sq[p]
    w_copy.start()
    loads[1].wait()
    loads[2].wait()
    q31 = qb.at[0:PACK - 1]
    pending.append(remote(q31, q31, ss.at[1], rs.at[1], g, sib).wait_send)
    pending.append(w_copy.wait_send)
    remote(q31, q31, ss.at[1], rs.at[1], g, sib).wait_recv()

    scale = 128 ** -0.5
    jr = iota((SLOTS, 128), 0)
    jl = iota((SLOTS, 128), 1)
    for n in range(8):
        dj = (2, 1, 3, 0)[n // 2]
        kz = (z, 1 - z)[1 - n % 2]
        kh = kz * 4 + lax.rem(lax.div(y, 2) + dj, 4)
        cols = pl.ds(pl.multiple_of(kh * 128, 128), 128)
        qs = qb[pl.ds(kh * 4, 4)].reshape(4 * SLOTS, 128)
        s = dot_t(qs, kk[:, cols]) * scale + bias[...]
        m = jnp.max(s, axis=1, keepdims=True)
        w = jnp.exp(s - m)
        l = jnp.sum(w, axis=1, keepdims=True)
        o = dot(w.astype(BF16), vv[:, cols]) / l
        lse = m + jnp.log(l)
        hi = lse.astype(BF16).astype(F32)
        mid = (lse - hi).astype(BF16).astype(F32)
        lo = lse - hi - mid
        for r in range(4):
            part = slice(r * SLOTS, (r + 1) * SLOTS)
            stat = jnp.where(
                jl == jr, hi[part], jnp.where(
                    jl == jr + 32, mid[part], jnp.where(jl == jr + 64, lo[part], 0.0)
                )
            )
            stat = jnp.sum(stat, axis=0, keepdims=True)
            ob_out[kh * 4 + r] = jnp.where(jr == STAT, stat, o[part]).astype(BF16)
        if n < 7:
            for r in range(4):
                to = kh * 4 + r
                remote(ob_out.at[to], ob.at[p], ss.at[2], rs.at[2], g, to).start()
        else:
            for r in range(1, 4):
                to = kh * 4 + lax.rem(lax.rem(p, 4) + r, 4)
                remote(ob_out.at[to], ob.at[p], ss.at[2], rs.at[2], g, to).start()
    ob[p] = ob_out[p]
    o31 = ob.at[0:PACK - 1]
    pending.append(remote(o31, o31, ss.at[2], rs.at[2], g, sib).wait_send)
    remote(o31, o31, ss.at[2], rs.at[2], g, sib).wait_recv()

    got = dot(sel[...], ob[...].reshape(PACK * SLOTS, 128))

    def stat_of(rows, slot):
        hit = (lane_f == slot) | (lane_f == slot + 32.0) | (lane_f == slot + 64.0)
        return jnp.sum(jnp.where(hit, rows, 0.0), axis=1, keepdims=True)

    lse_a = stat_of(got[2 * n_stmt:3 * n_stmt], slot_a)
    lse_b = stat_of(got[3 * n_stmt:], slot_b)
    top = jnp.maximum(lse_a, lse_b)
    w_a = jnp.exp(lse_a - top)
    w_b = jnp.where(block_a == block_b, 0.0, jnp.exp(lse_b - top))
    own_att = ((w_a * got[0:n_stmt] + w_b * got[n_stmt:2 * n_stmt]) / (w_a + w_b)).astype(BF16)
    att[c] = own_att
    remote(att.at[c], att.at[c], ss.at[3], rs.at[3], g, sib).start()
    pending.append(remote(att.at[c], att.at[c], ss.at[3], rs.at[3], g, sib).wait_send)
    loads[3].wait()
    w_copy.wait_recv()
    remote(att.at[c], att.at[1 - c], ss.at[3], rs.at[3], g, sib).wait_recv()
    heads = jnp.concatenate([att[0], att[1]], axis=1)
    for i in range(CHIPS):
        to = chip_peer(i)
        cols = pl.ds(pl.multiple_of((to * 2 + c) * 128, 128), 128)
        w2 = jnp.concatenate([wo[0, :, cols], wo[1, :, cols]], axis=0)
        part = dot(heads, w2)
        if i < CHIPS - 1:
            po_out[i] = part.astype(BF16)
            remote(po_out.at[i], po_in.at[i], ss.at[4], rs.at[4], g, to * 2 + c).start()
        else:
            own_part = part
    pending.append(remote(po_out, po_in, ss.at[4], rs.at[4], g, sib).wait_send)
    remote(po_out, po_in, ss.at[4], rs.at[4], g, sib).wait_recv()
    hid = hid_ref[...].astype(F32) + own_part
    for i in range(CHIPS - 1):
        hid = hid + po_in[i].astype(F32)

    fgain = fgain_ref[...]
    feat = (hid * fgain).astype(BF16)
    pb[g] = feat
    f32feat = feat.astype(F32)

    def p_start(i):
        remote(pb.at[g], pb.at[g], ss.at[5], rs.at[5], dp_peer(i), p).start()

    each(DP - 1, p_start)
    s1 = jnp.sum(hid * hid, axis=1, keepdims=True)
    s2 = jnp.sum(f32feat * f32feat, axis=1, keepdims=True)
    st_row = jnp.sum(
        jnp.where(same, s1, 0.0) + jnp.where(lane == sub + 64, s2, 0.0), axis=0, keepdims=True
    )
    st_own[...] = st_row
    st_in[p] = st_row

    def s_start(i):
        remote(st_own, st_in.at[p], ss.at[6], rs.at[6], g, pack_peer(i)).start()

    each(PACK - 1, s_start)
    s31 = st_in.at[0:PACK - 1]
    pending.append(remote(s31, s31, ss.at[6], rs.at[6], g, sib).wait_send)
    p15 = pb.at[0:DP - 1]
    pending.append(remote(p15, p15, ss.at[5], rs.at[5], g, sib).wait_send)
    remote(s31, s31, ss.at[6], rs.at[6], g, sib).wait_recv()
    st_row = jnp.sum(st_in[...], axis=0)
    odd = lax.rem(g, 2)
    half_row = lax.div(g, 2)
    in_half = lax.div(lane1, 64) == odd

    def own_half(row):
        return jnp.where(in_half, jnp.where(odd == 1, row, pltpu.roll(row, 64, 1)), 0.0)

    ds_own[...] = own_half(st_row)
    ds_in[odd, half_row] = ds_own[...]

    def d_start(i):
        remote(ds_own, ds_in.at[odd, half_row], ss.at[7], rs.at[7], dp_peer(i), p).start()

    each(DP - 1, d_start)
    dall = st_in.at[0:DP - 1]
    pending.append(remote(dall, dall, ss.at[7], rs.at[7], g, sib).wait_send)
    s1_all = to_col(jnp.where(lane1 < 64, st_row, 0.0))
    s2_all = to_col(jnp.where(lane1 < 64, pltpu.roll(st_row, 64, 1), 0.0))
    inv_norm = lax.rsqrt(s2_all)
    rms = jnp.sqrt(s1_all * (1.0 / (PACK * 128)) + EPSILON)
    pooled_ref[...] = (hid / rms * fgain).astype(BF16)
    remote(p15, p15, ss.at[5], rs.at[5], g, sib).wait_recv()

    for j in range(8):
        cols = pb[2 * j:2 * j + 2].reshape(128, 128)
        pls[pl.ds(j, n_stmt, stride=8), :] = dot_t(feat, cols)
    lb[...] = pls[...].astype(BF16).reshape(PACK, 16, 128)

    def l_start(i):
        to = pack_peer(i)
        remote(lb.at[to], lb_in.at[p], ss.at[8], rs.at[8], g, to).start()

    each(PACK - 1, l_start)
    lb_in[p] = lb[p]
    remote(dall, dall, ss.at[7], rs.at[7], g, sib).wait_recv()
    inv_all = lax.rsqrt((ds_in[0] + ds_in[1]).reshape(8, 128))
    l31 = lb_in.at[0:PACK - 1]
    pending.append(remote(l31, l31, ss.at[8], rs.at[8], g, sib).wait_send)
    remote(l31, l31, ss.at[8], rs.at[8], g, sib).wait_recv()
    acc = jnp.zeros((16, 128), F32)
    for i in range(PACK):
        acc = acc + lb_in[i].astype(F32)
    col_id = iota((8, 128), 0) * 128 + iota((8, 128), 1)
    partner = part_ref[...]

    def whole(x):
        return jnp.sum(jnp.sum(x, axis=1, keepdims=True), axis=0, keepdims=True)

    losses = []
    exps = []
    for i in range(2):
        row_id = g * n_stmt + p * 2 + i
        diag = col_id == row_id
        own_inv = whole(jnp.where(diag, inv_all, 0.0))
        logit = acc[8 * i:8 * i + 8] * inv_all * (own_inv * (1.0 / WARMTH))
        e = jnp.where(diag, 0.0, jnp.exp(logit))
        own_partner = whole(jnp.where(diag, partner.astype(F32), 0.0))
        target = whole(jnp.where(col_id.astype(F32) == own_partner, logit, 0.0))
        losses.append(jnp.log(whole(e)) - target)
        exps.append(e)
    lane2 = iota((1, 2), 1)
    loss_ref[...] = jnp.where(lane2 == 0, losses[0], losses[1])
    ub[p] = jnp.concatenate(exps, axis=0).astype(BF16)

    def u_start(i):
        remote(ub.at[p], ub.at[p], ss.at[9], rs.at[9], g, pack_peer(i)).start()

    each(PACK - 1, u_start)
    u31 = ub.at[0:PACK - 1]
    pending.append(remote(u31, u31, ss.at[9], rs.at[9], g, sib).wait_send)
    remote(u31, u31, ss.at[9], rs.at[9], g, sib).wait_recv()
    uf[...] = ub[...].reshape(PACK * 16, 128).astype(F32)
    mats = [uf[pl.ds(j, n_stmt, stride=8), :] for j in range(8)]
    row_sum = mats[0]
    for j in range(1, 8):
        row_sum = row_sum + mats[j]
    inv_sum = 1.0 / jnp.sum(row_sum, axis=1, keepdims=True)
    inv_row = jnp.sum(jnp.where(lane == sub + 64, inv_sum, 0.0), axis=0, keepdims=True)
    ls_own[...] = own_half(inv_row)
    ls_in[odd, half_row] = ls_own[...]

    def e_start(i):
        remote(ls_own, ls_in.at[odd, half_row], ss.at[10], rs.at[10], dp_peer(i), p).start()

    each(DP - 1, e_start)
    row_f = (g * n_stmt + iota((n_stmt, 1), 0)).astype(F32)
    part_f = partner.astype(F32)
    own_part_col = jnp.zeros((n_stmt, 1), F32)
    for j in range(8):
        own_part_col = own_part_col + jnp.sum(
            jnp.where((lane + 128 * j).astype(F32) == row_f, part_f[j:j + 1, :], 0.0), axis=1, keepdims=True
        )
    pairs = []
    logs = []
    for j in range(8):
        cid = (lane + 128 * j).astype(F32)
        pairs.append(
            jnp.where(cid == own_part_col, 1.0, 0.0) + jnp.where(part_f[j:j + 1, :] == row_f, 1.0, 0.0)
        )
        logs.append(jnp.log(jnp.maximum(mats[j], 1e-30)))
    pending.append(remote(dall, dall, ss.at[10], rs.at[10], g, sib).wait_send)
    remote(dall, dall, ss.at[10], rs.at[10], g, sib).wait_recv()
    sums_all = (ls_in[0] + ls_in[1]).reshape(8, 128)
    grad = jnp.zeros((n_stmt, 128), F32)
    inner_acc = jnp.zeros((n_stmt, 128), F32)
    for j in range(8):
        wj = mats[j] * (inv_sum + sums_all[j:j + 1, :]) - pairs[j]
        inner_acc = inner_acc + wj * logs[j]
        grad = grad + dot(
            (wj * inv_all[j:j + 1, :]).astype(BF16), pb[2 * j:2 * j + 2].reshape(128, 128)
        )
    inner = jnp.sum(inner_acc, axis=1, keepdims=True)
    out = grad * (1.0 / WARMTH) - f32feat * (inv_norm * inner)
    grad_ref[...] = (out * fgain * (inv_norm * float(PACK * 128) ** 0.5)).astype(BF16)

    for wait in pending:
        wait()


def local(
    hidden_in, attn_gain, w_query, query_gain, cached_keys, cached_values, w_out, final_gain,
    lengths, pack_order, partner,
):
    n = hidden_in.shape[0]
    toks, kvw = cached_keys.shape
    width = w_query.shape[0]
    vmem = pl.BlockSpec(memory_space=pltpu.VMEM)
    hbm = pl.BlockSpec(memory_space=pltpu.HBM)
    V = pltpu.VMEM
    dma = pltpu.SemaphoreType.DMA
    pooled, loss, grad = pl.pallas_call(
        kernel,
        out_shape=(
            jax.ShapeDtypeStruct((n, 128), BF16),
            jax.ShapeDtypeStruct((1, 2), F32),
            jax.ShapeDtypeStruct((n, 128), BF16),
        ),
        in_specs=[vmem, vmem, hbm, vmem, hbm, hbm, hbm, vmem, vmem, vmem, vmem],
        out_specs=(vmem, vmem, vmem),
        scratch_shapes=[
            V((CHIPS, n + 8, 128), BF16),
            V((2, n + 8, 128), F32),
            V((2, CHIPS, 128, 128), BF16),
            V((toks, kvw), BF16),
            V((toks, kvw), BF16),
            V((2, 128, width), BF16),
            V((n + 8, 128), BF16),
            V((8, 128), F32),
            V((PACK * SLOTS, 128), BF16),
            V((4 * n, PACK * SLOTS), BF16),
            V((4 * SLOTS, toks), F32),
            V((n, 128), F32),
            V((n, 128), F32),
            V((PACK, SLOTS, 128), BF16),
            V((PACK, SLOTS, 128), BF16),
            V((PACK, SLOTS, 128), BF16),
            V((PACK, SLOTS, 128), BF16),
            V((2, n, 128), BF16),
            V((CHIPS - 1, n, 128), BF16),
            V((CHIPS - 1, n, 128), BF16),
            V((DP, n, 128), BF16),
            V((1, 128), F32),
            V((PACK, 1, 128), F32),
            V((1, 128), F32),
            V((2, 8, 1, 128), F32),
            V((n * 8, 128), F32),
            V((PACK, 16, 128), BF16),
            V((PACK, 16, 128), BF16),
            V((PACK, 16, 128), BF16),
            V((1, 128), F32),
            V((2, 8, 1, 128), F32),
            V((n * 8, 128), F32),
            dma((4,)),
            dma((14,)),
            dma((14,)),
            dma((4,)),
        ],
        compiler_params=pltpu.CompilerParams(
            collective_id=0, has_side_effects=True
        ),
    )(
        hidden_in,
        attn_gain.reshape(1, 128),
        w_query.reshape(CHIPS, 2, 128, 128),
        query_gain.reshape(1, 128),
        cached_keys,
        cached_values,
        w_out,
        final_gain.reshape(1, 128),
        lengths,
        pack_order,
        partner.reshape(8, 128),
    )
    return pooled, loss.reshape(2), grad


def solution(mesh):
    in_specs = (
        P("dp", "pack"),
        P("pack"),
        P(None, "pack"),
        P(),
        P(("dp", "pack"), None),
        P(("dp", "pack"), None),
        P("pack", None),
        P("pack"),
        P("dp", None),
        P("dp", None),
        P(),
    )
    out_specs = (P("dp", "pack"), P(("dp", "pack")), P("dp", "pack"))
    return jax.shard_map(local, mesh=mesh, in_specs=in_specs, out_specs=out_specs, check_vma=False)
```

```python
import math

import jax
import jax.numpy as jnp
from jax import lax
from jax.experimental import pallas as pl
from jax.experimental.pallas import tpu as pltpu
from jax.sharding import PartitionSpec as P

EPSILON = 1e-06
WARMTH = 0.05
ROPE_BASE = 1000000.0
MASKED = -1e30
F32 = jnp.float32
BF16 = jnp.bfloat16
I32 = jnp.int32

SLOTS = 24
STAT = SLOTS - 1
PACK = 32
CHIPS = 16
DP = 16
MESH = pl.DeviceIdType.MESH


def far_first(k, half):
    return half + (1 - 2 * (k % 2)) * ((k + 1) // 2)


def each(n, step):
    for i in range(n):
        step(i)


def dot_t(a, b):
    return lax.dot_general(a, b, (((1,), (1,)), ((), ())), preferred_element_type=F32)


def dot(a, b):
    return jnp.dot(a, b, preferred_element_type=F32)


def iota(shape, dim):
    return lax.broadcasted_iota(I32, shape, dim)


def kernel(
    hid_ref, again_ref, wq_hbm, qgain_ref, k_hbm, v_hbm, wo_hbm, fgain_ref, len_ref, ord_ref, part_ref,
    out_ref, loss_ref,
    x_ref, qx, wq, kk, vv, wo, msg, ints, selbig, sel, bias, cosr, sinr,
    sq, qb, ob_out, ob, att, po_out, po_in, pb, st_own, st_in, ds_own, ds_in,
    pls, lb, lb_in, ub, ls_own, ls_in, uf,
    load_sem, ss, rs, x_recv, relay,
):
    g = lax.axis_index("dp")
    p = lax.axis_index("pack")
    z, y, c = lax.div(p, 16), lax.div(lax.rem(p, 16), 2), lax.rem(p, 2)
    sib = p + 1 - 2 * c
    chip = z * 8 + y
    n_stmt = hid_ref.shape[0]

    def pack_peer(i):
        k, r = i // 4, i % 4
        py = lax.rem(y + far_first(k, 4), 8)
        pz = (z, 1 - z)[1 - r // 2]
        pc = (c, 1 - c)[1 - r % 2]
        return pz * 16 + py * 2 + pc

    def chip_peer(i):
        py = lax.rem(y + far_first(i // 2, 4), 8)
        pz = (z, 1 - z)[1 - i % 2]
        return pz * 8 + py

    gx, gz = lax.div(g, 4), lax.rem(g, 4)

    def dp_peer(i):
        a, b = i // 4, i % 4
        return lax.rem(gx + far_first(a, 2), 4) * 4 + lax.rem(gz + far_first(b, 2), 4)

    def remote(src, dst, send, recv, dg, dp_):
        return pltpu.make_async_remote_copy(
            src_ref=src, dst_ref=dst, send_sem=send, recv_sem=recv,
            device_id=(dg, dp_), device_id_type=MESH,
        )

    pending = []
    loads = [
        pltpu.make_async_copy(wq_hbm.at[:, c], wq.at[c], load_sem.at[0]),
        pltpu.make_async_copy(k_hbm, kk, load_sem.at[1]),
        pltpu.make_async_copy(v_hbm, vv, load_sem.at[2]),
        pltpu.make_async_copy(wo_hbm, wo.at[c], load_sem.at[3]),
    ]
    barrier = pltpu.get_barrier_semaphore()

    def greet_pack(i):
        pl.semaphore_signal(barrier, inc=1, device_id=(g, pack_peer(i)), device_id_type=MESH)

    def group_at(dx, dz):
        return lax.rem(gx + dx, 4) * 4 + lax.rem(gz + dz, 4)

    near = [group_at(*d) for d in ((1, 0), (3, 0), (0, 1), (0, 3))]
    far = [group_at(*d) for d in ((2, 0), (0, 2), (1, 1), (1, 3), (3, 1), (3, 3))]

    def tell(groups, sem):
        for to in groups:
            pl.semaphore_signal(sem, inc=1, device_id=(to, p), device_id_type=MESH)

    tell(near, barrier)
    each(PACK - 1, greet_pack)
    for load in loads:
        load.start()

    lane = iota((n_stmt, 128), 1)
    sub = iota((n_stmt, 128), 0)
    same = lane == sub
    lane1 = iota((1, 128), 1)

    def to_row(col):
        return jnp.sum(jnp.where(same, col, 0.0), axis=0, keepdims=True)

    def to_col(row):
        return jnp.sum(jnp.where(same, row, 0.0), axis=1, keepdims=True)

    row8 = iota((8, 128), 0)
    h32 = hid_ref[...].astype(F32)
    msg[0:n_stmt, :] = (h32 * again_ref[...]).astype(BF16)
    sq_row = to_row(jnp.sum(h32 * h32, axis=1, keepdims=True))
    sq_hi = sq_row.astype(BF16).astype(F32)
    msg[n_stmt:, :] = jnp.where(
        row8 == 0, sq_hi, jnp.where(row8 == 1, sq_row - sq_hi, 0.0)
    ).astype(BF16)

    pl.semaphore_wait(barrier, PACK - 1 + 4)

    wq_copy = remote(wq_hbm.at[:, 1 - c], wq.at[c], ss.at[11], rs.at[11], g, sib)

    def x_start(i):
        remote(msg, x_ref.at[i], ss.at[0], x_recv.at[i // 4], g, chip_peer(i) * 2 + c).start()

    def source_chip(i):
        py = lax.rem(y + 8 - far_first(i // 2, 4), 8)
        pz = (z, 1 - z)[1 - i % 2]
        return pz * 8 + py

    each(CHIPS - 1, x_start)
    wq_copy.start()
    tell(near, relay.at[0])
    x_ref[CHIPS - 1] = msg[...]

    ints[...] = jnp.where(row8 == 1, -1.0, 0.0)
    ints[0:1, 0:n_stmt] = len_ref[...].astype(F32)
    ints[1:2, 0:n_stmt] = ord_ref[...].astype(F32)
    len_row = ints[0:1, :]
    ord_row = ints[1:2, :]
    len_col = to_col(len_row)
    lane_f = lane.astype(F32)
    sub_f = sub.astype(F32)
    at = sub_f == ord_row
    plen_row = jnp.sum(jnp.where(at, len_col, 0.0), axis=0, keepdims=True)
    plen_col = to_col(plen_row)
    end_row = jnp.sum(jnp.where(sub <= lane, plen_col, 0.0), axis=0, keepdims=True)
    start_row = end_row - plen_row
    place_col = jnp.sum(jnp.where(at, lane_f, 0.0), axis=1, keepdims=True)
    place_row = jnp.where(lane1 < n_stmt, to_row(place_col), -1000.0)
    start_col = jnp.sum(jnp.where(at, start_row, 0.0), axis=1, keepdims=True)
    end_col = jnp.sum(jnp.where(at, end_row, 0.0), axis=1, keepdims=True)
    tokens = float(k_hbm.shape[0])
    end_real = jnp.where(lane1 < n_stmt, end_row, 1e9)

    def before(tok):
        return jnp.sum(jnp.where(end_real <= tok, 1.0, 0.0), axis=1, keepdims=True)

    b3 = iota((PACK, SLOTS, 128), 0).reshape(PACK * SLOTS, 128).astype(F32)
    j3 = iota((PACK, SLOTS, 128), 1).reshape(PACK * SLOTS, 128).astype(F32)
    first_big = before(b3 * tokens)
    selbig[...] = jnp.where(place_row == first_big + j3, 1.0, 0.0).astype(BF16)

    block_a = jnp.floor((start_col + 0.5) * (1.0 / tokens))
    block_b = jnp.floor((end_col - 0.5) * (1.0 / tokens))
    slot_a = place_col - before(block_a * tokens)
    slot_b = place_col - before(block_b * tokens)
    wide = iota((n_stmt, PACK * SLOTS), 1).astype(F32)
    for i, (blk, slot) in enumerate(
        ((block_a, slot_a), (block_b, slot_b), (block_a, float(STAT)), (block_b, float(STAT)))
    ):
        sel[i * n_stmt:(i + 1) * n_stmt, :] = jnp.where(
            wide == blk * SLOTS + slot, 1.0, 0.0
        ).astype(BF16)

    pf = p.astype(F32)
    slot_id = before(jnp.zeros((SLOTS, 128), F32) + pf * tokens) + iota((SLOTS, 1), 0).astype(F32)
    lane24 = iota((SLOTS, 128), 1).astype(F32)
    st = jnp.sum(jnp.where(lane24 == slot_id, start_row, 0.0), axis=1, keepdims=True)
    en = jnp.sum(jnp.where(lane24 == slot_id, end_row, 0.0), axis=1, keepdims=True)
    tok = iota((SLOTS, k_hbm.shape[0]), 1).astype(F32) + pf * tokens
    own_bias = jnp.where((tok >= st) & (tok < en), 0.0, MASKED)
    for i in range(4):
        bias[i * SLOTS:(i + 1) * SLOTS, :] = own_bias

    freq = jnp.exp(
        jnp.where(lane1 < 64, lane1, lane1 - 64).astype(F32) * (-2.0 / 128.0 * math.log(ROPE_BASE))
    )
    angle = (len_col - 1.0) * freq
    cosr[...] = jnp.cos(angle)
    sinr[...] = jnp.where(lane < 64, -1.0, 1.0) * jnp.sin(angle)

    w_copy = remote(wo_hbm, wo.at[c], ss.at[13], rs.at[13], g, sib)
    loads[0].wait()
    x15 = x_ref.at[0:CHIPS - 1]
    wq_copy.wait_recv()
    pending.append(remote(x15, x15, ss.at[0], rs.at[0], g, sib).wait_send)
    pending.append(wq_copy.wait_send)
    parts = jnp.zeros((n_stmt, 256), F32)
    sq_sum = jnp.zeros((8, 128), F32)
    for k in (3, 2, 1, 0):
        group = x_ref.at[4 * k:min(4 * k + 4, CHIPS - 1)]
        remote(group, group, ss.at[0], x_recv.at[k], g, sib).wait_recv()
        if k == 0:
            pass
        slots = list(range(4 * k, 4 * k + 4))
        blocks = jnp.concatenate([x_ref[i, 0:n_stmt, :] for i in slots], axis=1)
        for i in slots:
            sq_sum = sq_sum + x_ref[i, n_stmt:, :].astype(F32)
        weights = jnp.concatenate(
            [jnp.concatenate([wq[1 - c, source_chip(i)], wq[c, source_chip(i)]], axis=1) for i in slots],
            axis=0,
        )
        parts = parts + dot(blocks, weights)
    qx[0, 0:n_stmt, :] = parts[:, 0:128]
    qx[0, n_stmt:, :] = sq_sum
    q_copy = remote(qx.at[0], qx.at[1], ss.at[12], rs.at[12], g, sib)
    q_copy.start()
    pending.append(q_copy.wait_send)
    q_copy.wait_recv()
    q_raw = parts[:, 128:] + qx[1, 0:n_stmt, :]
    sq_sum = sq_sum + qx[1, n_stmt:, :]
    total = to_col(sq_sum[0:1, :] + sq_sum[1:2, :])
    mean_sq = jnp.sum(q_raw * q_raw, axis=1, keepdims=True) * (1.0 / 128.0)
    inv = lax.rsqrt(mean_sq + EPSILON * (total * (1.0 / (PACK * 128)) + EPSILON))
    q = q_raw * inv * qgain_ref[...]
    q = (q * cosr[...] + pltpu.roll(q, 64, 1) * sinr[...]).astype(BF16)
    q128 = jnp.concatenate([q, jnp.zeros((128 - n_stmt, 128), BF16)], axis=0)
    sq[...] = dot(selbig[...], q128).astype(BF16).reshape(PACK, SLOTS, 128)

    def q_start(i):
        to = pack_peer(i)
        remote(sq.at[to], qb.at[p], ss.at[1], rs.at[1], g, to).start()

    each(PACK - 1, q_start)
    qb[p] = sq[p]
    w_copy.start()
    pl.semaphore_wait(relay.at[0], 4)
    tell(far, relay.at[1])
    loads[1].wait()
    loads[2].wait()
    q31 = qb.at[0:PACK - 1]
    pending.append(remote(q31, q31, ss.at[1], rs.at[1], g, sib).wait_send)
    pending.append(w_copy.wait_send)
    remote(q31, q31, ss.at[1], rs.at[1], g, sib).wait_recv()

    scale = 128 ** -0.5
    jr = iota((SLOTS, 128), 0)
    jl = iota((SLOTS, 128), 1)
    for n in range(8):
        dj = (2, 1, 3, 0)[n // 2]
        kz = (z, 1 - z)[1 - n % 2]
        kh = kz * 4 + lax.rem(lax.div(y, 2) + dj, 4)
        cols = pl.ds(pl.multiple_of(kh * 128, 128), 128)
        qs = qb[pl.ds(kh * 4, 4)].reshape(4 * SLOTS, 128)
        s = dot_t(qs, kk[:, cols]) * scale + bias[...]
        m = jnp.max(s, axis=1, keepdims=True)
        w = jnp.exp(s - m)
        l = jnp.sum(w, axis=1, keepdims=True)
        o = dot(w.astype(BF16), vv[:, cols]) / l
        lse = m + jnp.log(l)
        hi = lse.astype(BF16).astype(F32)
        mid = (lse - hi).astype(BF16).astype(F32)
        lo = lse - hi - mid
        for r in range(4):
            part = slice(r * SLOTS, (r + 1) * SLOTS)
            stat = jnp.where(
                jl == jr, hi[part], jnp.where(
                    jl == jr + 32, mid[part], jnp.where(jl == jr + 64, lo[part], 0.0)
                )
            )
            stat = jnp.sum(stat, axis=0, keepdims=True)
            ob_out[kh * 4 + r] = jnp.where(jr == STAT, stat, o[part]).astype(BF16)
        if n < 7:
            for r in range(4):
                to = kh * 4 + r
                remote(ob_out.at[to], ob.at[p], ss.at[2], rs.at[2], g, to).start()
        else:
            for r in range(1, 4):
                to = kh * 4 + lax.rem(lax.rem(p, 4) + r, 4)
                remote(ob_out.at[to], ob.at[p], ss.at[2], rs.at[2], g, to).start()
    ob[p] = ob_out[p]
    o31 = ob.at[0:PACK - 1]
    pending.append(remote(o31, o31, ss.at[2], rs.at[2], g, sib).wait_send)
    remote(o31, o31, ss.at[2], rs.at[2], g, sib).wait_recv()

    got = dot(sel[...], ob[...].reshape(PACK * SLOTS, 128))

    def stat_of(rows, slot):
        hit = (lane_f == slot) | (lane_f == slot + 32.0) | (lane_f == slot + 64.0)
        return jnp.sum(jnp.where(hit, rows, 0.0), axis=1, keepdims=True)

    lse_a = stat_of(got[2 * n_stmt:3 * n_stmt], slot_a)
    lse_b = stat_of(got[3 * n_stmt:], slot_b)
    top = jnp.maximum(lse_a, lse_b)
    w_a = jnp.exp(lse_a - top)
    w_b = jnp.where(block_a == block_b, 0.0, jnp.exp(lse_b - top))
    own_att = ((w_a * got[0:n_stmt] + w_b * got[n_stmt:2 * n_stmt]) / (w_a + w_b)).astype(BF16)
    att[c] = own_att
    remote(att.at[c], att.at[c], ss.at[3], rs.at[3], g, sib).start()
    pending.append(remote(att.at[c], att.at[c], ss.at[3], rs.at[3], g, sib).wait_send)
    loads[3].wait()
    w_copy.wait_recv()
    remote(att.at[c], att.at[1 - c], ss.at[3], rs.at[3], g, sib).wait_recv()
    pl.semaphore_wait(relay.at[1], 6)
    heads = jnp.concatenate([att[0], att[1]], axis=1)
    for k in range(CHIPS // 2):
        ends = [chip_peer(2 * k), chip_peer(2 * k + 1)]
        cols = [pl.ds(pl.multiple_of((to * 2 + c) * 128, 128), 128) for to in ends]
        w4 = jnp.concatenate(
            [jnp.concatenate([wo[0, :, at_], wo[1, :, at_]], axis=0) for at_ in cols], axis=1
        )
        part = dot(heads, w4)
        for r in range(2):
            i = 2 * k + r
            own_part = part[:, 128 * r:128 * r + 128]
            if i < CHIPS - 1:
                po_out[i] = own_part.astype(BF16)
                remote(po_out.at[i], po_in.at[i], ss.at[4], rs.at[4], g, ends[r] * 2 + c).start()
    pending.append(remote(po_out, po_in, ss.at[4], rs.at[4], g, sib).wait_send)
    remote(po_out, po_in, ss.at[4], rs.at[4], g, sib).wait_recv()
    hid = hid_ref[...].astype(F32) + own_part
    for i in range(CHIPS - 1):
        hid = hid + po_in[i].astype(F32)

    fgain = fgain_ref[...]
    feat = (hid * fgain).astype(BF16)
    pb[g] = feat
    f32feat = feat.astype(F32)

    def p_start(i):
        remote(pb.at[g], pb.at[g], ss.at[5], rs.at[5], dp_peer(i), p).start()

    each(DP - 1, p_start)
    s1 = jnp.sum(hid * hid, axis=1, keepdims=True)
    s2 = jnp.sum(f32feat * f32feat, axis=1, keepdims=True)
    st_row = jnp.sum(
        jnp.where(same, s1, 0.0) + jnp.where(lane == sub + 64, s2, 0.0), axis=0, keepdims=True
    )
    st_own[...] = st_row
    st_in[p] = st_row

    def s_start(i):
        remote(st_own, st_in.at[p], ss.at[6], rs.at[6], g, pack_peer(i)).start()

    each(PACK - 1, s_start)
    s31 = st_in.at[0:PACK - 1]
    pending.append(remote(s31, s31, ss.at[6], rs.at[6], g, sib).wait_send)
    p15 = pb.at[0:DP - 1]
    pending.append(remote(p15, p15, ss.at[5], rs.at[5], g, sib).wait_send)
    remote(s31, s31, ss.at[6], rs.at[6], g, sib).wait_recv()
    st_row = jnp.sum(st_in[...], axis=0)
    odd = lax.rem(g, 2)
    half_row = lax.div(g, 2)
    in_half = lax.div(lane1, 64) == odd

    def own_half(row):
        return jnp.where(in_half, jnp.where(odd == 1, row, pltpu.roll(row, 64, 1)), 0.0)

    ds_own[...] = own_half(st_row)
    ds_in[odd, half_row] = ds_own[...]

    def d_start(i):
        remote(ds_own, ds_in.at[odd, half_row], ss.at[7], rs.at[7], dp_peer(i), p).start()

    each(DP - 1, d_start)
    dall = st_in.at[0:DP - 1]
    pending.append(remote(dall, dall, ss.at[7], rs.at[7], g, sib).wait_send)
    s1_all = to_col(jnp.where(lane1 < 64, st_row, 0.0))
    s2_all = to_col(jnp.where(lane1 < 64, pltpu.roll(st_row, 64, 1), 0.0))
    inv_norm = lax.rsqrt(s2_all)
    rms = jnp.sqrt(s1_all * (1.0 / (PACK * 128)) + EPSILON)
    out_ref[0:n_stmt, :] = (hid / rms * fgain).astype(BF16)
    remote(p15, p15, ss.at[5], rs.at[5], g, sib).wait_recv()

    for j in range(4):
        part = dot_t(feat, pb[4 * j:4 * j + 4].reshape(256, 128))
        for r in range(2):
            pls[pl.ds(2 * j + r, n_stmt, stride=8), :] = part[:, 128 * r:128 * r + 128]
    lb[...] = pls[...].astype(BF16).reshape(PACK, 16, 128)

    def l_start(i):
        to = pack_peer(i)
        remote(lb.at[to], lb_in.at[p], ss.at[8], rs.at[8], g, to).start()

    each(PACK - 1, l_start)
    lb_in[p] = lb[p]
    remote(dall, dall, ss.at[7], rs.at[7], g, sib).wait_recv()
    inv_all = lax.rsqrt((ds_in[0] + ds_in[1]).reshape(8, 128))
    l31 = lb_in.at[0:PACK - 1]
    pending.append(remote(l31, l31, ss.at[8], rs.at[8], g, sib).wait_send)
    remote(l31, l31, ss.at[8], rs.at[8], g, sib).wait_recv()
    acc = jnp.zeros((16, 128), F32)
    for i in range(PACK):
        acc = acc + lb_in[i].astype(F32)
    col_id = iota((8, 128), 0) * 128 + iota((8, 128), 1)
    partner = part_ref[...]

    def whole(x):
        return jnp.sum(jnp.sum(x, axis=1, keepdims=True), axis=0, keepdims=True)

    losses = []
    exps = []
    for i in range(2):
        row_id = g * n_stmt + p * 2 + i
        diag = col_id == row_id
        own_inv = whole(jnp.where(diag, inv_all, 0.0))
        logit = acc[8 * i:8 * i + 8] * inv_all * (own_inv * (1.0 / WARMTH))
        e = jnp.where(diag, 0.0, jnp.exp(logit))
        own_partner = whole(jnp.where(diag, partner.astype(F32), 0.0))
        target = whole(jnp.where(col_id.astype(F32) == own_partner, logit, 0.0))
        losses.append(jnp.log(whole(e)) - target)
        exps.append(e)
    loss_ref[...] = jnp.where(iota((1, 2), 1) == 0, losses[0], losses[1])
    ub[p] = jnp.concatenate(exps, axis=0).astype(BF16)

    def u_start(i):
        remote(ub.at[p], ub.at[p], ss.at[9], rs.at[9], g, pack_peer(i)).start()

    each(PACK - 1, u_start)
    u31 = ub.at[0:PACK - 1]
    pending.append(remote(u31, u31, ss.at[9], rs.at[9], g, sib).wait_send)
    remote(u31, u31, ss.at[9], rs.at[9], g, sib).wait_recv()
    uf[...] = ub[...].reshape(PACK * 16, 128).astype(F32)
    mats = [uf[pl.ds(j, n_stmt, stride=8), :] for j in range(8)]
    row_sum = mats[0]
    for j in range(1, 8):
        row_sum = row_sum + mats[j]
    inv_sum = 1.0 / jnp.sum(row_sum, axis=1, keepdims=True)
    inv_row = jnp.sum(jnp.where(lane == sub + 64, inv_sum, 0.0), axis=0, keepdims=True)
    ls_own[...] = own_half(inv_row)
    ls_in[odd, half_row] = ls_own[...]

    def e_start(i):
        remote(ls_own, ls_in.at[odd, half_row], ss.at[10], rs.at[10], dp_peer(i), p).start()

    each(DP - 1, e_start)
    row_f = (g * n_stmt + iota((n_stmt, 1), 0)).astype(F32)
    part_f = partner.astype(F32)
    own_part_col = jnp.zeros((n_stmt, 1), F32)
    for j in range(8):
        own_part_col = own_part_col + jnp.sum(
            jnp.where((lane + 128 * j).astype(F32) == row_f, part_f[j:j + 1, :], 0.0), axis=1, keepdims=True
        )
    pairs = []
    logs = []
    for j in range(8):
        cid = (lane + 128 * j).astype(F32)
        pairs.append(
            jnp.where(cid == own_part_col, 1.0, 0.0) + jnp.where(part_f[j:j + 1, :] == row_f, 1.0, 0.0)
        )
        logs.append(jnp.log(jnp.maximum(mats[j], 1e-30)))
    pending.append(remote(dall, dall, ss.at[10], rs.at[10], g, sib).wait_send)
    remote(dall, dall, ss.at[10], rs.at[10], g, sib).wait_recv()
    sums_all = (ls_in[0] + ls_in[1]).reshape(8, 128)
    grad = jnp.zeros((n_stmt, 128), F32)
    inner_acc = jnp.zeros((n_stmt, 128), F32)
    for j in range(4):
        scaled = []
        for k in (2 * j, 2 * j + 1):
            wk = mats[k] * (inv_sum + sums_all[k:k + 1, :]) - pairs[k]
            inner_acc = inner_acc + wk * logs[k]
            scaled.append((wk * inv_all[k:k + 1, :]).astype(BF16))
        grad = grad + dot(jnp.concatenate(scaled, axis=1), pb[4 * j:4 * j + 4].reshape(256, 128))
    inner = jnp.sum(inner_acc, axis=1, keepdims=True)
    out = grad * (1.0 / WARMTH) - f32feat * (inv_norm * inner)
    out_ref[n_stmt:, :] = (out * fgain * (inv_norm * float(PACK * 128) ** 0.5)).astype(BF16)

    for wait in pending:
        wait()


def local(
    hidden_in, attn_gain, w_query, query_gain, cached_keys, cached_values, w_out, final_gain,
    lengths, pack_order, partner,
):
    n = hidden_in.shape[0]
    toks, kvw = cached_keys.shape
    width = w_query.shape[0]
    vmem = pl.BlockSpec(memory_space=pltpu.VMEM)
    hbm = pl.BlockSpec(memory_space=pltpu.HBM)
    V = pltpu.VMEM
    dma = pltpu.SemaphoreType.DMA
    out, loss = pl.pallas_call(
        kernel,
        out_shape=(
            jax.ShapeDtypeStruct((2 * n, 128), BF16),
            jax.ShapeDtypeStruct((1, 2), F32),
        ),
        in_specs=[vmem, vmem, hbm, vmem, hbm, hbm, hbm, vmem, vmem, vmem, vmem],
        out_specs=(vmem, vmem),
        scratch_shapes=[
            V((CHIPS, n + 8, 128), BF16),
            V((2, n + 8, 128), F32),
            V((2, CHIPS, 128, 128), BF16),
            V((toks, kvw), BF16),
            V((toks, kvw), BF16),
            V((2, 128, width), BF16),
            V((n + 8, 128), BF16),
            V((8, 128), F32),
            V((PACK * SLOTS, 128), BF16),
            V((4 * n, PACK * SLOTS), BF16),
            V((4 * SLOTS, toks), F32),
            V((n, 128), F32),
            V((n, 128), F32),
            V((PACK, SLOTS, 128), BF16),
            V((PACK, SLOTS, 128), BF16),
            V((PACK, SLOTS, 128), BF16),
            V((PACK, SLOTS, 128), BF16),
            V((2, n, 128), BF16),
            V((CHIPS - 1, n, 128), BF16),
            V((CHIPS - 1, n, 128), BF16),
            V((DP, n, 128), BF16),
            V((1, 128), F32),
            V((PACK, 1, 128), F32),
            V((1, 128), F32),
            V((2, 8, 1, 128), F32),
            V((n * 8, 128), F32),
            V((PACK, 16, 128), BF16),
            V((PACK, 16, 128), BF16),
            V((PACK, 16, 128), BF16),
            V((1, 128), F32),
            V((2, 8, 1, 128), F32),
            V((n * 8, 128), F32),
            dma((4,)),
            dma((14,)),
            dma((14,)),
            dma((4,)),
            pltpu.SemaphoreType.REGULAR((2,)),
        ],
        compiler_params=pltpu.CompilerParams(
            collective_id=0, has_side_effects=True
        ),
    )(
        hidden_in,
        attn_gain.reshape(1, 128),
        w_query.reshape(CHIPS, 2, 128, 128),
        query_gain.reshape(1, 128),
        cached_keys,
        cached_values,
        w_out,
        final_gain.reshape(1, 128),
        lengths,
        pack_order,
        partner.reshape(8, 128),
    )
    return out[0:n], loss.reshape(2), out[n:]


def solution(mesh):
    in_specs = (
        P("dp", "pack"),
        P("pack"),
        P(None, "pack"),
        P(),
        P(("dp", "pack"), None),
        P(("dp", "pack"), None),
        P("pack", None),
        P("pack"),
        P("dp", None),
        P("dp", None),
        P(),
    )
    out_specs = (P("dp", "pack"), P(("dp", "pack")), P("dp", "pack"))
    return jax.shard_map(local, mesh=mesh, in_specs=in_specs, out_specs=out_specs, check_vma=False)
```

```python
import math

import jax
import jax.numpy as jnp
from jax import lax
from jax.experimental import pallas as pl
from jax.experimental.pallas import tpu as pltpu
from jax.sharding import PartitionSpec as P

EPSILON = 1e-06
WARMTH = 0.05
ROPE_BASE = 1000000.0
MASKED = -1e30
F32 = jnp.float32
BF16 = jnp.bfloat16
I32 = jnp.int32

SLOTS = 24
STAT = SLOTS - 1
PACK = 32
CHIPS = 16
DP = 16
MESH = pl.DeviceIdType.MESH


def far_first(k, half):
    return half + (1 - 2 * (k % 2)) * ((k + 1) // 2)


def each(n, step):
    for i in range(n):
        step(i)


def dot_t(a, b):
    return lax.dot_general(a, b, (((1,), (1,)), ((), ())), preferred_element_type=F32)


def dot(a, b):
    return jnp.dot(a, b, preferred_element_type=F32)


def iota(shape, dim):
    return lax.broadcasted_iota(I32, shape, dim)


def kernel(
    hid_ref, again_ref, wq_hbm, qgain_ref, k_hbm, v_hbm, wo_hbm, fgain_ref, len_ref, ord_ref, part_ref,
    out_ref, loss_ref,
    x_ref, qx, wq, kk, vv, wo, msg, ints, selbig, sel, bias, cosr, sinr,
    sq, qb, ob_out, ob, att, po_out, po_in, pb, st_own, st_in, ds_own, ds_in,
    pls, lb, lb_in, ub, ls_own, ls_in, uf,
    load_sem, ss, rs, x_recv, relay,
):
    g = lax.axis_index("dp")
    p = lax.axis_index("pack")
    z, y, c = lax.div(p, 16), lax.div(lax.rem(p, 16), 2), lax.rem(p, 2)
    sib = p + 1 - 2 * c
    chip = z * 8 + y
    n_stmt = hid_ref.shape[0]

    def pack_peer(i):
        k, r = i // 4, i % 4
        py = lax.rem(y + far_first(k, 4), 8)
        pz = (z, 1 - z)[1 - r // 2]
        pc = (c, 1 - c)[1 - r % 2]
        return pz * 16 + py * 2 + pc

    def chip_peer(i):
        py = lax.rem(y + far_first(i // 2, 4), 8)
        pz = (z, 1 - z)[1 - i % 2]
        return pz * 8 + py

    gx, gz = lax.div(g, 4), lax.rem(g, 4)

    def dp_peer(i):
        a, b = i // 4, i % 4
        return lax.rem(gx + far_first(a, 2), 4) * 4 + lax.rem(gz + far_first(b, 2), 4)

    def remote(src, dst, send, recv, dg, dp_):
        return pltpu.make_async_remote_copy(
            src_ref=src, dst_ref=dst, send_sem=send, recv_sem=recv,
            device_id=(dg, dp_), device_id_type=MESH,
        )

    pending = []
    loads = [
        pltpu.make_async_copy(wq_hbm.at[:, c], wq.at[c], load_sem.at[0]),
        pltpu.make_async_copy(k_hbm, kk, load_sem.at[1]),
        pltpu.make_async_copy(v_hbm, vv, load_sem.at[2]),
        pltpu.make_async_copy(wo_hbm, wo.at[c], load_sem.at[3]),
    ]
    barrier = pltpu.get_barrier_semaphore()

    def greet_pack(i):
        pl.semaphore_signal(barrier, inc=1, device_id=(g, pack_peer(i)), device_id_type=MESH)

    def group_at(dx, dz):
        return lax.rem(gx + dx, 4) * 4 + lax.rem(gz + dz, 4)

    near = [group_at(*d) for d in ((1, 0), (3, 0), (0, 1), (0, 3))]
    far = [group_at(*d) for d in ((2, 0), (0, 2), (1, 1), (1, 3), (3, 1), (3, 3))]

    def tell(groups, sem):
        for to in groups:
            pl.semaphore_signal(sem, inc=1, device_id=(to, p), device_id_type=MESH)

    tell(near, barrier)
    each(PACK - 1, greet_pack)
    for load in loads:
        load.start()

    lane = iota((n_stmt, 128), 1)
    sub = iota((n_stmt, 128), 0)
    same = lane == sub
    lane1 = iota((1, 128), 1)

    def to_row(col):
        return jnp.sum(jnp.where(same, col, 0.0), axis=0, keepdims=True)

    def to_col(row):
        return jnp.sum(jnp.where(same, row, 0.0), axis=1, keepdims=True)

    row8 = iota((8, 128), 0)
    h32 = hid_ref[...].astype(F32)
    msg[0:n_stmt, :] = (h32 * again_ref[...]).astype(BF16)
    sq_row = to_row(jnp.sum(h32 * h32, axis=1, keepdims=True))
    sq_hi = sq_row.astype(BF16).astype(F32)
    msg[n_stmt:, :] = jnp.where(
        row8 == 0, sq_hi, jnp.where(row8 == 1, sq_row - sq_hi, 0.0)
    ).astype(BF16)

    pl.semaphore_wait(barrier, PACK - 1 + 4)

    wq_copy = remote(wq_hbm.at[:, 1 - c], wq.at[c], ss.at[11], rs.at[11], g, sib)

    def x_start(i):
        remote(msg, x_ref.at[i], ss.at[0], x_recv.at[i // 4], g, chip_peer(i) * 2 + c).start()

    def source_chip(i):
        py = lax.rem(y + 8 - far_first(i // 2, 4), 8)
        pz = (z, 1 - z)[1 - i % 2]
        return pz * 8 + py

    each(CHIPS - 1, x_start)
    wq_copy.start()
    tell(near, relay.at[0])
    x_ref[CHIPS - 1] = msg[...]

    ints[...] = jnp.where(row8 == 1, -1.0, 0.0)
    ints[0:1, 0:n_stmt] = len_ref[...].astype(F32)
    ints[1:2, 0:n_stmt] = ord_ref[...].astype(F32)
    len_row = ints[0:1, :]
    ord_row = ints[1:2, :]
    len_col = to_col(len_row)
    lane_f = lane.astype(F32)
    sub_f = sub.astype(F32)
    at = sub_f == ord_row
    plen_row = jnp.sum(jnp.where(at, len_col, 0.0), axis=0, keepdims=True)
    plen_col = to_col(plen_row)
    end_row = jnp.sum(jnp.where(sub <= lane, plen_col, 0.0), axis=0, keepdims=True)
    start_row = end_row - plen_row
    place_col = jnp.sum(jnp.where(at, lane_f, 0.0), axis=1, keepdims=True)
    place_row = jnp.where(lane1 < n_stmt, to_row(place_col), -1000.0)
    start_col = jnp.sum(jnp.where(at, start_row, 0.0), axis=1, keepdims=True)
    end_col = jnp.sum(jnp.where(at, end_row, 0.0), axis=1, keepdims=True)
    tokens = float(k_hbm.shape[0])
    end_real = jnp.where(lane1 < n_stmt, end_row, 1e9)

    def before(tok):
        return jnp.sum(jnp.where(end_real <= tok, 1.0, 0.0), axis=1, keepdims=True)

    b3 = iota((PACK, SLOTS, 128), 0).reshape(PACK * SLOTS, 128).astype(F32)
    j3 = iota((PACK, SLOTS, 128), 1).reshape(PACK * SLOTS, 128).astype(F32)
    first_big = before(b3 * tokens)
    selbig[...] = jnp.where(place_row == first_big + j3, 1.0, 0.0).astype(BF16)

    freq = jnp.exp(
        jnp.where(lane1 < 64, lane1, lane1 - 64).astype(F32) * (-2.0 / 128.0 * math.log(ROPE_BASE))
    )
    angle = (len_col - 1.0) * freq
    cosr[...] = jnp.cos(angle)
    sinr[...] = jnp.where(lane < 64, -1.0, 1.0) * jnp.sin(angle)

    w_copy = remote(wo_hbm, wo.at[c], ss.at[13], rs.at[13], g, sib)
    loads[0].wait()
    x15 = x_ref.at[0:CHIPS - 1]
    wq_copy.wait_recv()
    pending.append(remote(x15, x15, ss.at[0], rs.at[0], g, sib).wait_send)
    pending.append(wq_copy.wait_send)
    parts = jnp.zeros((n_stmt, 256), F32)
    sq_sum = jnp.zeros((8, 128), F32)
    for k in (3, 2, 1, 0):
        group = x_ref.at[4 * k:min(4 * k + 4, CHIPS - 1)]
        remote(group, group, ss.at[0], x_recv.at[k], g, sib).wait_recv()
        if k == 0:
            pass
        slots = list(range(4 * k, 4 * k + 4))
        blocks = jnp.concatenate([x_ref[i, 0:n_stmt, :] for i in slots], axis=1)
        for i in slots:
            sq_sum = sq_sum + x_ref[i, n_stmt:, :].astype(F32)
        weights = jnp.concatenate(
            [jnp.concatenate([wq[1 - c, source_chip(i)], wq[c, source_chip(i)]], axis=1) for i in slots],
            axis=0,
        )
        parts = parts + dot(blocks, weights)
    qx[0, 0:n_stmt, :] = parts[:, 0:128]
    qx[0, n_stmt:, :] = sq_sum
    q_copy = remote(qx.at[0], qx.at[1], ss.at[12], rs.at[12], g, sib)
    q_copy.start()
    pending.append(q_copy.wait_send)
    q_copy.wait_recv()
    q_raw = parts[:, 128:] + qx[1, 0:n_stmt, :]
    sq_sum = sq_sum + qx[1, n_stmt:, :]
    total = to_col(sq_sum[0:1, :] + sq_sum[1:2, :])
    mean_sq = jnp.sum(q_raw * q_raw, axis=1, keepdims=True) * (1.0 / 128.0)
    inv = lax.rsqrt(mean_sq + EPSILON * (total * (1.0 / (PACK * 128)) + EPSILON))
    q = q_raw * inv * qgain_ref[...]
    q = (q * cosr[...] + pltpu.roll(q, 64, 1) * sinr[...]).astype(BF16)
    q128 = jnp.concatenate([q, jnp.zeros((128 - n_stmt, 128), BF16)], axis=0)
    for k in range(8):
        py = lax.rem(y + far_first(k, 4), 8)
        firsts = [py * 2, py * 2 + 16]
        rows = [pl.ds(pl.multiple_of(f * SLOTS, 16), 2 * SLOTS) for f in firsts]
        chosen = dot(jnp.concatenate([selbig[r, :] for r in rows], axis=0), q128).astype(BF16)
        for f, r in zip(firsts, (0, 1)):
            sq[pl.ds(f, 2)] = chosen[2 * SLOTS * r:2 * SLOTS * (r + 1)].reshape(2, SLOTS, 128)
        for i in range(4 * k, min(4 * k + 4, PACK - 1)):
            to = pack_peer(i)
            remote(sq.at[to], qb.at[p], ss.at[1], rs.at[1], g, to).start()
    qb[p] = sq[p]
    w_copy.start()
    block_a = jnp.floor((start_col + 0.5) * (1.0 / tokens))
    block_b = jnp.floor((end_col - 0.5) * (1.0 / tokens))
    slot_a = place_col - before(block_a * tokens)
    slot_b = place_col - before(block_b * tokens)
    wide = iota((n_stmt, PACK * SLOTS), 1).astype(F32)
    for i, (blk, slot) in enumerate(
        ((block_a, slot_a), (block_b, slot_b), (block_a, float(STAT)), (block_b, float(STAT)))
    ):
        sel[i * n_stmt:(i + 1) * n_stmt, :] = jnp.where(
            wide == blk * SLOTS + slot, 1.0, 0.0
        ).astype(BF16)

    pf = p.astype(F32)
    slot_id = before(jnp.zeros((SLOTS, 128), F32) + pf * tokens) + iota((SLOTS, 1), 0).astype(F32)
    lane24 = iota((SLOTS, 128), 1).astype(F32)
    st = jnp.sum(jnp.where(lane24 == slot_id, start_row, 0.0), axis=1, keepdims=True)
    en = jnp.sum(jnp.where(lane24 == slot_id, end_row, 0.0), axis=1, keepdims=True)
    tok = iota((SLOTS, k_hbm.shape[0]), 1).astype(F32) + pf * tokens
    own_bias = jnp.where((tok >= st) & (tok < en), 0.0, MASKED)
    for i in range(4):
        bias[i * SLOTS:(i + 1) * SLOTS, :] = own_bias

    pl.semaphore_wait(relay.at[0], 4)
    tell(far, relay.at[1])
    loads[1].wait()
    loads[2].wait()
    q31 = qb.at[0:PACK - 1]
    pending.append(remote(q31, q31, ss.at[1], rs.at[1], g, sib).wait_send)
    pending.append(w_copy.wait_send)
    remote(q31, q31, ss.at[1], rs.at[1], g, sib).wait_recv()

    scale = 128 ** -0.5
    jr = iota((SLOTS, 128), 0)
    jl = iota((SLOTS, 128), 1)
    for n in range(8):
        dj = (2, 1, 3, 0)[n // 2]
        kz = (z, 1 - z)[1 - n % 2]
        kh = kz * 4 + lax.rem(lax.div(y, 2) + dj, 4)
        cols = pl.ds(pl.multiple_of(kh * 128, 128), 128)
        qs = qb[pl.ds(kh * 4, 4)].reshape(4 * SLOTS, 128)
        s = dot_t(qs, kk[:, cols]) * scale + bias[...]
        m = jnp.max(s, axis=1, keepdims=True)
        w = jnp.exp(s - m)
        l = jnp.sum(w, axis=1, keepdims=True)
        o = dot(w.astype(BF16), vv[:, cols]) / l
        lse = m + jnp.log(l)
        hi = lse.astype(BF16).astype(F32)
        mid = (lse - hi).astype(BF16).astype(F32)
        lo = lse - hi - mid
        for r in range(4):
            part = slice(r * SLOTS, (r + 1) * SLOTS)
            stat = jnp.where(
                jl == jr, hi[part], jnp.where(
                    jl == jr + 32, mid[part], jnp.where(jl == jr + 64, lo[part], 0.0)
                )
            )
            stat = jnp.sum(stat, axis=0, keepdims=True)
            ob_out[kh * 4 + r] = jnp.where(jr == STAT, stat, o[part]).astype(BF16)
        if n < 7:
            for r in range(4):
                to = kh * 4 + r
                remote(ob_out.at[to], ob.at[p], ss.at[2], rs.at[2], g, to).start()
        else:
            for r in range(1, 4):
                to = kh * 4 + lax.rem(lax.rem(p, 4) + r, 4)
                remote(ob_out.at[to], ob.at[p], ss.at[2], rs.at[2], g, to).start()
    ob[p] = ob_out[p]
    o31 = ob.at[0:PACK - 1]
    pending.append(remote(o31, o31, ss.at[2], rs.at[2], g, sib).wait_send)
    remote(o31, o31, ss.at[2], rs.at[2], g, sib).wait_recv()

    got = dot(sel[...], ob[...].reshape(PACK * SLOTS, 128))

    def stat_of(rows, slot):
        hit = (lane_f == slot) | (lane_f == slot + 32.0) | (lane_f == slot + 64.0)
        return jnp.sum(jnp.where(hit, rows, 0.0), axis=1, keepdims=True)

    lse_a = stat_of(got[2 * n_stmt:3 * n_stmt], slot_a)
    lse_b = stat_of(got[3 * n_stmt:], slot_b)
    top = jnp.maximum(lse_a, lse_b)
    w_a = jnp.exp(lse_a - top)
    w_b = jnp.where(block_a == block_b, 0.0, jnp.exp(lse_b - top))
    own_att = ((w_a * got[0:n_stmt] + w_b * got[n_stmt:2 * n_stmt]) / (w_a + w_b)).astype(BF16)
    att[c] = own_att
    remote(att.at[c], att.at[c], ss.at[3], rs.at[3], g, sib).start()
    pending.append(remote(att.at[c], att.at[c], ss.at[3], rs.at[3], g, sib).wait_send)
    loads[3].wait()
    w_copy.wait_recv()
    remote(att.at[c], att.at[1 - c], ss.at[3], rs.at[3], g, sib).wait_recv()
    pl.semaphore_wait(relay.at[1], 6)
    heads = jnp.concatenate([att[0], att[1]], axis=1)
    for k in range(CHIPS // 2):
        ends = [chip_peer(2 * k), chip_peer(2 * k + 1)]
        cols = [pl.ds(pl.multiple_of((to * 2 + c) * 128, 128), 128) for to in ends]
        w4 = jnp.concatenate(
            [jnp.concatenate([wo[0, :, at_], wo[1, :, at_]], axis=0) for at_ in cols], axis=1
        )
        part = dot(heads, w4)
        for r in range(2):
            i = 2 * k + r
            own_part = part[:, 128 * r:128 * r + 128]
            if i < CHIPS - 1:
                po_out[i] = own_part.astype(BF16)
                remote(po_out.at[i], po_in.at[i], ss.at[4], rs.at[4], g, ends[r] * 2 + c).start()
    pending.append(remote(po_out, po_in, ss.at[4], rs.at[4], g, sib).wait_send)
    remote(po_out, po_in, ss.at[4], rs.at[4], g, sib).wait_recv()
    hid = hid_ref[...].astype(F32) + own_part
    for i in range(CHIPS - 1):
        hid = hid + po_in[i].astype(F32)

    fgain = fgain_ref[...]
    feat = (hid * fgain).astype(BF16)
    pb[g] = feat
    f32feat = feat.astype(F32)

    def p_start(i):
        remote(pb.at[g], pb.at[g], ss.at[5], rs.at[5], dp_peer(i), p).start()

    each(DP - 1, p_start)
    s1 = jnp.sum(hid * hid, axis=1, keepdims=True)
    s2 = jnp.sum(f32feat * f32feat, axis=1, keepdims=True)
    st_row = jnp.sum(
        jnp.where(same, s1, 0.0) + jnp.where(lane == sub + 64, s2, 0.0), axis=0, keepdims=True
    )
    st_own[...] = st_row
    st_in[p] = st_row

    def s_start(i):
        remote(st_own, st_in.at[p], ss.at[6], rs.at[6], g, pack_peer(i)).start()

    each(PACK - 1, s_start)
    s31 = st_in.at[0:PACK - 1]
    pending.append(remote(s31, s31, ss.at[6], rs.at[6], g, sib).wait_send)
    p15 = pb.at[0:DP - 1]
    pending.append(remote(p15, p15, ss.at[5], rs.at[5], g, sib).wait_send)
    remote(s31, s31, ss.at[6], rs.at[6], g, sib).wait_recv()
    st_row = jnp.sum(st_in[...], axis=0)
    odd = lax.rem(g, 2)
    half_row = lax.div(g, 2)
    in_half = lax.div(lane1, 64) == odd

    def own_half(row):
        return jnp.where(in_half, jnp.where(odd == 1, row, pltpu.roll(row, 64, 1)), 0.0)

    ds_own[...] = own_half(st_row)
    ds_in[odd, half_row] = ds_own[...]

    def d_start(i):
        remote(ds_own, ds_in.at[odd, half_row], ss.at[7], rs.at[7], dp_peer(i), p).start()

    each(DP - 1, d_start)
    dall = st_in.at[0:DP - 1]
    pending.append(remote(dall, dall, ss.at[7], rs.at[7], g, sib).wait_send)
    s1_all = to_col(jnp.where(lane1 < 64, st_row, 0.0))
    s2_all = to_col(jnp.where(lane1 < 64, pltpu.roll(st_row, 64, 1), 0.0))
    inv_norm = lax.rsqrt(s2_all)
    rms = jnp.sqrt(s1_all * (1.0 / (PACK * 128)) + EPSILON)
    out_ref[0:n_stmt, :] = (hid / rms * fgain).astype(BF16)
    remote(p15, p15, ss.at[5], rs.at[5], g, sib).wait_recv()

    for j in range(4):
        part = dot_t(feat, pb[4 * j:4 * j + 4].reshape(256, 128))
        for r in range(2):
            pls[pl.ds(2 * j + r, n_stmt, stride=8), :] = part[:, 128 * r:128 * r + 128]
    lb[...] = pls[...].astype(BF16).reshape(PACK, 16, 128)

    def l_start(i):
        to = pack_peer(i)
        remote(lb.at[to], lb_in.at[p], ss.at[8], rs.at[8], g, to).start()

    each(PACK - 1, l_start)
    lb_in[p] = lb[p]
    remote(dall, dall, ss.at[7], rs.at[7], g, sib).wait_recv()
    inv_all = lax.rsqrt((ds_in[0] + ds_in[1]).reshape(8, 128))
    l31 = lb_in.at[0:PACK - 1]
    pending.append(remote(l31, l31, ss.at[8], rs.at[8], g, sib).wait_send)
    remote(l31, l31, ss.at[8], rs.at[8], g, sib).wait_recv()
    acc = jnp.zeros((16, 128), F32)
    for i in range(PACK):
        acc = acc + lb_in[i].astype(F32)
    col_id = iota((8, 128), 0) * 128 + iota((8, 128), 1)
    partner = part_ref[...]

    def whole(x):
        return jnp.sum(jnp.sum(x, axis=1, keepdims=True), axis=0, keepdims=True)

    losses = []
    exps = []
    for i in range(2):
        row_id = g * n_stmt + p * 2 + i
        diag = col_id == row_id
        own_inv = whole(jnp.where(diag, inv_all, 0.0))
        logit = acc[8 * i:8 * i + 8] * inv_all * (own_inv * (1.0 / WARMTH))
        e = jnp.where(diag, 0.0, jnp.exp(logit))
        own_partner = whole(jnp.where(diag, partner.astype(F32), 0.0))
        target = whole(jnp.where(col_id.astype(F32) == own_partner, logit, 0.0))
        losses.append(jnp.log(whole(e)) - target)
        exps.append(e)
    loss_ref[...] = jnp.where(iota((1, 2), 1) == 0, losses[0], losses[1])
    ub[p] = jnp.concatenate(exps, axis=0).astype(BF16)

    def u_start(i):
        remote(ub.at[p], ub.at[p], ss.at[9], rs.at[9], g, pack_peer(i)).start()

    each(PACK - 1, u_start)
    u31 = ub.at[0:PACK - 1]
    pending.append(remote(u31, u31, ss.at[9], rs.at[9], g, sib).wait_send)
    remote(u31, u31, ss.at[9], rs.at[9], g, sib).wait_recv()
    uf[...] = ub[...].reshape(PACK * 16, 128).astype(F32)
    mats = [uf[pl.ds(j, n_stmt, stride=8), :] for j in range(8)]
    row_sum = mats[0]
    for j in range(1, 8):
        row_sum = row_sum + mats[j]
    inv_sum = 1.0 / jnp.sum(row_sum, axis=1, keepdims=True)
    inv_row = jnp.sum(jnp.where(lane == sub + 64, inv_sum, 0.0), axis=0, keepdims=True)
    ls_own[...] = own_half(inv_row)
    ls_in[odd, half_row] = ls_own[...]

    def e_start(i):
        remote(ls_own, ls_in.at[odd, half_row], ss.at[10], rs.at[10], dp_peer(i), p).start()

    each(DP - 1, e_start)
    row_f = (g * n_stmt + iota((n_stmt, 1), 0)).astype(F32)
    part_f = partner.astype(F32)
    own_part_col = jnp.zeros((n_stmt, 1), F32)
    for j in range(8):
        own_part_col = own_part_col + jnp.sum(
            jnp.where((lane + 128 * j).astype(F32) == row_f, part_f[j:j + 1, :], 0.0), axis=1, keepdims=True
        )
    pairs = []
    logs = []
    for j in range(8):
        cid = (lane + 128 * j).astype(F32)
        pairs.append(
            jnp.where(cid == own_part_col, 1.0, 0.0) + jnp.where(part_f[j:j + 1, :] == row_f, 1.0, 0.0)
        )
        logs.append(jnp.log(jnp.maximum(mats[j], 1e-30)))
    pending.append(remote(dall, dall, ss.at[10], rs.at[10], g, sib).wait_send)
    remote(dall, dall, ss.at[10], rs.at[10], g, sib).wait_recv()
    sums_all = (ls_in[0] + ls_in[1]).reshape(8, 128)
    grad = jnp.zeros((n_stmt, 128), F32)
    inner_acc = jnp.zeros((n_stmt, 128), F32)
    for j in range(4):
        scaled = []
        for k in (2 * j, 2 * j + 1):
            wk = mats[k] * (inv_sum + sums_all[k:k + 1, :]) - pairs[k]
            inner_acc = inner_acc + wk * logs[k]
            scaled.append((wk * inv_all[k:k + 1, :]).astype(BF16))
        grad = grad + dot(jnp.concatenate(scaled, axis=1), pb[4 * j:4 * j + 4].reshape(256, 128))
    inner = jnp.sum(inner_acc, axis=1, keepdims=True)
    out = grad * (1.0 / WARMTH) - f32feat * (inv_norm * inner)
    out_ref[n_stmt:, :] = (out * fgain * (inv_norm * float(PACK * 128) ** 0.5)).astype(BF16)

    for wait in pending:
        wait()


def local(
    hidden_in, attn_gain, w_query, query_gain, cached_keys, cached_values, w_out, final_gain,
    lengths, pack_order, partner,
):
    n = hidden_in.shape[0]
    toks, kvw = cached_keys.shape
    width = w_query.shape[0]
    vmem = pl.BlockSpec(memory_space=pltpu.VMEM)
    hbm = pl.BlockSpec(memory_space=pltpu.HBM)
    V = pltpu.VMEM
    dma = pltpu.SemaphoreType.DMA
    out, loss = pl.pallas_call(
        kernel,
        out_shape=(
            jax.ShapeDtypeStruct((2 * n, 128), BF16),
            jax.ShapeDtypeStruct((1, 2), F32),
        ),
        in_specs=[vmem, vmem, hbm, vmem, hbm, hbm, hbm, vmem, vmem, vmem, vmem],
        out_specs=(vmem, vmem),
        scratch_shapes=[
            V((CHIPS, n + 8, 128), BF16),
            V((2, n + 8, 128), F32),
            V((2, CHIPS, 128, 128), BF16),
            V((toks, kvw), BF16),
            V((toks, kvw), BF16),
            V((2, 128, width), BF16),
            V((n + 8, 128), BF16),
            V((8, 128), F32),
            V((PACK * SLOTS, 128), BF16),
            V((4 * n, PACK * SLOTS), BF16),
            V((4 * SLOTS, toks), F32),
            V((n, 128), F32),
            V((n, 128), F32),
            V((PACK, SLOTS, 128), BF16),
            V((PACK, SLOTS, 128), BF16),
            V((PACK, SLOTS, 128), BF16),
            V((PACK, SLOTS, 128), BF16),
            V((2, n, 128), BF16),
            V((CHIPS - 1, n, 128), BF16),
            V((CHIPS - 1, n, 128), BF16),
            V((DP, n, 128), BF16),
            V((1, 128), F32),
            V((PACK, 1, 128), F32),
            V((1, 128), F32),
            V((2, 8, 1, 128), F32),
            V((n * 8, 128), F32),
            V((PACK, 16, 128), BF16),
            V((PACK, 16, 128), BF16),
            V((PACK, 16, 128), BF16),
            V((1, 128), F32),
            V((2, 8, 1, 128), F32),
            V((n * 8, 128), F32),
            dma((4,)),
            dma((14,)),
            dma((14,)),
            dma((4,)),
            pltpu.SemaphoreType.REGULAR((2,)),
        ],
        compiler_params=pltpu.CompilerParams(
            collective_id=0, has_side_effects=True
        ),
    )(
        hidden_in,
        attn_gain.reshape(1, 128),
        w_query.reshape(CHIPS, 2, 128, 128),
        query_gain.reshape(1, 128),
        cached_keys,
        cached_values,
        w_out,
        final_gain.reshape(1, 128),
        lengths,
        pack_order,
        partner.reshape(8, 128),
    )
    return out[0:n], loss.reshape(2), out[n:]


def solution(mesh):
    in_specs = (
        P("dp", "pack"),
        P("pack"),
        P(None, "pack"),
        P(),
        P(("dp", "pack"), None),
        P(("dp", "pack"), None),
        P("pack", None),
        P("pack"),
        P("dp", None),
        P("dp", None),
        P(),
    )
    out_specs = (P("dp", "pack"), P(("dp", "pack")), P("dp", "pack"))
    return jax.shard_map(local, mesh=mesh, in_specs=in_specs, out_specs=out_specs, check_vma=False)
```

```python
import math

import jax
import jax.numpy as jnp
from jax import lax
from jax.experimental import pallas as pl
from jax.experimental.pallas import tpu as pltpu
from jax.sharding import PartitionSpec as P

EPSILON = 1e-06
WARMTH = 0.05
ROPE_BASE = 1000000.0
MASKED = -1e30
F32 = jnp.float32
BF16 = jnp.bfloat16
I32 = jnp.int32

SLOTS = 24
STAT = SLOTS - 1
PACK = 32
CHIPS = 16
DP = 16
MESH = pl.DeviceIdType.MESH


def far_first(k, half):
    return half + (1 - 2 * (k % 2)) * ((k + 1) // 2)


def each(n, step):
    for i in range(n):
        step(i)


def dot_t(a, b):
    return lax.dot_general(a, b, (((1,), (1,)), ((), ())), preferred_element_type=F32)


def dot(a, b):
    return jnp.dot(a, b, preferred_element_type=F32)


def iota(shape, dim):
    return lax.broadcasted_iota(I32, shape, dim)


def kernel(
    hid_ref, again_ref, wq_hbm, qgain_ref, k_hbm, v_hbm, wo_hbm, fgain_ref, len_ref, ord_ref, part_ref,
    out_ref, loss_ref,
    x_ref, qx, wq, kk, vv, wo, msg, ints, selbig, sel, bias, cosr, sinr,
    sq, qb, ob_out, ob, att, po_out, po_in, pb, st_own, st_in, ds_own, ds_in,
    pls, lb, lb_in, ub, ls_own, ls_in, uf, a_own, a_in,
    load_sem, ss, rs, x_recv, relay,
):
    g = lax.axis_index("dp")
    p = lax.axis_index("pack")
    z, y, c = lax.div(p, 16), lax.div(lax.rem(p, 16), 2), lax.rem(p, 2)
    sib = p + 1 - 2 * c
    chip = z * 8 + y
    n_stmt = hid_ref.shape[0]

    def pack_peer(i):
        k, r = i // 4, i % 4
        py = lax.rem(y + far_first(k, 4), 8)
        pz = (z, 1 - z)[1 - r // 2]
        pc = (c, 1 - c)[1 - r % 2]
        return pz * 16 + py * 2 + pc

    def chip_peer(i):
        py = lax.rem(y + far_first(i // 2, 4), 8)
        pz = (z, 1 - z)[1 - i % 2]
        return pz * 8 + py

    gx, gz = lax.div(g, 4), lax.rem(g, 4)

    def dp_peer(i):
        a, b = i // 4, i % 4
        return lax.rem(gx + far_first(a, 2), 4) * 4 + lax.rem(gz + far_first(b, 2), 4)

    def remote(src, dst, send, recv, dg, dp_):
        return pltpu.make_async_remote_copy(
            src_ref=src, dst_ref=dst, send_sem=send, recv_sem=recv,
            device_id=(dg, dp_), device_id_type=MESH,
        )

    pending = []
    loads = [
        pltpu.make_async_copy(wq_hbm.at[:, c], wq.at[c], load_sem.at[0]),
        pltpu.make_async_copy(k_hbm, kk, load_sem.at[1]),
        pltpu.make_async_copy(v_hbm, vv, load_sem.at[2]),
        pltpu.make_async_copy(wo_hbm, wo.at[c], load_sem.at[3]),
    ]
    barrier = pltpu.get_barrier_semaphore()

    def greet_pack(i):
        pl.semaphore_signal(barrier, inc=1, device_id=(g, pack_peer(i)), device_id_type=MESH)

    def group_at(dx, dz):
        return lax.rem(gx + dx, 4) * 4 + lax.rem(gz + dz, 4)

    near = [group_at(*d) for d in ((1, 0), (3, 0), (0, 1), (0, 3))]
    far = [group_at(*d) for d in ((2, 0), (0, 2), (1, 1), (1, 3), (3, 1), (3, 3))]

    def tell(groups, sem):
        for to in groups:
            pl.semaphore_signal(sem, inc=1, device_id=(to, p), device_id_type=MESH)

    tell(near, barrier)
    each(PACK - 1, greet_pack)
    for load in loads:
        load.start()

    lane = iota((n_stmt, 128), 1)
    sub = iota((n_stmt, 128), 0)
    same = lane == sub
    lane1 = iota((1, 128), 1)

    def to_row(col):
        return jnp.sum(jnp.where(same, col, 0.0), axis=0, keepdims=True)

    def to_col(row):
        return jnp.sum(jnp.where(same, row, 0.0), axis=1, keepdims=True)

    row8 = iota((8, 128), 0)
    h32 = hid_ref[...].astype(F32)
    msg[0:n_stmt, :] = (h32 * again_ref[...]).astype(BF16)
    sq_row = to_row(jnp.sum(h32 * h32, axis=1, keepdims=True))
    sq_hi = sq_row.astype(BF16).astype(F32)
    msg[n_stmt:, :] = jnp.where(
        row8 == 0, sq_hi, jnp.where(row8 == 1, sq_row - sq_hi, 0.0)
    ).astype(BF16)

    pl.semaphore_wait(barrier, PACK - 1 + 4)

    wq_copy = remote(wq_hbm.at[:, 1 - c], wq.at[c], ss.at[11], rs.at[11], g, sib)

    def x_start(i):
        remote(msg, x_ref.at[i], ss.at[0], x_recv.at[i // 4], g, chip_peer(i) * 2 + c).start()

    def source_chip(i):
        py = lax.rem(y + 8 - far_first(i // 2, 4), 8)
        pz = (z, 1 - z)[1 - i % 2]
        return pz * 8 + py

    each(CHIPS - 1, x_start)
    wq_copy.start()
    tell(near, relay.at[0])
    x_ref[CHIPS - 1] = msg[...]

    ints[...] = jnp.where(row8 == 1, -1.0, 0.0)
    ints[0:1, 0:n_stmt] = len_ref[...].astype(F32)
    ints[1:2, 0:n_stmt] = ord_ref[...].astype(F32)
    len_row = ints[0:1, :]
    ord_row = ints[1:2, :]
    len_col = to_col(len_row)
    lane_f = lane.astype(F32)
    sub_f = sub.astype(F32)
    at = sub_f == ord_row
    plen_row = jnp.sum(jnp.where(at, len_col, 0.0), axis=0, keepdims=True)
    plen_col = to_col(plen_row)
    end_row = jnp.sum(jnp.where(sub <= lane, plen_col, 0.0), axis=0, keepdims=True)
    start_row = end_row - plen_row
    place_col = jnp.sum(jnp.where(at, lane_f, 0.0), axis=1, keepdims=True)
    place_row = jnp.where(lane1 < n_stmt, to_row(place_col), -1000.0)
    start_col = jnp.sum(jnp.where(at, start_row, 0.0), axis=1, keepdims=True)
    end_col = jnp.sum(jnp.where(at, end_row, 0.0), axis=1, keepdims=True)
    tokens = float(k_hbm.shape[0])
    end_real = jnp.where(lane1 < n_stmt, end_row, 1e9)

    def before(tok):
        return jnp.sum(jnp.where(end_real <= tok, 1.0, 0.0), axis=1, keepdims=True)

    b3 = iota((PACK, SLOTS, 128), 0).reshape(PACK * SLOTS, 128).astype(F32)
    j3 = iota((PACK, SLOTS, 128), 1).reshape(PACK * SLOTS, 128).astype(F32)
    first_big = before(b3 * tokens)
    selbig[...] = jnp.where(place_row == first_big + j3, 1.0, 0.0).astype(BF16)

    freq = jnp.exp(
        jnp.where(lane1 < 64, lane1, lane1 - 64).astype(F32) * (-2.0 / 128.0 * math.log(ROPE_BASE))
    )
    angle = (len_col - 1.0) * freq
    cosr[...] = jnp.cos(angle)
    sinr[...] = jnp.where(lane < 64, -1.0, 1.0) * jnp.sin(angle)

    w_copy = remote(wo_hbm, wo.at[c], ss.at[13], rs.at[13], g, sib)
    loads[0].wait()
    x15 = x_ref.at[0:CHIPS - 1]
    wq_copy.wait_recv()
    pending.append(remote(x15, x15, ss.at[0], rs.at[0], g, sib).wait_send)
    pending.append(wq_copy.wait_send)
    parts = jnp.zeros((n_stmt, 256), F32)
    sq_sum = jnp.zeros((8, 128), F32)
    for k in (3, 2, 1, 0):
        group = x_ref.at[4 * k:min(4 * k + 4, CHIPS - 1)]
        remote(group, group, ss.at[0], x_recv.at[k], g, sib).wait_recv()
        if k == 0:
            pass
        slots = list(range(4 * k, 4 * k + 4))
        blocks = jnp.concatenate([x_ref[i, 0:n_stmt, :] for i in slots], axis=1)
        for i in slots:
            sq_sum = sq_sum + x_ref[i, n_stmt:, :].astype(F32)
        weights = jnp.concatenate(
            [jnp.concatenate([wq[1 - c, source_chip(i)], wq[c, source_chip(i)]], axis=1) for i in slots],
            axis=0,
        )
        parts = parts + dot(blocks, weights)
    qx[0, 0:n_stmt, :] = parts[:, 0:128]
    qx[0, n_stmt:, :] = sq_sum
    q_copy = remote(qx.at[0], qx.at[1], ss.at[12], rs.at[12], g, sib)
    q_copy.start()
    pending.append(q_copy.wait_send)
    q_copy.wait_recv()
    q_raw = parts[:, 128:] + qx[1, 0:n_stmt, :]
    sq_sum = sq_sum + qx[1, n_stmt:, :]
    total = to_col(sq_sum[0:1, :] + sq_sum[1:2, :])
    mean_sq = jnp.sum(q_raw * q_raw, axis=1, keepdims=True) * (1.0 / 128.0)
    inv = lax.rsqrt(mean_sq + EPSILON * (total * (1.0 / (PACK * 128)) + EPSILON))
    q = q_raw * inv * qgain_ref[...]
    q = (q * cosr[...] + pltpu.roll(q, 64, 1) * sinr[...]).astype(BF16)
    q128 = jnp.concatenate([q, jnp.zeros((128 - n_stmt, 128), BF16)], axis=0)
    for k in range(8):
        py = lax.rem(y + far_first(k, 4), 8)
        firsts = [py * 2, py * 2 + 16]
        rows = [pl.ds(pl.multiple_of(f * SLOTS, 16), 2 * SLOTS) for f in firsts]
        chosen = dot(jnp.concatenate([selbig[r, :] for r in rows], axis=0), q128).astype(BF16)
        for f, r in zip(firsts, (0, 1)):
            sq[pl.ds(f, 2)] = chosen[2 * SLOTS * r:2 * SLOTS * (r + 1)].reshape(2, SLOTS, 128)
        for i in range(4 * k, min(4 * k + 4, PACK - 1)):
            to = pack_peer(i)
            remote(sq.at[to], qb.at[p], ss.at[1], rs.at[1], g, to).start()
    qb[p] = sq[p]
    w_copy.start()
    block_a = jnp.floor((start_col + 0.5) * (1.0 / tokens))
    block_b = jnp.floor((end_col - 0.5) * (1.0 / tokens))
    slot_a = place_col - before(block_a * tokens)
    slot_b = place_col - before(block_b * tokens)
    wide = iota((n_stmt, PACK * SLOTS), 1).astype(F32)
    for i, (blk, slot) in enumerate(
        ((block_a, slot_a), (block_b, slot_b), (block_a, float(STAT)), (block_b, float(STAT)))
    ):
        sel[i * n_stmt:(i + 1) * n_stmt, :] = jnp.where(
            wide == blk * SLOTS + slot, 1.0, 0.0
        ).astype(BF16)

    pf = p.astype(F32)
    slot_id = before(jnp.zeros((SLOTS, 128), F32) + pf * tokens) + iota((SLOTS, 1), 0).astype(F32)
    lane24 = iota((SLOTS, 128), 1).astype(F32)
    st = jnp.sum(jnp.where(lane24 == slot_id, start_row, 0.0), axis=1, keepdims=True)
    en = jnp.sum(jnp.where(lane24 == slot_id, end_row, 0.0), axis=1, keepdims=True)
    tok = iota((SLOTS, k_hbm.shape[0]), 1).astype(F32) + pf * tokens
    own_bias = jnp.where((tok >= st) & (tok < en), 0.0, MASKED)
    for i in range(4):
        bias[i * SLOTS:(i + 1) * SLOTS, :] = own_bias

    pl.semaphore_wait(relay.at[0], 4)
    tell(far, relay.at[1])
    loads[1].wait()
    loads[2].wait()
    q31 = qb.at[0:PACK - 1]
    pending.append(remote(q31, q31, ss.at[1], rs.at[1], g, sib).wait_send)
    pending.append(w_copy.wait_send)
    remote(q31, q31, ss.at[1], rs.at[1], g, sib).wait_recv()

    scale = 128 ** -0.5
    jr = iota((SLOTS, 128), 0)
    jl = iota((SLOTS, 128), 1)
    for n in range(8):
        dj = (2, 1, 3, 0)[n // 2]
        kz = (z, 1 - z)[1 - n % 2]
        kh = kz * 4 + lax.rem(lax.div(y, 2) + dj, 4)
        cols = pl.ds(pl.multiple_of(kh * 128, 128), 128)
        qs = qb[pl.ds(kh * 4, 4)].reshape(4 * SLOTS, 128)
        s = dot_t(qs, kk[:, cols]) * scale + bias[...]
        m = jnp.max(s, axis=1, keepdims=True)
        w = jnp.exp(s - m)
        l = jnp.sum(w, axis=1, keepdims=True)
        o = dot(w.astype(BF16), vv[:, cols]) / l
        lse = m + jnp.log(l)
        hi = lse.astype(BF16).astype(F32)
        mid = (lse - hi).astype(BF16).astype(F32)
        lo = lse - hi - mid
        for r in range(4):
            part = slice(r * SLOTS, (r + 1) * SLOTS)
            stat = jnp.where(
                jl == jr, hi[part], jnp.where(
                    jl == jr + 32, mid[part], jnp.where(jl == jr + 64, lo[part], 0.0)
                )
            )
            stat = jnp.sum(stat, axis=0, keepdims=True)
            ob_out[kh * 4 + r] = jnp.where(jr == STAT, stat, o[part]).astype(BF16)
        if n < 7:
            for r in range(4):
                to = kh * 4 + r
                remote(ob_out.at[to], ob.at[p], ss.at[2], rs.at[2], g, to).start()
        else:
            for r in range(1, 4):
                to = kh * 4 + lax.rem(lax.rem(p, 4) + r, 4)
                remote(ob_out.at[to], ob.at[p], ss.at[2], rs.at[2], g, to).start()
    ob[p] = ob_out[p]
    o31 = ob.at[0:PACK - 1]
    pending.append(remote(o31, o31, ss.at[2], rs.at[2], g, sib).wait_send)
    remote(o31, o31, ss.at[2], rs.at[2], g, sib).wait_recv()

    got = dot(sel[...], ob[...].reshape(PACK * SLOTS, 128))

    def stat_of(rows, slot):
        hit = (lane_f == slot) | (lane_f == slot + 32.0) | (lane_f == slot + 64.0)
        return jnp.sum(jnp.where(hit, rows, 0.0), axis=1, keepdims=True)

    lse_a = stat_of(got[2 * n_stmt:3 * n_stmt], slot_a)
    lse_b = stat_of(got[3 * n_stmt:], slot_b)
    top = jnp.maximum(lse_a, lse_b)
    w_a = jnp.exp(lse_a - top)
    w_b = jnp.where(block_a == block_b, 0.0, jnp.exp(lse_b - top))
    own_att = ((w_a * got[0:n_stmt] + w_b * got[n_stmt:2 * n_stmt]) / (w_a + w_b)).astype(BF16)
    att[c] = own_att
    remote(att.at[c], att.at[c], ss.at[3], rs.at[3], g, sib).start()
    pending.append(remote(att.at[c], att.at[c], ss.at[3], rs.at[3], g, sib).wait_send)
    loads[3].wait()
    w_copy.wait_recv()
    remote(att.at[c], att.at[1 - c], ss.at[3], rs.at[3], g, sib).wait_recv()
    pl.semaphore_wait(relay.at[1], 6)
    heads = jnp.concatenate([att[0], att[1]], axis=1)
    for k in range(CHIPS // 2):
        ends = [chip_peer(2 * k), chip_peer(2 * k + 1)]
        cols = [pl.ds(pl.multiple_of((to * 2 + c) * 128, 128), 128) for to in ends]
        w4 = jnp.concatenate(
            [jnp.concatenate([wo[0, :, at_], wo[1, :, at_]], axis=0) for at_ in cols], axis=1
        )
        part = dot(heads, w4)
        for r in range(2):
            i = 2 * k + r
            own_part = part[:, 128 * r:128 * r + 128]
            if i < CHIPS - 1:
                po_out[i] = own_part.astype(BF16)
                remote(po_out.at[i], po_in.at[i], ss.at[4], rs.at[4], g, ends[r] * 2 + c).start()
    pending.append(remote(po_out, po_in, ss.at[4], rs.at[4], g, sib).wait_send)
    remote(po_out, po_in, ss.at[4], rs.at[4], g, sib).wait_recv()
    hid = hid_ref[...].astype(F32) + own_part
    for i in range(CHIPS - 1):
        hid = hid + po_in[i].astype(F32)

    fgain = fgain_ref[...]
    feat = (hid * fgain).astype(BF16)
    pb[g] = feat
    f32feat = feat.astype(F32)

    def p_start(i):
        remote(pb.at[g], pb.at[g], ss.at[5], rs.at[5], dp_peer(i), p).start()

    each(DP - 1, p_start)
    s1 = jnp.sum(hid * hid, axis=1, keepdims=True)
    s2 = jnp.sum(f32feat * f32feat, axis=1, keepdims=True)
    st_row = jnp.sum(
        jnp.where(same, s1, 0.0) + jnp.where(lane == sub + 64, s2, 0.0), axis=0, keepdims=True
    )
    st_own[...] = st_row
    st_in[p] = st_row

    def s_start(i):
        remote(st_own, st_in.at[p], ss.at[6], rs.at[6], g, pack_peer(i)).start()

    each(PACK - 1, s_start)
    s31 = st_in.at[0:PACK - 1]
    pending.append(remote(s31, s31, ss.at[6], rs.at[6], g, sib).wait_send)
    p15 = pb.at[0:DP - 1]
    pending.append(remote(p15, p15, ss.at[5], rs.at[5], g, sib).wait_send)
    remote(s31, s31, ss.at[6], rs.at[6], g, sib).wait_recv()
    st_row = jnp.sum(st_in[...], axis=0)
    odd = lax.rem(g, 2)
    half_row = lax.div(g, 2)
    in_half = lax.div(lane1, 64) == odd

    def own_half(row):
        return jnp.where(in_half, jnp.where(odd == 1, row, pltpu.roll(row, 64, 1)), 0.0)

    ds_own[...] = own_half(st_row)
    ds_in[odd, half_row] = ds_own[...]

    def d_start(i):
        remote(ds_own, ds_in.at[odd, half_row], ss.at[7], rs.at[7], dp_peer(i), p).start()

    each(DP - 1, d_start)
    dall = st_in.at[0:DP - 1]
    pending.append(remote(dall, dall, ss.at[7], rs.at[7], g, sib).wait_send)
    s1_all = to_col(jnp.where(lane1 < 64, st_row, 0.0))
    s2_all = to_col(jnp.where(lane1 < 64, pltpu.roll(st_row, 64, 1), 0.0))
    inv_norm = lax.rsqrt(s2_all)
    rms = jnp.sqrt(s1_all * (1.0 / (PACK * 128)) + EPSILON)
    out_ref[0:n_stmt, :] = (hid / rms * fgain).astype(BF16)
    remote(p15, p15, ss.at[5], rs.at[5], g, sib).wait_recv()

    for j in range(4):
        part = dot_t(feat, pb[4 * j:4 * j + 4].reshape(256, 128))
        for r in range(2):
            pls[pl.ds(2 * j + r, n_stmt, stride=8), :] = part[:, 128 * r:128 * r + 128]
    lb[...] = pls[...].astype(BF16).reshape(PACK, 16, 128)

    def l_start(i):
        to = pack_peer(i)
        remote(lb.at[to], lb_in.at[p], ss.at[8], rs.at[8], g, to).start()

    each(PACK - 1, l_start)
    lb_in[p] = lb[p]
    remote(dall, dall, ss.at[7], rs.at[7], g, sib).wait_recv()
    inv_all = lax.rsqrt((ds_in[0] + ds_in[1]).reshape(8, 128))
    l31 = lb_in.at[0:PACK - 1]
    pending.append(remote(l31, l31, ss.at[8], rs.at[8], g, sib).wait_send)
    remote(l31, l31, ss.at[8], rs.at[8], g, sib).wait_recv()
    acc = jnp.zeros((16, 128), F32)
    for i in range(PACK):
        acc = acc + lb_in[i].astype(F32)
    col_id = iota((8, 128), 0) * 128 + iota((8, 128), 1)
    partner = part_ref[...]

    def whole(x):
        return jnp.sum(jnp.sum(x, axis=1, keepdims=True), axis=0, keepdims=True)

    losses = []
    exps = []
    sums = []
    for i in range(2):
        row_id = g * n_stmt + p * 2 + i
        diag = col_id == row_id
        own_inv = whole(jnp.where(diag, inv_all, 0.0))
        logit = acc[8 * i:8 * i + 8] * inv_all * (own_inv * (1.0 / WARMTH))
        e = jnp.where(diag, 0.0, jnp.exp(logit))
        own_partner = whole(jnp.where(diag, partner.astype(F32), 0.0))
        target = whole(jnp.where(col_id.astype(F32) == own_partner, logit, 0.0))
        sums.append(whole(e))
        losses.append(jnp.log(sums[i]) - target)
        exps.append(e)
    loss_ref[...] = jnp.where(iota((1, 2), 1) == 0, losses[0], losses[1])
    first = lane1 - 64 * odd
    ls_own[...] = jnp.where(first == 0, 1.0 / sums[0], jnp.where(first == 1, 1.0 / sums[1], 0.0))
    ls_in[odd, half_row] = ls_own[...]

    def e_start(i):
        remote(ls_own, ls_in.at[odd, half_row], ss.at[10], rs.at[10], dp_peer(i), p).start()

    each(DP - 1, e_start)
    ub[p] = jnp.concatenate(exps, axis=0).astype(BF16)

    def u_start(i):
        remote(ub.at[p], ub.at[p], ss.at[9], rs.at[9], g, pack_peer(i)).start()

    each(PACK - 1, u_start)
    u31 = ub.at[0:PACK - 1]
    pending.append(remote(u31, u31, ss.at[9], rs.at[9], g, sib).wait_send)
    row_f = (g * n_stmt + iota((n_stmt, 1), 0)).astype(F32)
    part_f = partner.astype(F32)
    own_part_col = jnp.zeros((n_stmt, 1), F32)
    for j in range(8):
        own_part_col = own_part_col + jnp.sum(
            jnp.where((lane + 128 * j).astype(F32) == row_f, part_f[j:j + 1, :], 0.0), axis=1, keepdims=True
        )
    pairs = []
    for j in range(8):
        cid = (lane + 128 * j).astype(F32)
        pairs.append(
            jnp.where(cid == own_part_col, 1.0, 0.0) + jnp.where(part_f[j:j + 1, :] == row_f, 1.0, 0.0)
        )
    pending.append(remote(dall, dall, ss.at[10], rs.at[10], g, sib).wait_send)
    remote(dall, dall, ss.at[10], rs.at[10], g, sib).wait_recv()
    mine = (ls_in[0] + ls_in[1]).reshape(8, 128)
    packed = mine[0:1, :]
    for j in range(1, 8):
        packed = packed + pltpu.roll(mine[j:j + 1, :], 2 * j, 1)
    a_own[...] = packed
    a_in[p] = packed

    def a_start(i):
        remote(a_own, a_in.at[p], ss.at[14], rs.at[14], g, pack_peer(i)).start()

    each(PACK - 1, a_start)
    a31 = a_in.at[0:PACK - 1]
    pending.append(remote(a31, a31, ss.at[14], rs.at[14], g, sib).wait_send)
    remote(u31, u31, ss.at[9], rs.at[9], g, sib).wait_recv()
    uf[...] = ub[...].reshape(PACK * 16, 128).astype(F32)
    mats = [uf[pl.ds(j, n_stmt, stride=8), :] for j in range(8)]
    row_sum = mats[0]
    for j in range(1, 8):
        row_sum = row_sum + mats[j]
    inv_sum = 1.0 / jnp.sum(row_sum, axis=1, keepdims=True)
    logs = [jnp.log(jnp.maximum(m, 1e-30)) for m in mats]
    remote(a31, a31, ss.at[14], rs.at[14], g, sib).wait_recv()
    arrived = a_in[...].reshape(PACK, 128)
    lane32 = iota((PACK, 128), 1)
    place = lax.rem(lane32, 64)
    here = lax.div(place, 2) == iota((PACK, 128), 0)
    second = lax.rem(place, 2) == 1
    upper = lane32 >= 64
    sums_all = []
    for j in range(8):
        low = jnp.where(second, arrived[:, 2 * j + 1:2 * j + 2], arrived[:, 2 * j:2 * j + 1])
        high = jnp.where(second, arrived[:, 64 + 2 * j + 1:64 + 2 * j + 2], arrived[:, 64 + 2 * j:64 + 2 * j + 1])
        sums_all.append(
            jnp.sum(jnp.where(here, jnp.where(upper, high, low), 0.0), axis=0, keepdims=True)
        )
    grad = jnp.zeros((n_stmt, 128), F32)
    inner_acc = jnp.zeros((n_stmt, 128), F32)
    for j in range(4):
        scaled = []
        for k in (2 * j, 2 * j + 1):
            wk = mats[k] * (inv_sum + sums_all[k]) - pairs[k]
            inner_acc = inner_acc + wk * logs[k]
            scaled.append((wk * inv_all[k:k + 1, :]).astype(BF16))
        grad = grad + dot(jnp.concatenate(scaled, axis=1), pb[4 * j:4 * j + 4].reshape(256, 128))
    inner = jnp.sum(inner_acc, axis=1, keepdims=True)
    out = grad * (1.0 / WARMTH) - f32feat * (inv_norm * inner)
    out_ref[n_stmt:, :] = (out * fgain * (inv_norm * float(PACK * 128) ** 0.5)).astype(BF16)

    for wait in pending:
        wait()


def local(
    hidden_in, attn_gain, w_query, query_gain, cached_keys, cached_values, w_out, final_gain,
    lengths, pack_order, partner,
):
    n = hidden_in.shape[0]
    toks, kvw = cached_keys.shape
    width = w_query.shape[0]
    vmem = pl.BlockSpec(memory_space=pltpu.VMEM)
    hbm = pl.BlockSpec(memory_space=pltpu.HBM)
    V = pltpu.VMEM
    dma = pltpu.SemaphoreType.DMA
    out, loss = pl.pallas_call(
        kernel,
        out_shape=(
            jax.ShapeDtypeStruct((2 * n, 128), BF16),
            jax.ShapeDtypeStruct((1, 2), F32),
        ),
        in_specs=[vmem, vmem, hbm, vmem, hbm, hbm, hbm, vmem, vmem, vmem, vmem],
        out_specs=(vmem, vmem),
        scratch_shapes=[
            V((CHIPS, n + 8, 128), BF16),
            V((2, n + 8, 128), F32),
            V((2, CHIPS, 128, 128), BF16),
            V((toks, kvw), BF16),
            V((toks, kvw), BF16),
            V((2, 128, width), BF16),
            V((n + 8, 128), BF16),
            V((8, 128), F32),
            V((PACK * SLOTS, 128), BF16),
            V((4 * n, PACK * SLOTS), BF16),
            V((4 * SLOTS, toks), F32),
            V((n, 128), F32),
            V((n, 128), F32),
            V((PACK, SLOTS, 128), BF16),
            V((PACK, SLOTS, 128), BF16),
            V((PACK, SLOTS, 128), BF16),
            V((PACK, SLOTS, 128), BF16),
            V((2, n, 128), BF16),
            V((CHIPS - 1, n, 128), BF16),
            V((CHIPS - 1, n, 128), BF16),
            V((DP, n, 128), BF16),
            V((1, 128), F32),
            V((PACK, 1, 128), F32),
            V((1, 128), F32),
            V((2, 8, 1, 128), F32),
            V((n * 8, 128), F32),
            V((PACK, 16, 128), BF16),
            V((PACK, 16, 128), BF16),
            V((PACK, 16, 128), BF16),
            V((1, 128), F32),
            V((2, 8, 1, 128), F32),
            V((n * 8, 128), F32),
            V((1, 128), F32),
            V((PACK, 1, 128), F32),
            dma((4,)),
            dma((15,)),
            dma((15,)),
            dma((4,)),
            pltpu.SemaphoreType.REGULAR((2,)),
        ],
        compiler_params=pltpu.CompilerParams(
            collective_id=0, has_side_effects=True
        ),
    )(
        hidden_in,
        attn_gain.reshape(1, 128),
        w_query.reshape(CHIPS, 2, 128, 128),
        query_gain.reshape(1, 128),
        cached_keys,
        cached_values,
        w_out,
        final_gain.reshape(1, 128),
        lengths,
        pack_order,
        partner.reshape(8, 128),
    )
    return out[0:n], loss.reshape(2), out[n:]


def solution(mesh):
    in_specs = (
        P("dp", "pack"),
        P("pack"),
        P(None, "pack"),
        P(),
        P(("dp", "pack"), None),
        P(("dp", "pack"), None),
        P("pack", None),
        P("pack"),
        P("dp", None),
        P("dp", None),
        P(),
    )
    out_specs = (P("dp", "pack"), P(("dp", "pack")), P("dp", "pack"))
    return jax.shard_map(local, mesh=mesh, in_specs=in_specs, out_specs=out_specs, check_vma=False)
```

```python
import math

import jax
import jax.numpy as jnp
from jax import lax
from jax.experimental import pallas as pl
from jax.experimental.pallas import tpu as pltpu
from jax.sharding import PartitionSpec as P

EPSILON = 1e-06
WARMTH = 0.05
ROPE_BASE = 1000000.0
MASKED = -1e30
F32 = jnp.float32
BF16 = jnp.bfloat16
I32 = jnp.int32

SLOTS = 24
STAT = SLOTS - 1
PACK = 32
CHIPS = 16
DP = 16
MESH = pl.DeviceIdType.MESH


def far_first(k, half):
    return half + (1 - 2 * (k % 2)) * ((k + 1) // 2)


def each(n, step):
    for i in range(n):
        step(i)


def dot_t(a, b):
    return lax.dot_general(a, b, (((1,), (1,)), ((), ())), preferred_element_type=F32)


def dot(a, b):
    return jnp.dot(a, b, preferred_element_type=F32)


def iota(shape, dim):
    return lax.broadcasted_iota(I32, shape, dim)


def kernel(
    hid_hbm, again_hbm, wq_hbm, qgain_hbm, k_hbm, v_hbm, wo_hbm, fgain_hbm, len_hbm, ord_hbm, part_hbm,
    out_ref, loss_ref,
    hid_ref, again_ref, qgain_ref, fgain_ref, len_ref, ord_ref, part_ref, x_ref, qx, wq, kk, vv, wo, msg, ints, selbig, sel, bias, cosr, sinr,
    sq, qb, ob_out, ob, att, po_out, po_in, pb, st_own, st_in, ds_own, ds_in,
    pls, lb, lb_in, ub, ls_own, ls_in, uf,
    load_sem, ss, rs, x_recv, relay,
):
    g = lax.axis_index("dp")
    p = lax.axis_index("pack")
    z, y, c = lax.div(p, 16), lax.div(lax.rem(p, 16), 2), lax.rem(p, 2)
    sib = p + 1 - 2 * c
    chip = z * 8 + y
    n_stmt = hid_hbm.shape[0]

    def pack_peer(i):
        k, r = i // 4, i % 4
        py = lax.rem(y + far_first(k, 4), 8)
        pz = (z, 1 - z)[1 - r // 2]
        pc = (c, 1 - c)[1 - r % 2]
        return pz * 16 + py * 2 + pc

    def chip_peer(i):
        py = lax.rem(y + far_first(i // 2, 4), 8)
        pz = (z, 1 - z)[1 - i % 2]
        return pz * 8 + py

    gx, gz = lax.div(g, 4), lax.rem(g, 4)

    def dp_peer(i):
        a, b = i // 4, i % 4
        return lax.rem(gx + far_first(a, 2), 4) * 4 + lax.rem(gz + far_first(b, 2), 4)

    def remote(src, dst, send, recv, dg, dp_):
        return pltpu.make_async_remote_copy(
            src_ref=src, dst_ref=dst, send_sem=send, recv_sem=recv,
            device_id=(dg, dp_), device_id_type=MESH,
        )

    pending = []
    loads = [
        pltpu.make_async_copy(wq_hbm.at[:, c], wq.at[c], load_sem.at[0]),
        pltpu.make_async_copy(k_hbm, kk, load_sem.at[1]),
        pltpu.make_async_copy(v_hbm, vv, load_sem.at[2]),
        pltpu.make_async_copy(wo_hbm, wo.at[c], load_sem.at[3]),
    ]
    small = [
        pltpu.make_async_copy(src, dst, load_sem.at[4 + i])
        for i, (src, dst) in enumerate((
            (hid_hbm, hid_ref), (again_hbm, again_ref), (len_hbm, len_ref), (ord_hbm, ord_ref),
            (qgain_hbm, qgain_ref), (fgain_hbm, fgain_ref), (part_hbm, part_ref),
        ))
    ]
    small[0].start()
    small[1].start()
    barrier = pltpu.get_barrier_semaphore()

    def greet_pack(i):
        pl.semaphore_signal(barrier, inc=1, device_id=(g, pack_peer(i)), device_id_type=MESH)

    def group_at(dx, dz):
        return lax.rem(gx + dx, 4) * 4 + lax.rem(gz + dz, 4)

    near = [group_at(*d) for d in ((1, 0), (3, 0), (0, 1), (0, 3))]
    far = [group_at(*d) for d in ((2, 0), (0, 2), (1, 1), (1, 3), (3, 1), (3, 3))]

    def tell(groups, sem):
        for to in groups:
            pl.semaphore_signal(sem, inc=1, device_id=(to, p), device_id_type=MESH)

    tell(near, barrier)
    each(PACK - 1, greet_pack)
    for load in small[2:] + loads:
        load.start()

    lane = iota((n_stmt, 128), 1)
    sub = iota((n_stmt, 128), 0)
    same = lane == sub
    lane1 = iota((1, 128), 1)

    def to_row(col):
        return jnp.sum(jnp.where(same, col, 0.0), axis=0, keepdims=True)

    def to_col(row):
        return jnp.sum(jnp.where(same, row, 0.0), axis=1, keepdims=True)

    row8 = iota((8, 128), 0)
    small[0].wait()
    small[1].wait()
    h32 = hid_ref[...].astype(F32)
    msg[0:n_stmt, :] = (h32 * again_ref[...]).astype(BF16)
    sq_row = to_row(jnp.sum(h32 * h32, axis=1, keepdims=True))
    sq_hi = sq_row.astype(BF16).astype(F32)
    msg[n_stmt:, :] = jnp.where(
        row8 == 0, sq_hi, jnp.where(row8 == 1, sq_row - sq_hi, 0.0)
    ).astype(BF16)

    pl.semaphore_wait(barrier, PACK - 1 + 4)

    wq_copy = remote(wq_hbm.at[:, 1 - c], wq.at[c], ss.at[11], rs.at[11], g, sib)

    def x_start(i):
        remote(msg, x_ref.at[i], ss.at[0], x_recv.at[i // 4], g, chip_peer(i) * 2 + c).start()

    def source_chip(i):
        py = lax.rem(y + 8 - far_first(i // 2, 4), 8)
        pz = (z, 1 - z)[1 - i % 2]
        return pz * 8 + py

    each(CHIPS - 1, x_start)
    wq_copy.start()
    tell(near, relay.at[0])
    x_ref[CHIPS - 1] = msg[...]

    for load in small[2:]:
        load.wait()
    ints[...] = jnp.where(row8 == 1, -1.0, 0.0)
    ints[0:1, 0:n_stmt] = len_ref[...].astype(F32)
    ints[1:2, 0:n_stmt] = ord_ref[...].astype(F32)
    len_row = ints[0:1, :]
    ord_row = ints[1:2, :]
    len_col = to_col(len_row)
    lane_f = lane.astype(F32)
    sub_f = sub.astype(F32)
    at = sub_f == ord_row
    plen_row = jnp.sum(jnp.where(at, len_col, 0.0), axis=0, keepdims=True)
    plen_col = to_col(plen_row)
    end_row = jnp.sum(jnp.where(sub <= lane, plen_col, 0.0), axis=0, keepdims=True)
    start_row = end_row - plen_row
    place_col = jnp.sum(jnp.where(at, lane_f, 0.0), axis=1, keepdims=True)
    place_row = jnp.where(lane1 < n_stmt, to_row(place_col), -1000.0)
    start_col = jnp.sum(jnp.where(at, start_row, 0.0), axis=1, keepdims=True)
    end_col = jnp.sum(jnp.where(at, end_row, 0.0), axis=1, keepdims=True)
    tokens = float(k_hbm.shape[0])
    end_real = jnp.where(lane1 < n_stmt, end_row, 1e9)

    def before(tok):
        return jnp.sum(jnp.where(end_real <= tok, 1.0, 0.0), axis=1, keepdims=True)

    b3 = iota((PACK, SLOTS, 128), 0).reshape(PACK * SLOTS, 128).astype(F32)
    j3 = iota((PACK, SLOTS, 128), 1).reshape(PACK * SLOTS, 128).astype(F32)
    first_big = before(b3 * tokens)
    selbig[...] = jnp.where(place_row == first_big + j3, 1.0, 0.0).astype(BF16)

    freq = jnp.exp(
        jnp.where(lane1 < 64, lane1, lane1 - 64).astype(F32) * (-2.0 / 128.0 * math.log(ROPE_BASE))
    )
    angle = (len_col - 1.0) * freq
    cosr[...] = jnp.cos(angle)
    sinr[...] = jnp.where(lane < 64, -1.0, 1.0) * jnp.sin(angle)

    w_copy = remote(wo_hbm, wo.at[c], ss.at[13], rs.at[13], g, sib)
    loads[0].wait()
    x15 = x_ref.at[0:CHIPS - 1]
    wq_copy.wait_recv()
    pending.append(remote(x15, x15, ss.at[0], rs.at[0], g, sib).wait_send)
    pending.append(wq_copy.wait_send)
    parts = jnp.zeros((n_stmt, 256), F32)
    sq_sum = jnp.zeros((8, 128), F32)
    for k in (3, 2, 1, 0):
        group = x_ref.at[4 * k:min(4 * k + 4, CHIPS - 1)]
        remote(group, group, ss.at[0], x_recv.at[k], g, sib).wait_recv()
        if k == 0:
            pass
        slots = list(range(4 * k, 4 * k + 4))
        blocks = jnp.concatenate([x_ref[i, 0:n_stmt, :] for i in slots], axis=1)
        for i in slots:
            sq_sum = sq_sum + x_ref[i, n_stmt:, :].astype(F32)
        weights = jnp.concatenate(
            [jnp.concatenate([wq[1 - c, source_chip(i)], wq[c, source_chip(i)]], axis=1) for i in slots],
            axis=0,
        )
        parts = parts + dot(blocks, weights)
    qx[0, 0:n_stmt, :] = parts[:, 0:128]
    qx[0, n_stmt:, :] = sq_sum
    q_copy = remote(qx.at[0], qx.at[1], ss.at[12], rs.at[12], g, sib)
    q_copy.start()
    pending.append(q_copy.wait_send)
    q_copy.wait_recv()
    q_raw = parts[:, 128:] + qx[1, 0:n_stmt, :]
    sq_sum = sq_sum + qx[1, n_stmt:, :]
    total = to_col(sq_sum[0:1, :] + sq_sum[1:2, :])
    mean_sq = jnp.sum(q_raw * q_raw, axis=1, keepdims=True) * (1.0 / 128.0)
    inv = lax.rsqrt(mean_sq + EPSILON * (total * (1.0 / (PACK * 128)) + EPSILON))
    q = q_raw * inv * qgain_ref[...]
    q = (q * cosr[...] + pltpu.roll(q, 64, 1) * sinr[...]).astype(BF16)
    q128 = jnp.concatenate([q, jnp.zeros((128 - n_stmt, 128), BF16)], axis=0)
    for k in range(8):
        py = lax.rem(y + far_first(k, 4), 8)
        firsts = [py * 2, py * 2 + 16]
        rows = [pl.ds(pl.multiple_of(f * SLOTS, 16), 2 * SLOTS) for f in firsts]
        chosen = dot(jnp.concatenate([selbig[r, :] for r in rows], axis=0), q128).astype(BF16)
        for f, r in zip(firsts, (0, 1)):
            sq[pl.ds(f, 2)] = chosen[2 * SLOTS * r:2 * SLOTS * (r + 1)].reshape(2, SLOTS, 128)
        for i in range(4 * k, min(4 * k + 4, PACK - 1)):
            to = pack_peer(i)
            remote(sq.at[to], qb.at[p], ss.at[1], rs.at[1], g, to).start()
    qb[p] = sq[p]
    w_copy.start()
    block_a = jnp.floor((start_col + 0.5) * (1.0 / tokens))
    block_b = jnp.floor((end_col - 0.5) * (1.0 / tokens))
    slot_a = place_col - before(block_a * tokens)
    slot_b = place_col - before(block_b * tokens)
    wide = iota((n_stmt, PACK * SLOTS), 1).astype(F32)
    for i, (blk, slot) in enumerate(
        ((block_a, slot_a), (block_b, slot_b), (block_a, float(STAT)), (block_b, float(STAT)))
    ):
        sel[i * n_stmt:(i + 1) * n_stmt, :] = jnp.where(
            wide == blk * SLOTS + slot, 1.0, 0.0
        ).astype(BF16)

    pf = p.astype(F32)
    slot_id = before(jnp.zeros((SLOTS, 128), F32) + pf * tokens) + iota((SLOTS, 1), 0).astype(F32)
    lane24 = iota((SLOTS, 128), 1).astype(F32)
    st = jnp.sum(jnp.where(lane24 == slot_id, start_row, 0.0), axis=1, keepdims=True)
    en = jnp.sum(jnp.where(lane24 == slot_id, end_row, 0.0), axis=1, keepdims=True)
    tok = iota((SLOTS, k_hbm.shape[0]), 1).astype(F32) + pf * tokens
    own_bias = jnp.where((tok >= st) & (tok < en), 0.0, MASKED)
    for i in range(4):
        bias[i * SLOTS:(i + 1) * SLOTS, :] = own_bias

    pl.semaphore_wait(relay.at[0], 4)
    tell(far, relay.at[1])
    loads[1].wait()
    loads[2].wait()
    q31 = qb.at[0:PACK - 1]
    pending.append(remote(q31, q31, ss.at[1], rs.at[1], g, sib).wait_send)
    pending.append(w_copy.wait_send)
    remote(q31, q31, ss.at[1], rs.at[1], g, sib).wait_recv()

    scale = 128 ** -0.5
    jr = iota((SLOTS, 128), 0)
    jl = iota((SLOTS, 128), 1)
    for n in range(8):
        dj = (2, 1, 3, 0)[n // 2]
        kz = (z, 1 - z)[1 - n % 2]
        kh = kz * 4 + lax.rem(lax.div(y, 2) + dj, 4)
        cols = pl.ds(pl.multiple_of(kh * 128, 128), 128)
        qs = qb[pl.ds(kh * 4, 4)].reshape(4 * SLOTS, 128)
        s = dot_t(qs, kk[:, cols]) * scale + bias[...]
        m = jnp.max(s, axis=1, keepdims=True)
        w = jnp.exp(s - m)
        l = jnp.sum(w, axis=1, keepdims=True)
        o = dot(w.astype(BF16), vv[:, cols]) / l
        lse = m + jnp.log(l)
        hi = lse.astype(BF16).astype(F32)
        mid = (lse - hi).astype(BF16).astype(F32)
        lo = lse - hi - mid
        for r in range(4):
            part = slice(r * SLOTS, (r + 1) * SLOTS)
            stat = jnp.where(
                jl == jr, hi[part], jnp.where(
                    jl == jr + 32, mid[part], jnp.where(jl == jr + 64, lo[part], 0.0)
                )
            )
            stat = jnp.sum(stat, axis=0, keepdims=True)
            ob_out[kh * 4 + r] = jnp.where(jr == STAT, stat, o[part]).astype(BF16)
        if n < 7:
            for r in range(4):
                to = kh * 4 + r
                remote(ob_out.at[to], ob.at[p], ss.at[2], rs.at[2], g, to).start()
        else:
            for r in range(1, 4):
                to = kh * 4 + lax.rem(lax.rem(p, 4) + r, 4)
                remote(ob_out.at[to], ob.at[p], ss.at[2], rs.at[2], g, to).start()
    ob[p] = ob_out[p]
    o31 = ob.at[0:PACK - 1]
    pending.append(remote(o31, o31, ss.at[2], rs.at[2], g, sib).wait_send)
    remote(o31, o31, ss.at[2], rs.at[2], g, sib).wait_recv()

    got = dot(sel[...], ob[...].reshape(PACK * SLOTS, 128))

    def stat_of(rows, slot):
        hit = (lane_f == slot) | (lane_f == slot + 32.0) | (lane_f == slot + 64.0)
        return jnp.sum(jnp.where(hit, rows, 0.0), axis=1, keepdims=True)

    lse_a = stat_of(got[2 * n_stmt:3 * n_stmt], slot_a)
    lse_b = stat_of(got[3 * n_stmt:], slot_b)
    top = jnp.maximum(lse_a, lse_b)
    w_a = jnp.exp(lse_a - top)
    w_b = jnp.where(block_a == block_b, 0.0, jnp.exp(lse_b - top))
    own_att = ((w_a * got[0:n_stmt] + w_b * got[n_stmt:2 * n_stmt]) / (w_a + w_b)).astype(BF16)
    att[c] = own_att
    remote(att.at[c], att.at[c], ss.at[3], rs.at[3], g, sib).start()
    pending.append(remote(att.at[c], att.at[c], ss.at[3], rs.at[3], g, sib).wait_send)
    loads[3].wait()
    w_copy.wait_recv()
    remote(att.at[c], att.at[1 - c], ss.at[3], rs.at[3], g, sib).wait_recv()
    pl.semaphore_wait(relay.at[1], 6)
    heads = jnp.concatenate([att[0], att[1]], axis=1)
    for k in range(CHIPS // 2):
        ends = [chip_peer(2 * k), chip_peer(2 * k + 1)]
        cols = [pl.ds(pl.multiple_of((to * 2 + c) * 128, 128), 128) for to in ends]
        w4 = jnp.concatenate(
            [jnp.concatenate([wo[0, :, at_], wo[1, :, at_]], axis=0) for at_ in cols], axis=1
        )
        part = dot(heads, w4)
        for r in range(2):
            i = 2 * k + r
            own_part = part[:, 128 * r:128 * r + 128]
            if i < CHIPS - 1:
                po_out[i] = own_part.astype(BF16)
                remote(po_out.at[i], po_in.at[i], ss.at[4], rs.at[4], g, ends[r] * 2 + c).start()
    pending.append(remote(po_out, po_in, ss.at[4], rs.at[4], g, sib).wait_send)
    remote(po_out, po_in, ss.at[4], rs.at[4], g, sib).wait_recv()
    hid = hid_ref[...].astype(F32) + own_part
    for i in range(CHIPS - 1):
        hid = hid + po_in[i].astype(F32)

    fgain = fgain_ref[...]
    feat = (hid * fgain).astype(BF16)
    pb[g] = feat
    f32feat = feat.astype(F32)

    def p_start(i):
        remote(pb.at[g], pb.at[g], ss.at[5], rs.at[5], dp_peer(i), p).start()

    each(DP - 1, p_start)
    s1 = jnp.sum(hid * hid, axis=1, keepdims=True)
    s2 = jnp.sum(f32feat * f32feat, axis=1, keepdims=True)
    st_row = jnp.sum(
        jnp.where(same, s1, 0.0) + jnp.where(lane == sub + 64, s2, 0.0), axis=0, keepdims=True
    )
    st_own[...] = st_row
    st_in[p] = st_row

    def s_start(i):
        remote(st_own, st_in.at[p], ss.at[6], rs.at[6], g, pack_peer(i)).start()

    each(PACK - 1, s_start)
    s31 = st_in.at[0:PACK - 1]
    pending.append(remote(s31, s31, ss.at[6], rs.at[6], g, sib).wait_send)
    p15 = pb.at[0:DP - 1]
    pending.append(remote(p15, p15, ss.at[5], rs.at[5], g, sib).wait_send)
    remote(s31, s31, ss.at[6], rs.at[6], g, sib).wait_recv()
    st_row = jnp.sum(st_in[...], axis=0)
    odd = lax.rem(g, 2)
    half_row = lax.div(g, 2)
    in_half = lax.div(lane1, 64) == odd

    def own_half(row):
        return jnp.where(in_half, jnp.where(odd == 1, row, pltpu.roll(row, 64, 1)), 0.0)

    ds_own[...] = own_half(st_row)
    ds_in[odd, half_row] = ds_own[...]

    def d_start(i):
        remote(ds_own, ds_in.at[odd, half_row], ss.at[7], rs.at[7], dp_peer(i), p).start()

    each(DP - 1, d_start)
    dall = st_in.at[0:DP - 1]
    pending.append(remote(dall, dall, ss.at[7], rs.at[7], g, sib).wait_send)
    s1_all = to_col(jnp.where(lane1 < 64, st_row, 0.0))
    s2_all = to_col(jnp.where(lane1 < 64, pltpu.roll(st_row, 64, 1), 0.0))
    inv_norm = lax.rsqrt(s2_all)
    rms = jnp.sqrt(s1_all * (1.0 / (PACK * 128)) + EPSILON)
    out_ref[0:n_stmt, :] = (hid / rms * fgain).astype(BF16)
    remote(p15, p15, ss.at[5], rs.at[5], g, sib).wait_recv()

    for j in range(4):
        part = dot_t(feat, pb[4 * j:4 * j + 4].reshape(256, 128))
        for r in range(2):
            pls[pl.ds(2 * j + r, n_stmt, stride=8), :] = part[:, 128 * r:128 * r + 128]
    lb[...] = pls[...].astype(BF16).reshape(PACK, 16, 128)

    def l_start(i):
        to = pack_peer(i)
        remote(lb.at[to], lb_in.at[p], ss.at[8], rs.at[8], g, to).start()

    each(PACK - 1, l_start)
    lb_in[p] = lb[p]
    remote(dall, dall, ss.at[7], rs.at[7], g, sib).wait_recv()
    inv_all = lax.rsqrt((ds_in[0] + ds_in[1]).reshape(8, 128))
    l31 = lb_in.at[0:PACK - 1]
    pending.append(remote(l31, l31, ss.at[8], rs.at[8], g, sib).wait_send)
    remote(l31, l31, ss.at[8], rs.at[8], g, sib).wait_recv()
    acc = jnp.zeros((16, 128), F32)
    for i in range(PACK):
        acc = acc + lb_in[i].astype(F32)
    col_id = iota((8, 128), 0) * 128 + iota((8, 128), 1)
    partner = part_ref[...]

    def whole(x):
        return jnp.sum(jnp.sum(x, axis=1, keepdims=True), axis=0, keepdims=True)

    losses = []
    exps = []
    for i in range(2):
        row_id = g * n_stmt + p * 2 + i
        diag = col_id == row_id
        own_inv = whole(jnp.where(diag, inv_all, 0.0))
        logit = acc[8 * i:8 * i + 8] * inv_all * (own_inv * (1.0 / WARMTH))
        e = jnp.where(diag, 0.0, jnp.exp(logit))
        own_partner = whole(jnp.where(diag, partner.astype(F32), 0.0))
        target = whole(jnp.where(col_id.astype(F32) == own_partner, logit, 0.0))
        losses.append(jnp.log(whole(e)) - target)
        exps.append(e)
    loss_ref[...] = jnp.where(iota((1, 2), 1) == 0, losses[0], losses[1])
    ub[p] = jnp.concatenate(exps, axis=0).astype(BF16)

    def u_start(i):
        remote(ub.at[p], ub.at[p], ss.at[9], rs.at[9], g, pack_peer(i)).start()

    each(PACK - 1, u_start)
    u31 = ub.at[0:PACK - 1]
    pending.append(remote(u31, u31, ss.at[9], rs.at[9], g, sib).wait_send)
    remote(u31, u31, ss.at[9], rs.at[9], g, sib).wait_recv()
    uf[...] = ub[...].reshape(PACK * 16, 128).astype(F32)
    mats = [uf[pl.ds(j, n_stmt, stride=8), :] for j in range(8)]
    row_sum = mats[0]
    for j in range(1, 8):
        row_sum = row_sum + mats[j]
    inv_sum = 1.0 / jnp.sum(row_sum, axis=1, keepdims=True)
    inv_row = jnp.sum(jnp.where(lane == sub + 64, inv_sum, 0.0), axis=0, keepdims=True)
    ls_own[...] = own_half(inv_row)
    ls_in[odd, half_row] = ls_own[...]

    def e_start(i):
        remote(ls_own, ls_in.at[odd, half_row], ss.at[10], rs.at[10], dp_peer(i), p).start()

    each(DP - 1, e_start)
    row_f = (g * n_stmt + iota((n_stmt, 1), 0)).astype(F32)
    part_f = partner.astype(F32)
    own_part_col = jnp.zeros((n_stmt, 1), F32)
    for j in range(8):
        own_part_col = own_part_col + jnp.sum(
            jnp.where((lane + 128 * j).astype(F32) == row_f, part_f[j:j + 1, :], 0.0), axis=1, keepdims=True
        )
    pairs = []
    logs = []
    for j in range(8):
        cid = (lane + 128 * j).astype(F32)
        pairs.append(
            jnp.where(cid == own_part_col, 1.0, 0.0) + jnp.where(part_f[j:j + 1, :] == row_f, 1.0, 0.0)
        )
        logs.append(jnp.log(jnp.maximum(mats[j], 1e-30)))
    pending.append(remote(dall, dall, ss.at[10], rs.at[10], g, sib).wait_send)
    remote(dall, dall, ss.at[10], rs.at[10], g, sib).wait_recv()
    sums_all = (ls_in[0] + ls_in[1]).reshape(8, 128)
    grad = jnp.zeros((n_stmt, 128), F32)
    inner_acc = jnp.zeros((n_stmt, 128), F32)
    for j in range(4):
        scaled = []
        for k in (2 * j, 2 * j + 1):
            wk = mats[k] * (inv_sum + sums_all[k:k + 1, :]) - pairs[k]
            inner_acc = inner_acc + wk * logs[k]
            scaled.append((wk * inv_all[k:k + 1, :]).astype(BF16))
        grad = grad + dot(jnp.concatenate(scaled, axis=1), pb[4 * j:4 * j + 4].reshape(256, 128))
    inner = jnp.sum(inner_acc, axis=1, keepdims=True)
    out = grad * (1.0 / WARMTH) - f32feat * (inv_norm * inner)
    out_ref[n_stmt:, :] = (out * fgain * (inv_norm * float(PACK * 128) ** 0.5)).astype(BF16)

    for wait in pending:
        wait()


def local(
    hidden_in, attn_gain, w_query, query_gain, cached_keys, cached_values, w_out, final_gain,
    lengths, pack_order, partner,
):
    n = hidden_in.shape[0]
    toks, kvw = cached_keys.shape
    width = w_query.shape[0]
    vmem = pl.BlockSpec(memory_space=pltpu.VMEM)
    hbm = pl.BlockSpec(memory_space=pltpu.HBM)
    V = pltpu.VMEM
    dma = pltpu.SemaphoreType.DMA
    out, loss = pl.pallas_call(
        kernel,
        out_shape=(
            jax.ShapeDtypeStruct((2 * n, 128), BF16),
            jax.ShapeDtypeStruct((1, 2), F32),
        ),
        in_specs=[hbm] * 11,
        out_specs=(vmem, vmem),
        scratch_shapes=[
            V((n, 128), BF16),
            V((1, 128), F32),
            V((1, 128), F32),
            V((1, 128), F32),
            V(lengths.shape, I32),
            V(pack_order.shape, I32),
            V((8, 128), I32),
            V((CHIPS, n + 8, 128), BF16),
            V((2, n + 8, 128), F32),
            V((2, CHIPS, 128, 128), BF16),
            V((toks, kvw), BF16),
            V((toks, kvw), BF16),
            V((2, 128, width), BF16),
            V((n + 8, 128), BF16),
            V((8, 128), F32),
            V((PACK * SLOTS, 128), BF16),
            V((4 * n, PACK * SLOTS), BF16),
            V((4 * SLOTS, toks), F32),
            V((n, 128), F32),
            V((n, 128), F32),
            V((PACK, SLOTS, 128), BF16),
            V((PACK, SLOTS, 128), BF16),
            V((PACK, SLOTS, 128), BF16),
            V((PACK, SLOTS, 128), BF16),
            V((2, n, 128), BF16),
            V((CHIPS - 1, n, 128), BF16),
            V((CHIPS - 1, n, 128), BF16),
            V((DP, n, 128), BF16),
            V((1, 128), F32),
            V((PACK, 1, 128), F32),
            V((1, 128), F32),
            V((2, 8, 1, 128), F32),
            V((n * 8, 128), F32),
            V((PACK, 16, 128), BF16),
            V((PACK, 16, 128), BF16),
            V((PACK, 16, 128), BF16),
            V((1, 128), F32),
            V((2, 8, 1, 128), F32),
            V((n * 8, 128), F32),
            dma((11,)),
            dma((14,)),
            dma((14,)),
            dma((4,)),
            pltpu.SemaphoreType.REGULAR((2,)),
        ],
        compiler_params=pltpu.CompilerParams(
            collective_id=0, has_side_effects=True
        ),
    )(
        hidden_in,
        attn_gain.reshape(1, 128),
        w_query.reshape(CHIPS, 2, 128, 128),
        query_gain.reshape(1, 128),
        cached_keys,
        cached_values,
        w_out,
        final_gain.reshape(1, 128),
        lengths,
        pack_order,
        partner.reshape(8, 128),
    )
    return out[0:n], loss.reshape(2), out[n:]


def solution(mesh):
    in_specs = (
        P("dp", "pack"),
        P("pack"),
        P(None, "pack"),
        P(),
        P(("dp", "pack"), None),
        P(("dp", "pack"), None),
        P("pack", None),
        P("pack"),
        P("dp", None),
        P("dp", None),
        P(),
    )
    out_specs = (P("dp", "pack"), P(("dp", "pack")), P("dp", "pack"))
    return jax.shard_map(local, mesh=mesh, in_specs=in_specs, out_specs=out_specs, check_vma=False)
```

```python
import math

import jax
import jax.numpy as jnp
from jax import lax
from jax.experimental import pallas as pl
from jax.experimental.pallas import tpu as pltpu
from jax.sharding import PartitionSpec as P

EPSILON = 1e-06
WARMTH = 0.05
ROPE_BASE = 1000000.0
MASKED = -1e30
F32 = jnp.float32
BF16 = jnp.bfloat16
I32 = jnp.int32

SLOTS = 24
STAT = SLOTS - 1
PACK = 32
CHIPS = 16
DP = 16
MESH = pl.DeviceIdType.MESH


def far_first(k, half):
    return half + (1 - 2 * (k % 2)) * ((k + 1) // 2)


def each(n, step):
    for i in range(n):
        step(i)


def dot_t(a, b):
    return lax.dot_general(a, b, (((1,), (1,)), ((), ())), preferred_element_type=F32)


def dot(a, b):
    return jnp.dot(a, b, preferred_element_type=F32)


def iota(shape, dim):
    return lax.broadcasted_iota(I32, shape, dim)


def kernel(
    hid_hbm, again_hbm, wq_hbm, qgain_hbm, k_hbm, v_hbm, wo_hbm, fgain_hbm, len_hbm, ord_hbm, part_hbm,
    out_ref, loss_ref,
    hid_ref, again_ref, qgain_ref, fgain_ref, len_ref, ord_ref, part_ref, x_ref, qx, wq, kk, vv, wo, msg, ints, selbig, sel, bias, cosr, sinr,
    sq, qb, ob_out, ob, att, po_out, po_in, pb, st_own, st_in, ds_own, ds_in,
    pls, lb, lb_in, ub, ls_own, ls_in, uf,
    load_sem, ss, rs, x_recv, relay,
):
    g = lax.axis_index("dp")
    p = lax.axis_index("pack")
    z, y, c = lax.div(p, 16), lax.div(lax.rem(p, 16), 2), lax.rem(p, 2)
    sib = p + 1 - 2 * c
    chip = z * 8 + y
    n_stmt = hid_hbm.shape[0]

    def pack_peer(i):
        k, r = i // 4, i % 4
        py = lax.rem(y + far_first(k, 4), 8)
        pz = (z, 1 - z)[1 - r // 2]
        pc = (c, 1 - c)[1 - r % 2]
        return pz * 16 + py * 2 + pc

    def chip_peer(i):
        py = lax.rem(y + far_first(i // 2, 4), 8)
        pz = (z, 1 - z)[1 - i % 2]
        return pz * 8 + py

    gx, gz = lax.div(g, 4), lax.rem(g, 4)

    def dp_peer(i):
        a, b = i // 4, i % 4
        return lax.rem(gx + far_first(a, 2), 4) * 4 + lax.rem(gz + far_first(b, 2), 4)

    def remote(src, dst, send, recv, dg, dp_):
        return pltpu.make_async_remote_copy(
            src_ref=src, dst_ref=dst, send_sem=send, recv_sem=recv,
            device_id=(dg, dp_), device_id_type=MESH,
        )

    pending = []
    loads = [
        pltpu.make_async_copy(wq_hbm.at[:, c], wq.at[c], load_sem.at[0]),
        pltpu.make_async_copy(k_hbm, kk, load_sem.at[1]),
        pltpu.make_async_copy(v_hbm, vv, load_sem.at[2]),
        pltpu.make_async_copy(wo_hbm, wo.at[c], load_sem.at[3]),
    ]
    small = [
        pltpu.make_async_copy(src, dst, load_sem.at[4 + i])
        for i, (src, dst) in enumerate((
            (hid_hbm, hid_ref), (again_hbm, again_ref), (len_hbm, len_ref), (ord_hbm, ord_ref),
            (qgain_hbm, qgain_ref), (fgain_hbm, fgain_ref), (part_hbm, part_ref),
        ))
    ]
    small[0].start()
    small[1].start()
    barrier = pltpu.get_barrier_semaphore()

    def greet_pack(i):
        pl.semaphore_signal(barrier, inc=1, device_id=(g, pack_peer(i)), device_id_type=MESH)

    def group_at(dx, dz):
        return lax.rem(gx + dx, 4) * 4 + lax.rem(gz + dz, 4)

    near = [group_at(*d) for d in ((1, 0), (3, 0), (0, 1), (0, 3))]
    far = [group_at(*d) for d in ((2, 0), (0, 2), (1, 1), (1, 3), (3, 1), (3, 3))]

    def tell(groups, sem):
        for to in groups:
            pl.semaphore_signal(sem, inc=1, device_id=(to, p), device_id_type=MESH)

    tell(near, barrier)
    each(PACK - 1, greet_pack)
    for load in small[2:] + loads:
        load.start()

    lane = iota((n_stmt, 128), 1)
    sub = iota((n_stmt, 128), 0)
    same = lane == sub
    lane1 = iota((1, 128), 1)

    def to_row(col):
        return jnp.sum(jnp.where(same, col, 0.0), axis=0, keepdims=True)

    def to_col(row):
        return jnp.sum(jnp.where(same, row, 0.0), axis=1, keepdims=True)

    row8 = iota((8, 128), 0)
    small[0].wait()
    small[1].wait()
    h32 = hid_ref[...].astype(F32)
    msg[0:n_stmt, :] = (h32 * again_ref[...]).astype(BF16)
    sq_row = to_row(jnp.sum(h32 * h32, axis=1, keepdims=True))
    sq_hi = sq_row.astype(BF16).astype(F32)
    msg[n_stmt:, :] = jnp.where(
        row8 == 0, sq_hi, jnp.where(row8 == 1, sq_row - sq_hi, 0.0)
    ).astype(BF16)

    pl.semaphore_wait(barrier, PACK - 1 + 4)

    wq_copy = remote(wq_hbm.at[:, 1 - c], wq.at[c], ss.at[11], rs.at[11], g, sib)

    def x_start(i):
        remote(msg, x_ref.at[i], ss.at[0], x_recv.at[i // 4], g, chip_peer(i) * 2 + c).start()

    def source_chip(i):
        py = lax.rem(y + 8 - far_first(i // 2, 4), 8)
        pz = (z, 1 - z)[1 - i % 2]
        return pz * 8 + py

    each(CHIPS - 1, x_start)
    wq_copy.start()
    tell(near, relay.at[0])
    x_ref[CHIPS - 1] = msg[...]

    for load in small[2:]:
        load.wait()
    ints[...] = jnp.where(row8 == 1, -1.0, 0.0)
    ints[0:1, 0:n_stmt] = len_ref[...].astype(F32)
    ints[1:2, 0:n_stmt] = ord_ref[...].astype(F32)
    len_row = ints[0:1, :]
    ord_row = ints[1:2, :]
    len_col = to_col(len_row)
    lane_f = lane.astype(F32)
    sub_f = sub.astype(F32)
    at = sub_f == ord_row
    plen_row = jnp.sum(jnp.where(at, len_col, 0.0), axis=0, keepdims=True)
    plen_col = to_col(plen_row)
    end_row = jnp.sum(jnp.where(sub <= lane, plen_col, 0.0), axis=0, keepdims=True)
    start_row = end_row - plen_row
    place_col = jnp.sum(jnp.where(at, lane_f, 0.0), axis=1, keepdims=True)
    place_row = jnp.where(lane1 < n_stmt, to_row(place_col), -1000.0)
    start_col = jnp.sum(jnp.where(at, start_row, 0.0), axis=1, keepdims=True)
    end_col = jnp.sum(jnp.where(at, end_row, 0.0), axis=1, keepdims=True)
    tokens = float(k_hbm.shape[0])
    end_real = jnp.where(lane1 < n_stmt, end_row, 1e9)

    def before(tok):
        return jnp.sum(jnp.where(end_real <= tok, 1.0, 0.0), axis=1, keepdims=True)

    b3 = iota((PACK, SLOTS, 128), 0).reshape(PACK * SLOTS, 128).astype(F32)
    j3 = iota((PACK, SLOTS, 128), 1).reshape(PACK * SLOTS, 128).astype(F32)
    first_big = before(b3 * tokens)
    selbig[...] = jnp.where(place_row == first_big + j3, 1.0, 0.0).astype(BF16)

    freq = jnp.exp(
        jnp.where(lane1 < 64, lane1, lane1 - 64).astype(F32) * (-2.0 / 128.0 * math.log(ROPE_BASE))
    )
    angle = (len_col - 1.0) * freq
    cosr[...] = jnp.cos(angle)
    sinr[...] = jnp.where(lane < 64, -1.0, 1.0) * jnp.sin(angle)

    w_copy = remote(wo_hbm, wo.at[c], ss.at[13], rs.at[13], g, sib)
    loads[0].wait()
    x15 = x_ref.at[0:CHIPS - 1]
    wq_copy.wait_recv()
    pending.append(remote(x15, x15, ss.at[0], rs.at[0], g, sib).wait_send)
    pending.append(wq_copy.wait_send)
    parts = jnp.zeros((n_stmt, 256), F32)
    sq_sum = jnp.zeros((8, 128), F32)
    for k in (3, 2, 1, 0):
        group = x_ref.at[4 * k:min(4 * k + 4, CHIPS - 1)]
        remote(group, group, ss.at[0], x_recv.at[k], g, sib).wait_recv()
        if k == 0:
            pass
        slots = list(range(4 * k, 4 * k + 4))
        blocks = jnp.concatenate([x_ref[i, 0:n_stmt, :] for i in slots], axis=1)
        for i in slots:
            sq_sum = sq_sum + x_ref[i, n_stmt:, :].astype(F32)
        weights = jnp.concatenate(
            [jnp.concatenate([wq[1 - c, source_chip(i)], wq[c, source_chip(i)]], axis=1) for i in slots],
            axis=0,
        )
        parts = parts + dot(blocks, weights)
    qx[0, 0:n_stmt, :] = parts[:, 0:128]
    qx[0, n_stmt:, :] = sq_sum
    q_copy = remote(qx.at[0], qx.at[1], ss.at[12], rs.at[12], g, sib)
    q_copy.start()
    pending.append(q_copy.wait_send)
    q_copy.wait_recv()
    q_raw = parts[:, 128:] + qx[1, 0:n_stmt, :]
    sq_sum = sq_sum + qx[1, n_stmt:, :]
    total = to_col(sq_sum[0:1, :] + sq_sum[1:2, :])
    mean_sq = jnp.sum(q_raw * q_raw, axis=1, keepdims=True) * (1.0 / 128.0)
    inv = lax.rsqrt(mean_sq + EPSILON * (total * (1.0 / (PACK * 128)) + EPSILON))
    q = q_raw * inv * qgain_ref[...]
    q = (q * cosr[...] + pltpu.roll(q, 64, 1) * sinr[...]).astype(BF16)
    q128 = jnp.concatenate([q, jnp.zeros((128 - n_stmt, 128), BF16)], axis=0)
    for k in range(8):
        py = lax.rem(y + far_first(k, 4), 8)
        firsts = [py * 2, py * 2 + 16]
        rows = [pl.ds(pl.multiple_of(f * SLOTS, 16), 2 * SLOTS) for f in firsts]
        chosen = dot(jnp.concatenate([selbig[r, :] for r in rows], axis=0), q128).astype(BF16)
        for f, r in zip(firsts, (0, 1)):
            sq[pl.ds(f, 2)] = chosen[2 * SLOTS * r:2 * SLOTS * (r + 1)].reshape(2, SLOTS, 128)
        for i in range(4 * k, min(4 * k + 4, PACK - 1)):
            to = pack_peer(i)
            remote(sq.at[to], qb.at[p], ss.at[1], rs.at[1], g, to).start()
    qb[p] = sq[p]
    w_copy.start()
    block_a = jnp.floor((start_col + 0.5) * (1.0 / tokens))
    block_b = jnp.floor((end_col - 0.5) * (1.0 / tokens))
    slot_a = place_col - before(block_a * tokens)
    slot_b = place_col - before(block_b * tokens)
    wide = iota((n_stmt, PACK * SLOTS), 1).astype(F32)
    for i, (blk, slot) in enumerate(
        ((block_a, slot_a), (block_b, slot_b), (block_a, float(STAT)), (block_b, float(STAT)))
    ):
        sel[i * n_stmt:(i + 1) * n_stmt, :] = jnp.where(
            wide == blk * SLOTS + slot, 1.0, 0.0
        ).astype(BF16)

    pf = p.astype(F32)
    slot_id = before(jnp.zeros((SLOTS, 128), F32) + pf * tokens) + iota((SLOTS, 1), 0).astype(F32)
    lane24 = iota((SLOTS, 128), 1).astype(F32)
    st = jnp.sum(jnp.where(lane24 == slot_id, start_row, 0.0), axis=1, keepdims=True)
    en = jnp.sum(jnp.where(lane24 == slot_id, end_row, 0.0), axis=1, keepdims=True)
    tok = iota((SLOTS, k_hbm.shape[0]), 1).astype(F32) + pf * tokens
    own_bias = jnp.where((tok >= st) & (tok < en), 0.0, MASKED)
    for i in range(4):
        bias[i * SLOTS:(i + 1) * SLOTS, :] = own_bias

    pl.semaphore_wait(relay.at[0], 4)
    tell(far, relay.at[1])
    loads[1].wait()
    loads[2].wait()
    q31 = qb.at[0:PACK - 1]
    pending.append(remote(q31, q31, ss.at[1], rs.at[1], g, sib).wait_send)
    pending.append(w_copy.wait_send)
    remote(q31, q31, ss.at[1], rs.at[1], g, sib).wait_recv()

    scale = 128 ** -0.5
    jr = iota((SLOTS, 128), 0)
    jl = iota((SLOTS, 128), 1)
    for n in range(8):
        dj = (2, 1, 3, 0)[n // 2]
        kz = (z, 1 - z)[1 - n % 2]
        kh = kz * 4 + lax.rem(lax.div(y, 2) + dj, 4)
        cols = pl.ds(pl.multiple_of(kh * 128, 128), 128)
        qs = qb[pl.ds(kh * 4, 4)].reshape(4 * SLOTS, 128)
        s = dot_t(qs, kk[:, cols]) * scale + bias[...]
        m = jnp.max(s, axis=1, keepdims=True)
        w = jnp.exp(s - m)
        l = jnp.sum(w, axis=1, keepdims=True)
        o = dot(w.astype(BF16), vv[:, cols]) / l
        lse = m + jnp.log(l)
        hi = lse.astype(BF16).astype(F32)
        mid = (lse - hi).astype(BF16).astype(F32)
        lo = lse - hi - mid
        for r in range(4):
            part = slice(r * SLOTS, (r + 1) * SLOTS)
            stat = jnp.where(
                jl == jr, hi[part], jnp.where(
                    jl == jr + 32, mid[part], jnp.where(jl == jr + 64, lo[part], 0.0)
                )
            )
            stat = jnp.sum(stat, axis=0, keepdims=True)
            ob_out[kh * 4 + r] = jnp.where(jr == STAT, stat, o[part]).astype(BF16)
        if n < 7:
            for r in range(4):
                to = kh * 4 + r
                remote(ob_out.at[to], ob.at[p], ss.at[2], rs.at[2], g, to).start()
        else:
            for r in range(1, 4):
                to = kh * 4 + lax.rem(lax.rem(p, 4) + r, 4)
                remote(ob_out.at[to], ob.at[p], ss.at[2], rs.at[2], g, to).start()
    ob[p] = ob_out[p]
    o31 = ob.at[0:PACK - 1]
    pending.append(remote(o31, o31, ss.at[2], rs.at[2], g, sib).wait_send)
    remote(o31, o31, ss.at[2], rs.at[2], g, sib).wait_recv()

    got = dot(sel[...], ob[...].reshape(PACK * SLOTS, 128))

    def stat_of(rows, slot):
        hit = (lane_f == slot) | (lane_f == slot + 32.0) | (lane_f == slot + 64.0)
        return jnp.sum(jnp.where(hit, rows, 0.0), axis=1, keepdims=True)

    lse_a = stat_of(got[2 * n_stmt:3 * n_stmt], slot_a)
    lse_b = stat_of(got[3 * n_stmt:], slot_b)
    top = jnp.maximum(lse_a, lse_b)
    w_a = jnp.exp(lse_a - top)
    w_b = jnp.where(block_a == block_b, 0.0, jnp.exp(lse_b - top))
    own_att = ((w_a * got[0:n_stmt] + w_b * got[n_stmt:2 * n_stmt]) / (w_a + w_b)).astype(BF16)
    att[c] = own_att
    remote(att.at[c], att.at[c], ss.at[3], rs.at[3], g, sib).start()
    pending.append(remote(att.at[c], att.at[c], ss.at[3], rs.at[3], g, sib).wait_send)
    loads[3].wait()
    w_copy.wait_recv()
    remote(att.at[c], att.at[1 - c], ss.at[3], rs.at[3], g, sib).wait_recv()
    pl.semaphore_wait(relay.at[1], 6)
    heads = jnp.concatenate([att[0], att[1]], axis=1)
    for k in range(CHIPS // 2):
        ends = [chip_peer(2 * k), chip_peer(2 * k + 1)]
        cols = [pl.ds(pl.multiple_of((to * 2 + c) * 128, 128), 128) for to in ends]
        w4 = jnp.concatenate(
            [jnp.concatenate([wo[0, :, at_], wo[1, :, at_]], axis=0) for at_ in cols], axis=1
        )
        part = dot(heads, w4)
        for r in range(2):
            i = 2 * k + r
            own_part = part[:, 128 * r:128 * r + 128]
            if i < CHIPS - 1:
                po_out[i] = own_part.astype(BF16)
                remote(po_out.at[i], po_in.at[i], ss.at[4], rs.at[4], g, ends[r] * 2 + c).start()
    pending.append(remote(po_out, po_in, ss.at[4], rs.at[4], g, sib).wait_send)
    remote(po_out, po_in, ss.at[4], rs.at[4], g, sib).wait_recv()
    hid = hid_ref[...].astype(F32) + own_part
    for i in range(CHIPS - 1):
        hid = hid + po_in[i].astype(F32)

    fgain = fgain_ref[...]
    feat = (hid * fgain).astype(BF16)
    pb[g] = feat
    f32feat = feat.astype(F32)

    def p_start(i):
        remote(pb.at[g], pb.at[g], ss.at[5], rs.at[5], dp_peer(i), p).start()

    each(DP - 1, p_start)
    s1 = jnp.sum(hid * hid, axis=1, keepdims=True)
    s2 = jnp.sum(f32feat * f32feat, axis=1, keepdims=True)
    st_row = jnp.sum(
        jnp.where(same, s1, 0.0) + jnp.where(lane == sub + 64, s2, 0.0), axis=0, keepdims=True
    )
    st_own[...] = st_row
    st_in[p] = st_row

    def s_start(i):
        remote(st_own, st_in.at[p], ss.at[6], rs.at[6], g, pack_peer(i)).start()

    each(PACK - 1, s_start)
    s31 = st_in.at[0:PACK - 1]
    pending.append(remote(s31, s31, ss.at[6], rs.at[6], g, sib).wait_send)
    p15 = pb.at[0:DP - 1]
    pending.append(remote(p15, p15, ss.at[5], rs.at[5], g, sib).wait_send)
    remote(s31, s31, ss.at[6], rs.at[6], g, sib).wait_recv()
    st_row = jnp.sum(st_in[...], axis=0)
    odd = lax.rem(g, 2)
    half_row = lax.div(g, 2)
    in_half = lax.div(lane1, 64) == odd

    def own_half(row):
        return jnp.where(in_half, jnp.where(odd == 1, row, pltpu.roll(row, 64, 1)), 0.0)

    ds_own[...] = own_half(st_row)
    ds_in[odd, half_row] = ds_own[...]

    def d_start(i):
        remote(ds_own, ds_in.at[odd, half_row], ss.at[7], rs.at[7], dp_peer(i), p).start()

    each(DP - 1, d_start)
    dall = st_in.at[0:DP - 1]
    pending.append(remote(dall, dall, ss.at[7], rs.at[7], g, sib).wait_send)
    s1_all = to_col(jnp.where(lane1 < 64, st_row, 0.0))
    s2_all = to_col(jnp.where(lane1 < 64, pltpu.roll(st_row, 64, 1), 0.0))
    inv_norm = lax.rsqrt(s2_all)
    rms = jnp.sqrt(s1_all * (1.0 / (PACK * 128)) + EPSILON)
    out_ref[0:n_stmt, :] = (hid / rms * fgain).astype(BF16)
    remote(p15, p15, ss.at[5], rs.at[5], g, sib).wait_recv()

    for j in range(4):
        part = dot_t(feat, pb[4 * j:4 * j + 4].reshape(256, 128))
        for r in range(2):
            pls[pl.ds(2 * j + r, n_stmt, stride=8), :] = part[:, 128 * r:128 * r + 128]
    lb[...] = pls[...].astype(BF16).reshape(PACK, 16, 128)

    def l_start(i):
        to = pack_peer(i)
        remote(lb.at[to], lb_in.at[p], ss.at[8], rs.at[8], g, to).start()

    each(PACK - 1, l_start)
    lb_in[p] = lb[p]
    remote(dall, dall, ss.at[7], rs.at[7], g, sib).wait_recv()
    inv_all = lax.rsqrt((ds_in[0] + ds_in[1]).reshape(8, 128))
    l31 = lb_in.at[0:PACK - 1]
    pending.append(remote(l31, l31, ss.at[8], rs.at[8], g, sib).wait_send)
    remote(l31, l31, ss.at[8], rs.at[8], g, sib).wait_recv()
    acc = jnp.zeros((16, 128), F32)
    for i in range(PACK):
        acc = acc + lb_in[i].astype(F32)
    col_id = iota((8, 128), 0) * 128 + iota((8, 128), 1)
    partner = part_ref[...]

    def whole(x):
        return jnp.sum(jnp.sum(x, axis=1, keepdims=True), axis=0, keepdims=True)

    losses = []
    exps = []
    for i in range(2):
        row_id = g * n_stmt + p * 2 + i
        diag = col_id == row_id
        own_inv = whole(jnp.where(diag, inv_all, 0.0))
        logit = acc[8 * i:8 * i + 8] * inv_all * (own_inv * (1.0 / WARMTH))
        e = jnp.where(diag, 0.0, jnp.exp(logit))
        own_partner = whole(jnp.where(diag, partner.astype(F32), 0.0))
        target = whole(jnp.where(col_id.astype(F32) == own_partner, logit, 0.0))
        losses.append(jnp.log(whole(e)) - target)
        exps.append(e)
    loss_ref[...] = jnp.where(iota((8, 128), 1) == 0, losses[0], losses[1])
    ub[p] = jnp.concatenate(exps, axis=0).astype(BF16)

    def u_start(i):
        remote(ub.at[p], ub.at[p], ss.at[9], rs.at[9], g, pack_peer(i)).start()

    each(PACK - 1, u_start)
    u31 = ub.at[0:PACK - 1]
    pending.append(remote(u31, u31, ss.at[9], rs.at[9], g, sib).wait_send)
    remote(u31, u31, ss.at[9], rs.at[9], g, sib).wait_recv()
    uf[...] = ub[...].reshape(PACK * 16, 128).astype(F32)
    mats = [uf[pl.ds(j, n_stmt, stride=8), :] for j in range(8)]
    row_sum = mats[0]
    for j in range(1, 8):
        row_sum = row_sum + mats[j]
    inv_sum = 1.0 / jnp.sum(row_sum, axis=1, keepdims=True)
    inv_row = jnp.sum(jnp.where(lane == sub + 64, inv_sum, 0.0), axis=0, keepdims=True)
    ls_own[...] = own_half(inv_row)
    ls_in[odd, half_row] = ls_own[...]

    def e_start(i):
        remote(ls_own, ls_in.at[odd, half_row], ss.at[10], rs.at[10], dp_peer(i), p).start()

    each(DP - 1, e_start)
    row_f = (g * n_stmt + iota((n_stmt, 1), 0)).astype(F32)
    part_f = partner.astype(F32)
    own_part_col = jnp.zeros((n_stmt, 1), F32)
    for j in range(8):
        own_part_col = own_part_col + jnp.sum(
            jnp.where((lane + 128 * j).astype(F32) == row_f, part_f[j:j + 1, :], 0.0), axis=1, keepdims=True
        )
    pairs = []
    logs = []
    for j in range(8):
        cid = (lane + 128 * j).astype(F32)
        pairs.append(
            jnp.where(cid == own_part_col, 1.0, 0.0) + jnp.where(part_f[j:j + 1, :] == row_f, 1.0, 0.0)
        )
        logs.append(jnp.log(jnp.maximum(mats[j], 1e-30)))
    pending.append(remote(dall, dall, ss.at[10], rs.at[10], g, sib).wait_send)
    remote(dall, dall, ss.at[10], rs.at[10], g, sib).wait_recv()
    sums_all = (ls_in[0] + ls_in[1]).reshape(8, 128)
    grad = jnp.zeros((n_stmt, 128), F32)
    inner_acc = jnp.zeros((n_stmt, 128), F32)
    for j in range(4):
        scaled = []
        for k in (2 * j, 2 * j + 1):
            wk = mats[k] * (inv_sum + sums_all[k:k + 1, :]) - pairs[k]
            inner_acc = inner_acc + wk * logs[k]
            scaled.append((wk * inv_all[k:k + 1, :]).astype(BF16))
        grad = grad + dot(jnp.concatenate(scaled, axis=1), pb[4 * j:4 * j + 4].reshape(256, 128))
    inner = jnp.sum(inner_acc, axis=1, keepdims=True)
    out = grad * (1.0 / WARMTH) - f32feat * (inv_norm * inner)
    out_ref[n_stmt:, :] = (out * fgain * (inv_norm * float(PACK * 128) ** 0.5)).astype(BF16)

    for wait in pending:
        wait()


def local(
    hidden_in, attn_gain, w_query, query_gain, cached_keys, cached_values, w_out, final_gain,
    lengths, pack_order, partner,
):
    n = hidden_in.shape[0]
    toks, kvw = cached_keys.shape
    width = w_query.shape[0]
    vmem = pl.BlockSpec(memory_space=pltpu.VMEM)
    hbm = pl.BlockSpec(memory_space=pltpu.HBM)
    V = pltpu.VMEM
    dma = pltpu.SemaphoreType.DMA
    out, loss = pl.pallas_call(
        kernel,
        out_shape=(
            jax.ShapeDtypeStruct((2 * n, 128), BF16),
            jax.ShapeDtypeStruct((8, 128), F32),
        ),
        in_specs=[hbm] * 11,
        out_specs=(vmem, vmem),
        scratch_shapes=[
            V((n, 128), BF16),
            V((1, 128), F32),
            V((1, 128), F32),
            V((1, 128), F32),
            V(lengths.shape, I32),
            V(pack_order.shape, I32),
            V((8, 128), I32),
            V((CHIPS, n + 8, 128), BF16),
            V((2, n + 8, 128), F32),
            V((2, CHIPS, 128, 128), BF16),
            V((toks, kvw), BF16),
            V((toks, kvw), BF16),
            V((2, 128, width), BF16),
            V((n + 8, 128), BF16),
            V((8, 128), F32),
            V((PACK * SLOTS, 128), BF16),
            V((4 * n, PACK * SLOTS), BF16),
            V((4 * SLOTS, toks), F32),
            V((n, 128), F32),
            V((n, 128), F32),
            V((PACK, SLOTS, 128), BF16),
            V((PACK, SLOTS, 128), BF16),
            V((PACK, SLOTS, 128), BF16),
            V((PACK, SLOTS, 128), BF16),
            V((2, n, 128), BF16),
            V((CHIPS - 1, n, 128), BF16),
            V((CHIPS - 1, n, 128), BF16),
            V((DP, n, 128), BF16),
            V((1, 128), F32),
            V((PACK, 1, 128), F32),
            V((1, 128), F32),
            V((2, 8, 1, 128), F32),
            V((n * 8, 128), F32),
            V((PACK, 16, 128), BF16),
            V((PACK, 16, 128), BF16),
            V((PACK, 16, 128), BF16),
            V((1, 128), F32),
            V((2, 8, 1, 128), F32),
            V((n * 8, 128), F32),
            dma((11,)),
            dma((14,)),
            dma((14,)),
            dma((4,)),
            pltpu.SemaphoreType.REGULAR((2,)),
        ],
        compiler_params=pltpu.CompilerParams(
            collective_id=0, has_side_effects=True
        ),
    )(
        hidden_in,
        attn_gain.reshape(1, 128),
        w_query.reshape(CHIPS, 2, 128, 128),
        query_gain.reshape(1, 128),
        cached_keys,
        cached_values,
        w_out,
        final_gain.reshape(1, 128),
        lengths,
        pack_order,
        partner.reshape(8, 128),
    )
    return out[0:n], loss[0, 0:2], out[n:]


def solution(mesh):
    in_specs = (
        P("dp", "pack"),
        P("pack"),
        P(None, "pack"),
        P(),
        P(("dp", "pack"), None),
        P(("dp", "pack"), None),
        P("pack", None),
        P("pack"),
        P("dp", None),
        P("dp", None),
        P(),
    )
    out_specs = (P("dp", "pack"), P(("dp", "pack")), P("dp", "pack"))
    return jax.shard_map(local, mesh=mesh, in_specs=in_specs, out_specs=out_specs, check_vma=False)
```
